512 devices in a mesh: rows: 16 (over x, z_hi, core), batch: 32 (over z_lo, y).
Axes of the slice: x: 4, y: 4, z: 16 (z_hi: 2, z_lo: 8; z = z_hi * 8 + z_lo), core: 2. Of those that a mesh axis runs over, the one named last changes fastest.
Arguments:
- features: bfloat16 [384, 32, 32, 512], P('batch', 'rows'), may hold values from -12 to 12
- norm_gain: float32 [512], replicated, may hold values from 0.25 to 1.75
- norm_bias: float32 [512], replicated, may hold values from -2.5 to 2.5
- conv_weight: bfloat16 [4, 4608], replicated, may hold values from -0.09375 to 0.09375
- embed_weight: float32 [16, 1024], replicated, may hold values from -1.5 to 1.5
- embed_bias: float32 [1024], replicated, may hold values from -2.5 to 2.5
- proj_in: bfloat16 [1024, 2048], P('rows'), may hold values from -0.1875 to 0.1875
- proj_in_bias: float32 [2048], replicated, may hold values from -2.5 to 2.5
- proj_out: bfloat16 [2048, 768], P('rows'), may hold values from -0.125 to 0.125
- proj_out_bias: float32 [768], replicated, may hold values from -2.5 to 2.5
- targets: bfloat16 [384, 16, 16, 768], P('batch', 'rows'), may hold values from -6 to 6
Outputs:
- grad_features: bfloat16 [384, 32, 32, 512], P('batch', 'rows')
- grad_conv: float32 [4, 4608], replicated
- grad_gain: float32 [512], replicated
- grad_bias: float32 [512], replicated
- grad_embed: float32 [16, 1024], replicated
The draws below stay inside these ranges and needn't reach their ends.
All inputs are finite; a program needn't handle non-finite values.
Results may differ from the reference program's by a relative error of at most 0.012.
Values may be sent and summed in bfloat16 or wider, within the bound.
No kernel may reach another device: no remote copies, remote signals or barrier semaphores. Data moves between devices by JAX's collectives and lax.ppermute only.
A program may use at most 128 MiB of HBM per device.

```python
import jax
import jax.numpy as jnp
from jax import lax

CHANNELS = 512
GROUPS = 32
LATENT = 4
PATCH = 2
WIDTH = 1024
PROJ = 2048
ALIGN = 768
COLS = 32
IMAGES = 384
HEIGHT = 32
TOK_ROWS = 16
TOK_COLS = 16


def draw_features(key, part):
    key_base, key_chan = jax.random.split(key, 2)
    positions = jnp.arange(HEIGHT, dtype=jnp.float32)
    ramp = 1.0 + 2.0 * positions / max(HEIGHT - 1, 1)
    channel_scale = jnp.exp(jax.random.uniform(key_chan, (IMAGES, 1, 1, CHANNELS), minval=-0.7, maxval=0.7))
    base = jax.random.normal(key_base, (IMAGES, HEIGHT, COLS, CHANNELS))
    values = base * ramp[None, :, None, None] * channel_scale
    return jnp.clip(values, -12.0, 12.0).astype(jnp.bfloat16)


def block_levels(rng, shape, cuts, least, largest):
    def one(dim, shards_of):
        heights = jax.random.uniform(jax.random.fold_in(jax.random.fold_in(rng, 6), dim), (shards_of,), jnp.float32, least / len(cuts), largest / len(cuts))
        return jnp.repeat(jnp.exp(heights), shape[dim] // shards_of).reshape((-1,) + (1,) * (len(shape) - dim - 1))

    level = one(*cuts[0])
    for cut in cuts[1:]:
        level = level * one(*cut)
    return level


def noise(rng, dims, scale, most, cuts=(), kind=jnp.bfloat16):
    loudness = block_levels(rng, dims, cuts, -0.22, 0.18) if cuts else 1.0
    values = jax.random.normal(rng, dims, jnp.float32) * scale * loudness
    return jnp.minimum(jnp.maximum(values, -most), most).astype(kind)


def setup_inputs(seed: int = 0) -> dict:
    key_list = jax.random.split(jax.random.key(seed), 12)
    features = draw_features(jax.random.fold_in(key_list[11], 71), 0)
    norm_gain = jnp.clip(1.0 + 0.15 * jax.random.normal(key_list[1], (CHANNELS,), jnp.float32), 0.25, 1.75)
    norm_bias = noise(key_list[2], (CHANNELS,), 0.4, 2.5, (), jnp.float32)
    conv_weight = noise(key_list[3], (LATENT, 9 * CHANNELS), (9 * CHANNELS) ** -0.5, 0.09375)
    embed_weight = noise(key_list[4], (PATCH * PATCH * LATENT, WIDTH), (PATCH * PATCH * LATENT) ** -0.5, 1.5, (), jnp.float32)
    embed_bias = noise(key_list[5], (WIDTH,), 0.4, 2.5, (), jnp.float32)
    proj_in = noise(key_list[6], (WIDTH, PROJ), WIDTH ** -0.5, 0.1875, ((0, 16),))
    proj_in_bias = noise(key_list[7], (PROJ,), 0.4, 2.5, (), jnp.float32)
    proj_out = noise(key_list[8], (PROJ, ALIGN), PROJ ** -0.5, 0.125, ((0, 16),))
    proj_out_bias = noise(key_list[9], (ALIGN,), 0.4, 2.5, (), jnp.float32)
    targets = noise(key_list[10], (IMAGES, TOK_ROWS, TOK_COLS, ALIGN), 1.0, 6.0, ((0, 32), (1, 16)))
    return {"features": features, "norm_gain": norm_gain, "norm_bias": norm_bias, "conv_weight": conv_weight, "embed_weight": embed_weight, "embed_bias": embed_bias, "proj_in": proj_in, "proj_in_bias": proj_in_bias, "proj_out": proj_out, "proj_out_bias": proj_out_bias, "targets": targets}


EPS_NORM = 1e-06
EPS_UNIT = 1e-06

def swish_slope(values):
    sig = jax.nn.sigmoid(values)
    return sig * (1.0 + values * (1.0 - sig))

def one_image(feature_map, target_map, norm_gain, norm_bias, conv_weight, embed_weight, embed_bias, proj_in, proj_in_bias, proj_out, proj_out_bias):
    height, across, channels = feature_map.shape
    per_group = channels // GROUPS
    cell_count = height * across
    values = feature_map.astype(jnp.float32)
    grouped = values.reshape(cell_count, GROUPS, per_group)
    group_mean = lax.optimization_barrier(jnp.mean(grouped, axis=(0, 2), keepdims=True))
    centred = grouped - group_mean
    variance = lax.optimization_barrier(jnp.mean(centred * centred, axis=(0, 2), keepdims=True))
    inverse = lax.rsqrt(variance + EPS_NORM)
    normed = (centred * inverse).reshape(height, across, channels)
    shifted = normed * norm_gain + norm_bias
    active = (shifted * jax.nn.sigmoid(shifted)).astype(jnp.bfloat16)
    padded = jnp.pad(active, ((1, 1), (1, 1), (0, 0)))
    latent = jnp.zeros((cell_count, LATENT), jnp.float32)
    windows = []
    for position in range(9):
        row_off, col_off = (position // 3, position % 3)
        window = padded[row_off:row_off + height, col_off:col_off + across, :].reshape(cell_count, channels)
        windows.append(window)
        kernel = conv_weight[:, position * channels:(position + 1) * channels]
        latent = latent + lax.dot_general(window, kernel, (((1,), (1,)), ((), ())), preferred_element_type=jnp.float32)
    tok_rows = height // PATCH
    tok_cols = across // PATCH
    patches = latent.reshape(tok_rows, PATCH, tok_cols, PATCH, LATENT).transpose(0, 2, 1, 3, 4).reshape(tok_rows * tok_cols, PATCH * PATCH * LATENT)
    embedded = (jnp.dot(patches, embed_weight, precision=lax.Precision.HIGHEST) + embed_bias).astype(jnp.bfloat16)
    hidden_pre = jnp.dot(embedded, proj_in, preferred_element_type=jnp.float32) + proj_in_bias
    hidden_act = (hidden_pre * jax.nn.sigmoid(hidden_pre)).astype(jnp.bfloat16)
    projected = jnp.dot(hidden_act, proj_out, preferred_element_type=jnp.float32) + proj_out_bias
    target = target_map.reshape(tok_rows * tok_cols, -1).astype(jnp.float32)
    unit_target = target * lax.rsqrt(lax.optimization_barrier(jnp.sum(target * target, axis=1, keepdims=True)) + EPS_UNIT)
    inv_len = lax.rsqrt(lax.optimization_barrier(jnp.sum(projected * projected, axis=1, keepdims=True)) + EPS_UNIT)
    unit_proj = projected * inv_len
    cosine = lax.optimization_barrier(jnp.sum(unit_proj * unit_target, axis=1, keepdims=True))
    grad_out = (-inv_len * (unit_target - cosine * unit_proj)).astype(jnp.bfloat16)
    back_hidden = lax.dot_general(grad_out, proj_out, (((1,), (1,)), ((), ())), preferred_element_type=jnp.float32)
    grad_hidden = (back_hidden * swish_slope(hidden_pre)).astype(jnp.bfloat16)
    grad_embedded = lax.dot_general(grad_hidden, proj_in, (((1,), (1,)), ((), ())), preferred_element_type=jnp.float32)
    embed_part = lax.dot_general(patches, grad_embedded, (((0,), (0,)), ((), ())), precision=lax.Precision.HIGHEST)
    grad_patch = lax.dot_general(grad_embedded, embed_weight, (((1,), (1,)), ((), ())), precision=lax.Precision.HIGHEST)
    grad_latent = grad_patch.reshape(tok_rows, tok_cols, PATCH, PATCH, LATENT).transpose(0, 2, 1, 3, 4).reshape(height, across, LATENT).astype(jnp.bfloat16)
    grad_flat = grad_latent.reshape(cell_count, LATENT)
    grad_pad = jnp.pad(grad_latent, ((1, 1), (1, 1), (0, 0)))
    grad_active = jnp.zeros((cell_count, channels), jnp.float32)
    conv_parts = []
    for position in range(9):
        row_off, col_off = (position // 3, position % 3)
        conv_parts.append(lax.dot_general(grad_flat, windows[position], (((0,), (0,)), ((), ())), preferred_element_type=jnp.float32))
        back = grad_pad[2 - row_off:2 - row_off + height, 2 - col_off:2 - col_off + across, :].reshape(cell_count, LATENT)
        kernel = conv_weight[:, position * channels:(position + 1) * channels]
        grad_active = grad_active + jnp.dot(back, kernel, preferred_element_type=jnp.float32)
    conv_part = jnp.concatenate(conv_parts, axis=1)
    flat_shift = shifted.reshape(cell_count, channels)
    flat_normed = normed.reshape(cell_count, channels)
    grad_shift = grad_active * swish_slope(flat_shift)
    gain_part = lax.optimization_barrier(jnp.sum(grad_shift * flat_normed, axis=0))
    bias_part = lax.optimization_barrier(jnp.sum(grad_shift, axis=0))
    grad_norm = (grad_shift * norm_gain).reshape(cell_count, GROUPS, per_group)
    normed_groups = flat_normed.reshape(cell_count, GROUPS, per_group)
    first = lax.optimization_barrier(jnp.mean(grad_norm, axis=(0, 2), keepdims=True))
    second = lax.optimization_barrier(jnp.mean(grad_norm * normed_groups, axis=(0, 2), keepdims=True))
    grad_values = inverse * (grad_norm - first - normed_groups * second)
    grad_map = grad_values.reshape(height, across, channels).astype(jnp.bfloat16)
    return (grad_map, conv_part, gain_part, bias_part, embed_part)

def reference(features, norm_gain, norm_bias, conv_weight, embed_weight, embed_bias, proj_in, proj_in_bias, proj_out, proj_out_bias, targets):

    def step(pair):
        return one_image(pair[0], pair[1], norm_gain, norm_bias, conv_weight, embed_weight, embed_bias, proj_in, proj_in_bias, proj_out, proj_out_bias)
    grad_features, conv_parts, gain_parts, bias_parts, embed_parts = lax.map(step, (features, targets))
    return (grad_features, lax.optimization_barrier(jnp.sum(conv_parts, axis=0)), lax.optimization_barrier(jnp.sum(gain_parts, axis=0)), lax.optimization_barrier(jnp.sum(bias_parts, axis=0)), lax.optimization_barrier(jnp.sum(embed_parts, axis=0)))
```

```python
import jax
import jax.numpy as jnp
from jax import lax
from jax.experimental import pallas as pl
from jax.experimental.pallas import tpu as pltpu
from jax.sharding import PartitionSpec as P

GROUPS = 32
LATENT = 4
PATCH = 2
EPS_NORM = 1e-06
EPS_UNIT = 1e-06

XS, ZHI, CORES, ZLO, YS = 4, 2, 2, 8, 4

HIGH = lax.Precision.HIGHEST
F32 = jnp.float32
BF16 = jnp.bfloat16
TAPS = 9
SUB = 8
LANES = 128
STAT_ROWS = 16
CHUNK = 32
AT_EMBED, AT_GAIN, AT_STAT = 9, 17, 18
PARAM_ROWS = 24


def params(limit_mb=48):
    return pltpu.CompilerParams(vmem_limit_bytes=limit_mb << 20)


def vmem():
    return pl.BlockSpec(memory_space=pltpu.VMEM)


def sigmoid(v):
    return 0.5 + 0.5 * jnp.tanh(0.5 * v)


def nt(a, b, precision=None):
    return lax.dot_general(
        a, b, (((1,), (1,)), ((), ())), preferred_element_type=F32, precision=precision
    )


def nn(a, b, precision=None):
    return lax.dot_general(
        a, b, (((1,), (0,)), ((), ())), preferred_element_type=F32, precision=precision
    )


def iota(shape, dim):
    return lax.broadcasted_iota(jnp.int32, shape, dim)


def to_groups(channels, per_group, offset):
    shape = (channels, LANES)
    return (iota(shape, 0) // per_group + offset == iota(shape, 1)).astype(F32)


def from_groups(channels, per_group, offset):
    shape = (LANES, channels)
    return (iota(shape, 1) // per_group + offset == iota(shape, 0)).astype(F32)


def stats_kernel(f_ref, out_ref, sums, squares):
    images, _, channels = f_ref.shape
    sums[...] = jnp.zeros_like(sums)
    squares[...] = jnp.zeros_like(squares)
    for i in range(images):
        v = f_ref[i].astype(F32)
        sums[i : i + 1, :] = jnp.sum(v, axis=0, keepdims=True)
        squares[i : i + 1, :] = jnp.sum(v * v, axis=0, keepdims=True)
    per_group = channels // GROUPS
    total = nn(sums[...], to_groups(channels, per_group, 0), HIGH) + nn(
        squares[...], to_groups(channels, per_group, GROUPS), HIGH
    )
    for r in range(out_ref.shape[0]):
        out_ref[r] = total


def group_stats(features, peers):
    channels = features.shape[-1]
    return pl.pallas_call(
        stats_kernel,
        out_shape=jax.ShapeDtypeStruct((peers, STAT_ROWS, LANES), F32),
        in_specs=[vmem()],
        out_specs=vmem(),
        scratch_shapes=[pltpu.VMEM((STAT_ROWS, channels), F32)] * 2,
        compiler_params=params(),
        name="stats",
    )(features)


def lane_masks(shape, across):
    lane = iota(shape, 1)
    return lane % across, (lane // across) % 2


def roll(v, shift):
    return pltpu.roll(v, shift % v.shape[1], 1)


def conv_kernel(
    across, members, st_ref, f_ref, gain_ref, bias_ref, k_ref,
    lat_ref, up_ref, down_ref, mean_ref, inv_ref, act,
):
    images, cells, channels = f_ref.shape
    per_group = channels // GROUPS
    total = jnp.sum(st_ref[...], axis=0)
    mean = nn(total, from_groups(channels, per_group, 0), HIGH) * (1.0 / members)
    square = nn(total, from_groups(channels, per_group, GROUPS), HIGH) * (1.0 / members)
    inv = lax.rsqrt(jnp.maximum(square - mean * mean, 0.0) + EPS_NORM)
    mean_ref[...] = mean
    inv_ref[...] = inv
    gain, bias = gain_ref[...], bias_ref[...]
    for i in range(images):
        v = f_ref[i].astype(F32)
        shifted = (v - mean[i : i + 1]) * inv[i : i + 1] * gain + bias
        act[i * cells : (i + 1) * cells, :] = (shifted * sigmoid(shifted)).astype(BF16)
    taps = nt(k_ref[...], act[...])
    shape = (SUB, images * cells)
    col, row = lane_masks(shape, across)

    def tap(position):
        return taps[position * SUB : (position + 1) * SUB]

    def line(dy):
        low = jnp.where(col > 0, roll(tap(3 * dy), 1), 0.0)
        high = jnp.where(col < across - 1, roll(tap(3 * dy + 2), -1), 0.0)
        return tap(3 * dy + 1) + low + high

    first, middle, last = line(0), line(1), line(2)
    last_up, first_down = roll(last, -across), roll(first, across)
    lat_ref[...] = middle + jnp.where(row == 0, last_up, first_down)
    up_ref[...] = jnp.where(row == 1, roll(last, across), 0.0)
    down_ref[...] = jnp.where(row == 0, roll(first, -across), 0.0)


def conv_forward(stats, features, gain, bias, kernel_rows, across, members):
    images, cells, channels = features.shape
    line = jax.ShapeDtypeStruct((SUB, images * cells), F32)
    stat = jax.ShapeDtypeStruct((STAT_ROWS, channels), F32)
    return pl.pallas_call(
        lambda *refs: conv_kernel(across, members, *refs),
        out_shape=(line, line, line, stat, stat),
        in_specs=[vmem()] * 5,
        out_specs=(vmem(),) * 5,
        scratch_shapes=[pltpu.VMEM((images * cells, channels), BF16)],
        compiler_params=params(),
        name="conv",
    )(stats, features, gain, bias, kernel_rows)


def mlp_kernel(
    across, width, hidden, align, at_ref, lat_ref, below_ref, above_ref, target_ref,
    ew_ref, eb_ref, pib_ref, pob_ref,
    h0, p0, m0, l0, t0, h1, p1, m1, l1, t1,
    embed_ref, gl_ref, w_in, w_out, pre, emb, acc, grad_emb, sems,
):
    x, core = at_ref[0], at_ref[1]
    depth = width // (XS * ZHI * CORES)
    slab = hidden // (XS * ZHI * CORES)
    copies = []

    def place(piece, at, source_x, zhi, of_core):
        shard = lax.rem(source_x, XS) * (ZHI * CORES) + zhi * CORES + of_core
        lines = pl.ds(at, depth)

        def put(columns, into):
            copy = pltpu.make_async_copy(piece.at[lines, columns], into, sems.at[len(copies)])
            copy.start()
            copies.append(copy)

        put(pl.ds(0, hidden), w_in.at[pl.ds(pl.multiple_of(shard * depth, depth), depth), :])
        for part in range(slab // depth):
            begin = pl.multiple_of(shard * slab + part * depth, depth)
            put(pl.ds(hidden + part * align, align), w_out.at[pl.ds(begin, depth), :])

    for of_core, (own, plus, minus, low, high) in (
        (core, (h0, p0, m0, l0, t0)),
        (1 - core, (h1, p1, m1, l1, t1)),
    ):
        for piece, step in ((own, 0), (plus, 1), (minus, XS - 1)):
            for zhi in range(ZHI):
                place(piece, zhi * depth, x + step, zhi, of_core)
        place(low, 0, x + 2, 0, of_core)
        place(high, 0, x + 2, 1, of_core)

    lat = lat_ref[...] + below_ref[...] + above_ref[...]
    top = lat.astype(BF16)
    rest = lat - top.astype(F32)
    mid = rest.astype(BF16)
    low_part = (rest - mid.astype(F32)).astype(BF16)
    split = jnp.concatenate(
        [top.astype(F32), mid.astype(F32), low_part.astype(F32)], axis=0
    ).astype(BF16)
    cells = lat.shape[1]
    tokens = target_ref.shape[0]
    room = 256
    cols = across // PATCH

    def selection(u, v):
        shape = (cells, room)
        token = iota(shape, 1)
        lane = (token // cols) * (PATCH * across) + u * across + (token % cols) * PATCH + v
        return jnp.where((lane == iota(shape, 0)) & (token < tokens), 1.0, 0.0).astype(BF16)

    picks = [selection(u, v) for u in range(PATCH) for v in range(PATCH)]
    lines = []
    for pick in picks:
        got = nn(split, pick)
        lines.append(got[0:SUB] + got[SUB : 2 * SUB] + got[2 * SUB :])
    patches_t = jnp.concatenate(lines, axis=0)
    patches = patches_t.T
    emb[...] = (nn(patches, ew_ref[...], HIGH) + eb_ref[...])[:tokens].astype(BF16)

    for copy in copies:
        copy.wait()

    step = 512
    acc[...] = jnp.zeros_like(acc)

    @pl.loop(0, hidden // step)
    def _(tile):
        at = pl.ds(pl.multiple_of(tile * step, step), step)
        h = nn(emb[...], w_in[:, at]) + pib_ref[:, at]
        pre[:, at] = h
        acc[...] += nn((h * sigmoid(h)).astype(BF16), w_out[at, :])

    projected = acc[...] + pob_ref[...]
    target = target_ref[...].astype(F32)
    unit_target = target * lax.rsqrt(jnp.sum(target * target, axis=1, keepdims=True) + EPS_UNIT)
    inv_len = lax.rsqrt(jnp.sum(projected * projected, axis=1, keepdims=True) + EPS_UNIT)
    unit_proj = projected * inv_len
    cosine = jnp.sum(unit_proj * unit_target, axis=1, keepdims=True)
    grad_out = (-inv_len * (unit_target - cosine * unit_proj)).astype(BF16)
    grad_emb[...] = jnp.zeros_like(grad_emb)

    @pl.loop(0, hidden // step)
    def _(tile):
        at = pl.ds(pl.multiple_of(tile * step, step), step)
        back = nt(grad_out, w_out[at, :])
        h = pre[:, at]
        sig = sigmoid(h)
        grad_hidden = (back * (sig * (1.0 + h * (1.0 - sig)))).astype(BF16)
        grad_emb[0:tokens, :] += nt(grad_hidden, w_in[:, at])

    grad = grad_emb[...]
    embed_ref[...] = nn(patches_t, grad, HIGH)
    grad_patch = nt(ew_ref[...], grad, HIGH)
    total = jnp.zeros((SUB, cells), F32)
    for position, pick in enumerate(picks):
        part = grad_patch[position * SUB : (position + 1) * SUB].astype(BF16)
        total = total + nt(part, pick)
    gl_ref[...] = total


def projector(at, lat, below, above, target, ew, eb, pib, pob, pieces, across):
    rows, width = ew.shape
    hidden, align = pib.shape[1], pob.shape[1]
    tokens = target.shape[0]
    flops = 2 * tokens * (2 * width * hidden + 2 * hidden * align)
    return pl.pallas_call(
        lambda *refs: mlp_kernel(across, width, hidden, align, *refs),
        out_shape=(
            jax.ShapeDtypeStruct((rows, width), F32),
            jax.ShapeDtypeStruct(lat.shape, F32),
        ),
        in_specs=[pl.BlockSpec(memory_space=pltpu.SMEM)]
        + [vmem()] * 8
        + [pl.BlockSpec(memory_space=pl.ANY)] * len(pieces),
        out_specs=(vmem(), vmem()),
        scratch_shapes=[
            pltpu.VMEM((width, hidden), BF16),
            pltpu.VMEM((hidden, align), BF16),
            pltpu.VMEM((tokens, hidden), F32),
            pltpu.VMEM((tokens, width), BF16),
            pltpu.VMEM((tokens, align), F32),
            pltpu.VMEM((256, width), F32),
            pltpu.SemaphoreType.DMA((48,)),
        ],
        compiler_params=params(),
        cost_estimate=pl.CostEstimate(
            flops=flops, bytes_accessed=8 << 20, transcendentals=2 * tokens * hidden
        ),
        name="projector",
    )(at, lat, below, above, target, ew, eb, pib, pob, *pieces)


def back_kernel(
    across, gl_ref, before_ref, after_ref, f_ref, mean_ref, inv_ref, gain_ref, bias_ref,
    k_ref, embed_ref, send_ref, gs_ref, act, grads_t, by_bias, by_gain,
):
    images, cells, channels = f_ref.shape
    per_group = channels // GROUPS
    gl, before, after = gl_ref[...], before_ref[...], after_ref[...]
    col, row = lane_masks(gl.shape, across)
    lines = (
        jnp.where(row == 0, roll(gl, -across), roll(after, across)),
        gl,
        jnp.where(row == 0, roll(before, -across), roll(gl, across)),
    )
    parts = []
    for g in lines:
        parts.append(jnp.where(col < across - 1, roll(g, -1), 0.0))
        parts.append(g)
        parts.append(jnp.where(col > 0, roll(g, 1), 0.0))
    parts.append(jnp.zeros((LANES - TAPS * SUB, gl.shape[1]), F32))
    grads = jnp.concatenate(parts, axis=0)
    grads_t[...] = grads.T.astype(BF16)
    gain, bias = gain_ref[...], bias_ref[...]
    by_bias[...] = jnp.zeros_like(by_bias)
    by_gain[...] = jnp.zeros_like(by_gain)
    for i in range(images):
        at = slice(i * cells, (i + 1) * cells)
        v = f_ref[i].astype(F32)
        normed = (v - mean_ref[i : i + 1, :]) * inv_ref[i : i + 1, :]
        shifted = normed * gain + bias
        sig = sigmoid(shifted)
        act[at, :] = (shifted * sig).astype(BF16)
        grad_active = nn(grads_t[at, :], k_ref[...])
        gs = grad_active * (sig * (1.0 + shifted * (1.0 - sig)))
        gs_ref[i] = gs
        by_bias[i : i + 1, :] = jnp.sum(gs, axis=0, keepdims=True)
        by_gain[i : i + 1, :] = jnp.sum(gs * normed, axis=0, keepdims=True)
    conv = nn(grads.astype(BF16), act[...])
    stat = nn(by_bias[...] * gain, to_groups(channels, per_group, 0), HIGH) + nn(
        by_gain[...] * gain, to_groups(channels, per_group, GROUPS), HIGH
    )
    bias_part = jnp.sum(by_bias[...], axis=0, keepdims=True)
    gain_part = jnp.sum(by_gain[...], axis=0, keepdims=True)
    blocks = channels // LANES
    for r in range(send_ref.shape[0]):
        block, latent = r // LATENT, r % LATENT
        lanes = slice(block * LANES, (block + 1) * LANES)
        for position in range(TAPS):
            line = position * SUB + latent
            send_ref[r, position : position + 1, :] = conv[line : line + 1, lanes]
        lanes = slice((r // 2) * LANES, (r // 2 + 1) * LANES)
        for half in range(2):
            line = (r % 2) * 2 * SUB + half * SUB
            send_ref[r, AT_EMBED + half * LATENT : AT_EMBED + (half + 1) * LATENT, :] = embed_ref[
                line : line + LATENT, lanes
            ]
        one = gain_part if r < blocks else bias_part
        lanes = slice((r % blocks) * LANES, (r % blocks + 1) * LANES)
        send_ref[r, AT_GAIN : AT_GAIN + 1, :] = one[:, lanes]
        send_ref[r, AT_STAT : AT_STAT + images, :] = stat[0:images]
        send_ref[r, AT_STAT + images : CHUNK, :] = jnp.zeros(
            (CHUNK - AT_STAT - images, LANES), F32
        )


def conv_backward(gl, before, after, features, mean, inv, gain, bias, kernel_rows, embed, across, peers):
    images, cells, channels = features.shape
    return pl.pallas_call(
        lambda *refs: back_kernel(across, *refs),
        out_shape=(
            jax.ShapeDtypeStruct((peers, CHUNK, LANES), F32),
            jax.ShapeDtypeStruct((images, cells, channels), F32),
        ),
        in_specs=[vmem()] * 10,
        out_specs=(vmem(), vmem()),
        scratch_shapes=[
            pltpu.VMEM((images * cells, channels), BF16),
            pltpu.VMEM((images * cells, LANES), BF16),
            pltpu.VMEM((STAT_ROWS, channels), F32),
            pltpu.VMEM((STAT_ROWS, channels), F32),
        ],
        compiler_params=params(),
        name="back",
    )(gl, before, after, features, mean, inv, gain, bias, kernel_rows, embed)


def last_kernel(members, got_ref, f_ref, mean_ref, inv_ref, gain_ref, gs_ref, out_ref):
    images, _, channels = f_ref.shape
    per_group = channels // GROUPS
    total = jnp.sum(got_ref[:, STAT_ROWS:CHUNK, :], axis=0)
    first = nn(total, from_groups(channels, per_group, 0), HIGH) * (1.0 / members)
    second = nn(total, from_groups(channels, per_group, GROUPS), HIGH) * (1.0 / members)
    gain = gain_ref[...]
    skip = AT_STAT - STAT_ROWS
    for i in range(images):
        v = f_ref[i].astype(F32)
        inv = inv_ref[i : i + 1, :]
        normed = (v - mean_ref[i : i + 1, :]) * inv
        j = i + skip
        out = inv * (gs_ref[i] * gain - first[j : j + 1] - normed * second[j : j + 1])
        out_ref[i] = out.astype(BF16)


def feature_grad(got, features, mean, inv, gain, grad_shift, members):
    return pl.pallas_call(
        lambda *refs: last_kernel(members, *refs),
        out_shape=jax.ShapeDtypeStruct(features.shape, BF16),
        in_specs=[vmem()] * 6,
        out_specs=vmem(),
        compiler_params=params(),
        cost_estimate=pl.CostEstimate(
            flops=10 * features.size, bytes_accessed=8 * features.size, transcendentals=0
        ),
        name="last",
    )(got, features, mean, inv, gain, grad_shift)


def unpack_kernel(got_ref, conv_ref, gain_ref, bias_ref, embed_ref):
    channels = gain_ref.shape[1]
    blocks = channels // LANES
    for r in range(got_ref.shape[0]):
        block, latent = r // LATENT, r % LATENT
        for position in range(TAPS):
            at = position * channels + block * LANES
            conv_ref[latent : latent + 1, at : at + LANES] = got_ref[r, position : position + 1, :]
        lanes = slice((r // 2) * LANES, (r // 2 + 1) * LANES)
        line = (r % 2) * SUB
        embed_ref[line : line + SUB, lanes] = got_ref[r, AT_EMBED : AT_EMBED + SUB, :]
        lanes = slice((r % blocks) * LANES, (r % blocks + 1) * LANES)
        if r < blocks:
            gain_ref[:, lanes] = got_ref[r, AT_GAIN : AT_GAIN + 1, :]
        elif r < 2 * blocks:
            bias_ref[:, lanes] = got_ref[r, AT_GAIN : AT_GAIN + 1, :]


def unpack(got, channels, width):
    return pl.pallas_call(
        unpack_kernel,
        out_shape=(
            jax.ShapeDtypeStruct((LATENT, TAPS * channels), F32),
            jax.ShapeDtypeStruct((1, channels), F32),
            jax.ShapeDtypeStruct((1, channels), F32),
            jax.ShapeDtypeStruct((PATCH * PATCH * LATENT, width), F32),
        ),
        in_specs=[vmem()],
        out_specs=(vmem(),) * 4,
        compiler_params=params(),
        name="unpack",
    )(got)


def from_everyone(value, axis):
    length = lax.axis_size(axis)
    return lax.all_to_all(
        jnp.broadcast_to(value[None], (length, *value.shape)), axis, 0, 0, tiled=True
    )


def moved(value, where):
    pairs = []
    for x in range(XS):
        for zhi in range(ZHI):
            for core in range(CORES):
                for zlo in range(ZLO):
                    for y in range(YS):
                        a, b, c, d, e = where(x, zhi, core, zlo, y)
                        source = ((x * ZHI + zhi) * CORES + core) * (ZLO * YS) + zlo * YS + y
                        goal = ((a * ZHI + b) * CORES + c) * (ZLO * YS) + d * YS + e
                        pairs.append((source, goal))
    return lax.ppermute(value, ("rows", "batch"), pairs)


def gathered(shard):
    depth = shard.shape[0]
    rows, batch = lax.axis_index("rows"), lax.axis_index("batch")
    zhi, y = (rows // CORES) % ZHI, batch % YS
    part = depth // YS
    mine = lax.dynamic_slice_in_dim(shard, y * part, part, axis=0)
    cross = moved(mine, lambda x, h, c, d, y: (x, 1 - h, c, ZLO - 1 - d, y))
    other = moved(cross, lambda x, h, c, d, y: (x, h, c, d, y ^ 1))
    even = y % 2 == 0
    pair = jnp.concatenate(
        [jnp.where(even, cross, other), jnp.where(even, other, cross)], axis=0
    )
    far = moved(pair, lambda x, h, c, d, y: (x, h, c, d, YS - 1 - y))
    low = y < 2
    across = jnp.concatenate([jnp.where(low, pair, far), jnp.where(low, far, pair)], axis=0)
    first = zhi == 0
    both = jnp.concatenate(
        [jnp.where(first, shard, across), jnp.where(first, across, shard)], axis=0
    )
    plus = moved(both, lambda x, h, c, d, y: ((x + XS - 1) % XS, h, c, d, y))
    minus = moved(both, lambda x, h, c, d, y: ((x + 1) % XS, h, c, d, y))
    low_half = moved(plus[:depth], lambda x, h, c, d, y: ((x + XS - 1) % XS, h, c, d, y))
    high_half = moved(minus[depth:], lambda x, h, c, d, y: ((x + 1) % XS, h, c, d, y))
    held = [both, plus, minus, low_half, high_half]
    swapped = [moved(v, lambda x, h, c, d, y: (x, h, 1 - c, d, y)) for v in held]
    return held + swapped


def neighbours(up, down):
    count = lax.axis_size("rows")
    forward = [(i, i + 1) for i in range(count - 1)]
    backward = [(b, a) for a, b in forward]
    return lax.ppermute(up, "rows", backward), lax.ppermute(down, "rows", forward)


def shards(
    features,
    norm_gain,
    norm_bias,
    conv_weight,
    embed_weight,
    embed_bias,
    proj_in,
    proj_in_bias,
    proj_out,
    proj_out_bias,
    targets,
):
    images, height, across, channels = features.shape
    width, align = embed_weight.shape[1], proj_out.shape[1]
    peers = lax.axis_size("rows")
    members = peers * height * across * (channels // GROUPS)
    flat = features.reshape(images, height * across, channels)
    gain, bias = norm_gain.reshape(1, channels), norm_bias.reshape(1, channels)
    depth = proj_in.shape[0]
    shard = jnp.concatenate(
        [proj_in] + [proj_out[at : at + depth] for at in range(0, proj_out.shape[0], depth)], axis=1
    )
    pieces = gathered(shard)
    taps = conv_weight.reshape(LATENT, TAPS, channels).transpose(1, 0, 2)
    taps = jnp.pad(taps, ((0, 0), (0, SUB - LATENT), (0, 0))).reshape(TAPS * SUB, channels)
    taps_full = jnp.pad(taps, ((0, LANES - TAPS * SUB), (0, 0)))
    spread = jnp.pad(
        embed_weight.reshape(PATCH * PATCH, LATENT, width), ((0, 0), (0, SUB - LATENT), (0, 0))
    ).reshape(PATCH * PATCH * SUB, width)

    stats = lax.all_to_all(group_stats(flat, peers), "rows", 0, 0, tiled=True)
    lat, up, down, mean, inv = conv_forward(stats, flat, gain, bias, taps, across, members)
    above, below = neighbours(up, down)
    rows = lax.axis_index("rows")
    at = jnp.stack([rows // (ZHI * CORES), rows % CORES]).astype(jnp.int32)
    target = targets.reshape(-1, align)
    embed_part, grad_lat = projector(
        at, lat, below, above, target, spread, embed_bias.reshape(1, -1),
        proj_in_bias.reshape(1, -1), proj_out_bias.reshape(1, -1), pieces, across,
    )
    after, before = neighbours(grad_lat, grad_lat)
    send, grad_shift = conv_backward(
        grad_lat, before, after, flat, mean, inv, gain, bias, taps_full, embed_part, across, peers
    )
    got = lax.all_to_all(send, "rows", 0, 0, tiled=True)
    chunk = jnp.sum(got[:, :PARAM_ROWS], axis=0)
    grad_features = feature_grad(got, flat, mean, inv, gain, grad_shift, members)
    chunk = jnp.sum(from_everyone(chunk, "batch"), axis=0)
    everything = from_everyone(chunk, "rows")
    grad_conv, grad_gain, grad_bias, grad_embed = unpack(everything, channels, width)
    return (
        grad_features.reshape(features.shape),
        grad_conv,
        grad_gain.reshape(channels),
        grad_bias.reshape(channels),
        grad_embed,
    )


def solution(mesh):
    in_specs = (
        P("batch", "rows", None, None),
        P(),
        P(),
        P(),
        P(),
        P(),
        P("rows", None),
        P(),
        P("rows", None),
        P(),
        P("batch", "rows", None, None),
    )
    out_specs = (P("batch", "rows", None, None), P(), P(), P(), P())
    return jax.shard_map(shards, mesh=mesh, in_specs=in_specs, out_specs=out_specs, check_vma=False)
```

```python
import jax
import jax.numpy as jnp
from jax import lax
from jax.experimental import pallas as pl
from jax.experimental.pallas import tpu as pltpu
from jax.sharding import PartitionSpec as P

GROUPS = 32
LATENT = 4
PATCH = 2
EPS_NORM = 1e-06
EPS_UNIT = 1e-06

XS, ZHI, CORES, ZLO, YS = 4, 2, 2, 8, 4

HIGH = lax.Precision.HIGHEST
F32 = jnp.float32
BF16 = jnp.bfloat16
TAPS = 9
SUB = 8
LANES = 128
STAT_ROWS = 16
CHUNKS, CHUNK_ROWS, ALL_ROWS = 32, 16, 32


def params(limit_mb=48):
    return pltpu.CompilerParams(vmem_limit_bytes=limit_mb << 20)


def vmem():
    return pl.BlockSpec(memory_space=pltpu.VMEM)


def sigmoid(v):
    return 0.5 + 0.5 * jnp.tanh(0.5 * v)


def nt(a, b, precision=None):
    return lax.dot_general(
        a, b, (((1,), (1,)), ((), ())), preferred_element_type=F32, precision=precision
    )


def nn(a, b, precision=None):
    return lax.dot_general(
        a, b, (((1,), (0,)), ((), ())), preferred_element_type=F32, precision=precision
    )


def iota(shape, dim):
    return lax.broadcasted_iota(jnp.int32, shape, dim)


def to_groups(channels, per_group, offset):
    shape = (channels, LANES)
    return (iota(shape, 0) // per_group + offset == iota(shape, 1)).astype(F32)


def from_groups(channels, per_group, offset):
    shape = (LANES, channels)
    return (iota(shape, 1) // per_group + offset == iota(shape, 0)).astype(F32)


def pack_stats(total):
    lane = iota((SUB, LANES), 1)
    return jnp.where(lane < LANES // 2, total[:SUB], pltpu.roll(total[SUB:], LANES // 2, 1))


def unpack_stats(packed):
    return jnp.concatenate([packed, pltpu.roll(packed, LANES // 2, 1)], axis=0)


def halves(packed):
    top = packed.astype(BF16).astype(F32)
    return jnp.concatenate([top, packed - top], axis=0).astype(BF16)


def stats_kernel(f_ref, out_ref, sums, squares):
    images, _, channels = f_ref.shape
    sums[...] = jnp.zeros_like(sums)
    squares[...] = jnp.zeros_like(squares)
    for i in range(images):
        v = f_ref[i].astype(F32)
        sums[i : i + 1, :] = jnp.sum(v, axis=0, keepdims=True)
        squares[i : i + 1, :] = jnp.sum(v * v, axis=0, keepdims=True)
    per_group = channels // GROUPS
    total = nn(sums[...], to_groups(channels, per_group, 0), HIGH) + nn(
        squares[...], to_groups(channels, per_group, GROUPS), HIGH
    )
    packed = pack_stats(total)
    for r in range(out_ref.shape[0]):
        out_ref[r] = packed


def group_stats(features, peers):
    channels = features.shape[-1]
    return pl.pallas_call(
        stats_kernel,
        out_shape=jax.ShapeDtypeStruct((peers, SUB, LANES), F32),
        in_specs=[vmem()],
        out_specs=vmem(),
        scratch_shapes=[pltpu.VMEM((STAT_ROWS, channels), F32)] * 2,
        compiler_params=params(),
        name="stats",
    )(features)


def lane_masks(shape, across):
    lane = iota(shape, 1)
    return lane % across, (lane // across) % 2


def roll(v, shift):
    return pltpu.roll(v, shift % v.shape[1], 1)


def conv_kernel(
    across, members, st_ref, f_ref, gain_ref, bias_ref, k_ref,
    lat_ref, up_ref, down_ref, mean_ref, inv_ref, act,
):
    images, cells, channels = f_ref.shape
    per_group = channels // GROUPS
    total = unpack_stats(jnp.sum(st_ref[...], axis=0))
    mean = nn(total, from_groups(channels, per_group, 0), HIGH) * (1.0 / members)
    square = nn(total, from_groups(channels, per_group, GROUPS), HIGH) * (1.0 / members)
    inv = lax.rsqrt(jnp.maximum(square - mean * mean, 0.0) + EPS_NORM)
    mean_ref[...] = mean
    inv_ref[...] = inv
    gain, bias = gain_ref[...], bias_ref[...]
    for i in range(images):
        v = f_ref[i].astype(F32)
        shifted = (v - mean[i : i + 1]) * inv[i : i + 1] * gain + bias
        act[i * cells : (i + 1) * cells, :] = (shifted * sigmoid(shifted)).astype(BF16)
    taps = nt(k_ref[...], act[...])
    shape = (SUB, images * cells)
    col, row = lane_masks(shape, across)

    def tap(position):
        return taps[position * SUB : (position + 1) * SUB]

    def line(dy):
        low = jnp.where(col > 0, roll(tap(3 * dy), 1), 0.0)
        high = jnp.where(col < across - 1, roll(tap(3 * dy + 2), -1), 0.0)
        return tap(3 * dy + 1) + low + high

    first, middle, last = line(0), line(1), line(2)
    last_up, first_down = roll(last, -across), roll(first, across)
    lat_ref[...] = middle + jnp.where(row == 0, last_up, first_down)
    up_ref[...] = jnp.where(row == 1, roll(last, across), 0.0)
    down_ref[...] = jnp.where(row == 0, roll(first, -across), 0.0)


def conv_forward(stats, features, gain, bias, kernel_rows, across, members):
    images, cells, channels = features.shape
    line = jax.ShapeDtypeStruct((SUB, images * cells), F32)
    stat = jax.ShapeDtypeStruct((STAT_ROWS, channels), F32)
    return pl.pallas_call(
        lambda *refs: conv_kernel(across, members, *refs),
        out_shape=(line, line, line, stat, stat),
        in_specs=[vmem()] * 5,
        out_specs=(vmem(),) * 5,
        scratch_shapes=[pltpu.VMEM((images * cells, channels), BF16)],
        compiler_params=params(),
        name="conv",
    )(stats, features, gain, bias, kernel_rows)


def mlp_kernel(
    across, width, hidden, align, at_ref, lat_ref, below_ref, above_ref, target_ref,
    ew_ref, eb_ref, pib_ref, pob_ref,
    own, cross, own_other, cross_other,
    embed_ref, gl_ref, w_in, w_out, pre, emb, acc, grad_emb, sems,
):
    zhi, core = at_ref[0], at_ref[1]
    depth = width // (XS * ZHI * CORES)
    slab = hidden // (XS * ZHI * CORES)
    copies = []

    for piece, of_zhi, of_core in (
        (own, zhi, core),
        (own_other, zhi, 1 - core),
        (cross, 1 - zhi, core),
        (cross_other, 1 - zhi, 1 - core),
    ):
        for x in range(XS):
            shard = x * (ZHI * CORES) + of_zhi * CORES + of_core
            lines = pl.ds(x * depth, depth)

            def put(columns, into):
                copy = pltpu.make_async_copy(piece.at[lines, columns], into, sems.at[len(copies)])
                copy.start()
                copies.append(copy)

            put(pl.ds(0, hidden), w_in.at[pl.ds(pl.multiple_of(shard * depth, depth), depth), :])
            for part in range(slab // depth):
                begin = pl.multiple_of(shard * slab + part * depth, depth)
                put(pl.ds(hidden + part * align, align), w_out.at[pl.ds(begin, depth), :])

    lat = lat_ref[...] + below_ref[...] + above_ref[...]
    top = lat.astype(BF16)
    rest = lat - top.astype(F32)
    mid = rest.astype(BF16)
    low_part = (rest - mid.astype(F32)).astype(BF16)
    split = jnp.concatenate(
        [top.astype(F32), mid.astype(F32), low_part.astype(F32)], axis=0
    ).astype(BF16)
    cells = lat.shape[1]
    tokens = target_ref.shape[0]
    room = 256
    cols = across // PATCH

    def selection(u, v):
        shape = (cells, room)
        token = iota(shape, 1)
        lane = (token // cols) * (PATCH * across) + u * across + (token % cols) * PATCH + v
        return jnp.where((lane == iota(shape, 0)) & (token < tokens), 1.0, 0.0).astype(BF16)

    picks = [selection(u, v) for u in range(PATCH) for v in range(PATCH)]
    lines = []
    for pick in picks:
        got = nn(split, pick)
        lines.append(got[0:SUB] + got[SUB : 2 * SUB] + got[2 * SUB :])
    patches_t = jnp.concatenate(lines, axis=0)
    patches = patches_t.T
    emb[...] = (nn(patches, ew_ref[...], HIGH) + eb_ref[...])[:tokens].astype(BF16)

    for copy in copies:
        copy.wait()

    step = 512
    acc[...] = jnp.zeros_like(acc)

    @pl.loop(0, hidden // step)
    def _(tile):
        at = pl.ds(pl.multiple_of(tile * step, step), step)
        h = nn(emb[...], w_in[:, at]) + pib_ref[:, at]
        pre[:, at] = h
        acc[...] += nn((h * sigmoid(h)).astype(BF16), w_out[at, :])

    projected = acc[...] + pob_ref[...]
    target = target_ref[...].astype(F32)
    unit_target = target * lax.rsqrt(jnp.sum(target * target, axis=1, keepdims=True) + EPS_UNIT)
    inv_len = lax.rsqrt(jnp.sum(projected * projected, axis=1, keepdims=True) + EPS_UNIT)
    unit_proj = projected * inv_len
    cosine = jnp.sum(unit_proj * unit_target, axis=1, keepdims=True)
    grad_out = (-inv_len * (unit_target - cosine * unit_proj)).astype(BF16)
    grad_emb[...] = jnp.zeros_like(grad_emb)

    @pl.loop(0, hidden // step)
    def _(tile):
        at = pl.ds(pl.multiple_of(tile * step, step), step)
        back = nt(grad_out, w_out[at, :])
        h = pre[:, at]
        sig = sigmoid(h)
        grad_hidden = (back * (sig * (1.0 + h * (1.0 - sig)))).astype(BF16)
        grad_emb[0:tokens, :] += nt(grad_hidden, w_in[:, at])

    grad = grad_emb[...]
    embed_ref[...] = nn(patches_t, grad, HIGH)
    grad_patch = nt(ew_ref[...], grad, HIGH)
    total = jnp.zeros((SUB, cells), F32)
    for position, pick in enumerate(picks):
        part = grad_patch[position * SUB : (position + 1) * SUB].astype(BF16)
        total = total + nt(part, pick)
    gl_ref[...] = total


def projector(at, lat, below, above, target, ew, eb, pib, pob, pieces, across):
    rows, width = ew.shape
    hidden, align = pib.shape[1], pob.shape[1]
    tokens = target.shape[0]
    flops = 2 * tokens * (2 * width * hidden + 2 * hidden * align)
    return pl.pallas_call(
        lambda *refs: mlp_kernel(across, width, hidden, align, *refs),
        out_shape=(
            jax.ShapeDtypeStruct((rows, width), F32),
            jax.ShapeDtypeStruct(lat.shape, F32),
        ),
        in_specs=[pl.BlockSpec(memory_space=pltpu.SMEM)]
        + [vmem()] * 8
        + [pl.BlockSpec(memory_space=pl.ANY)] * len(pieces),
        out_specs=(vmem(), vmem()),
        scratch_shapes=[
            pltpu.VMEM((width, hidden), BF16),
            pltpu.VMEM((hidden, align), BF16),
            pltpu.VMEM((tokens, hidden), F32),
            pltpu.VMEM((tokens, width), BF16),
            pltpu.VMEM((tokens, align), F32),
            pltpu.VMEM((256, width), F32),
            pltpu.SemaphoreType.DMA((48,)),
        ],
        compiler_params=params(),
        cost_estimate=pl.CostEstimate(
            flops=flops, bytes_accessed=8 << 20, transcendentals=2 * tokens * hidden
        ),
        name="projector",
    )(at, lat, below, above, target, ew, eb, pib, pob, *pieces)


def back_kernel(
    across, gl_ref, before_ref, after_ref, f_ref, mean_ref, inv_ref, gain_ref, bias_ref,
    k_ref, embed_ref, send_ref, gs_ref, act, grads_t, by_bias, by_gain, pack,
):
    images, cells, channels = f_ref.shape
    per_group = channels // GROUPS
    gl, before, after = gl_ref[...], before_ref[...], after_ref[...]
    col, row = lane_masks(gl.shape, across)
    lines = (
        jnp.where(row == 0, roll(gl, -across), roll(after, across)),
        gl,
        jnp.where(row == 0, roll(before, -across), roll(gl, across)),
    )
    parts = []
    for g in lines:
        parts.append(jnp.where(col < across - 1, roll(g, -1), 0.0))
        parts.append(g)
        parts.append(jnp.where(col > 0, roll(g, 1), 0.0))
    parts.append(jnp.zeros((LANES - TAPS * SUB, gl.shape[1]), F32))
    grads = jnp.concatenate(parts, axis=0)
    grads_t[...] = grads.T.astype(BF16)
    gain, bias = gain_ref[...], bias_ref[...]
    by_bias[...] = jnp.zeros_like(by_bias)
    by_gain[...] = jnp.zeros_like(by_gain)
    for i in range(images):
        at = slice(i * cells, (i + 1) * cells)
        v = f_ref[i].astype(F32)
        normed = (v - mean_ref[i : i + 1, :]) * inv_ref[i : i + 1, :]
        shifted = normed * gain + bias
        sig = sigmoid(shifted)
        act[at, :] = (shifted * sig).astype(BF16)
        grad_active = nn(grads_t[at, :], k_ref[...])
        gs = grad_active * (sig * (1.0 + shifted * (1.0 - sig)))
        gs_ref[i] = gs
        by_bias[i : i + 1, :] = jnp.sum(gs, axis=0, keepdims=True)
        by_gain[i : i + 1, :] = jnp.sum(gs * normed, axis=0, keepdims=True)
    conv = nn(grads.astype(BF16), act[...])
    stat = nn(by_bias[...] * gain, to_groups(channels, per_group, 0), HIGH) + nn(
        by_gain[...] * gain, to_groups(channels, per_group, GROUPS), HIGH
    )
    bias_part = jnp.sum(by_bias[...], axis=0, keepdims=True)
    gain_part = jnp.sum(by_gain[...], axis=0, keepdims=True)
    packed = halves(pack_stats(stat))
    for r in range(CHUNKS):
        send_ref[r, CHUNK_ROWS:ALL_ROWS, :] = packed
    blocks = channels // LANES
    half = CHUNKS // 2
    pack[...] = jnp.zeros_like(pack)
    for r in range(half):
        block, latent = r // LATENT, r % LATENT
        lanes = slice(block * LANES, (block + 1) * LANES)
        for position in range(TAPS):
            line = position * SUB + latent
            pack[r, position : position + 1, :] = conv[line : line + 1, lanes]
        lanes = slice((r // 2) * LANES, (r // 2 + 1) * LANES)
        for part in range(2):
            line = (r % 2) * 2 * SUB + part * SUB
            pack[half + r, part * LATENT : (part + 1) * LATENT, :] = embed_ref[
                line : line + LATENT, lanes
            ]
        if r < 2 * blocks:
            one = gain_part if r < blocks else bias_part
            lanes = slice((r % blocks) * LANES, (r % blocks + 1) * LANES)
            pack[half + r, SUB : SUB + 1, :] = one[:, lanes]
    for r in range(CHUNKS):
        send_ref[r, 0:CHUNK_ROWS, :] = pack[r].astype(BF16)


def conv_backward(gl, before, after, features, mean, inv, gain, bias, kernel_rows, embed, across):
    images, cells, channels = features.shape
    return pl.pallas_call(
        lambda *refs: back_kernel(across, *refs),
        out_shape=(
            jax.ShapeDtypeStruct((CHUNKS, ALL_ROWS, LANES), BF16),
            jax.ShapeDtypeStruct((images, cells, channels), F32),
        ),
        in_specs=[vmem()] * 10,
        out_specs=(vmem(),) * 2,
        scratch_shapes=[
            pltpu.VMEM((images * cells, channels), BF16),
            pltpu.VMEM((images * cells, LANES), BF16),
            pltpu.VMEM((STAT_ROWS, channels), F32),
            pltpu.VMEM((STAT_ROWS, channels), F32),
            pltpu.VMEM((CHUNKS, CHUNK_ROWS, LANES), F32),
        ],
        compiler_params=params(),
        name="back",
    )(gl, before, after, features, mean, inv, gain, bias, kernel_rows, embed)


def last_kernel(members, got_ref, f_ref, mean_ref, inv_ref, gain_ref, gs_ref, out_ref):
    images, _, channels = f_ref.shape
    per_group = channels // GROUPS
    total = unpack_stats(got_ref[...])
    first = nn(total, from_groups(channels, per_group, 0), HIGH) * (1.0 / members)
    second = nn(total, from_groups(channels, per_group, GROUPS), HIGH) * (1.0 / members)
    gain = gain_ref[...]
    for i in range(images):
        v = f_ref[i].astype(F32)
        inv = inv_ref[i : i + 1, :]
        normed = (v - mean_ref[i : i + 1, :]) * inv
        out = inv * (gs_ref[i] * gain - first[i : i + 1] - normed * second[i : i + 1])
        out_ref[i] = out.astype(BF16)


def feature_grad(got, features, mean, inv, gain, grad_shift, members):
    return pl.pallas_call(
        lambda *refs: last_kernel(members, *refs),
        out_shape=jax.ShapeDtypeStruct(features.shape, BF16),
        in_specs=[vmem()] * 6,
        out_specs=vmem(),
        compiler_params=params(),
        cost_estimate=pl.CostEstimate(
            flops=10 * features.size, bytes_accessed=8 * features.size, transcendentals=0
        ),
        name="last",
    )(got, features, mean, inv, gain, grad_shift)


def plane_kernel(at_ref, got_ref, out_ref):
    chunk = jnp.zeros((CHUNK_ROWS, LANES), F32)
    stat = jnp.zeros((SUB, LANES), F32)
    for r in range(CHUNKS):
        chunk = chunk + got_ref[r, 0:CHUNK_ROWS, :].astype(F32)
        pair = got_ref[r, CHUNK_ROWS:ALL_ROWS, :].astype(F32)
        stat = stat + jnp.where(at_ref[2] == (r // CORES) % YS, pair[:SUB] + pair[SUB:], 0.0)
    chunk, stat = chunk.astype(BF16), halves(stat)
    for r in range(out_ref.shape[0]):
        out_ref[r, 0:CHUNK_ROWS, :] = chunk
        out_ref[r, CHUNK_ROWS:ALL_ROWS, :] = stat


def plane_total(at, got):
    return pl.pallas_call(
        plane_kernel,
        out_shape=jax.ShapeDtypeStruct((ZHI * ZLO, ALL_ROWS, LANES), BF16),
        in_specs=[pl.BlockSpec(memory_space=pltpu.SMEM), vmem()],
        out_specs=vmem(),
        compiler_params=params(),
        name="plane",
    )(at, got)


def column_kernel(at_ref, got_ref, out_ref, stat_ref):
    chunk = jnp.zeros((CHUNK_ROWS, LANES), F32)
    stat = jnp.zeros((SUB, LANES), F32)
    for r in range(ZHI * ZLO):
        chunk = chunk + got_ref[r, 0:CHUNK_ROWS, :].astype(F32)
        pair = got_ref[r, CHUNK_ROWS:ALL_ROWS, :].astype(F32)
        stat = stat + jnp.where(at_ref[3] == r % ZLO, pair[:SUB] + pair[SUB:], 0.0)
    chunk = chunk.astype(BF16)
    for r in range(out_ref.shape[0]):
        out_ref[r] = chunk
    stat_ref[...] = stat


def column_total(at, got):
    return pl.pallas_call(
        column_kernel,
        out_shape=(
            jax.ShapeDtypeStruct((CHUNKS, CHUNK_ROWS, LANES), BF16),
            jax.ShapeDtypeStruct((SUB, LANES), F32),
        ),
        in_specs=[pl.BlockSpec(memory_space=pltpu.SMEM), vmem()],
        out_specs=(vmem(), vmem()),
        compiler_params=params(),
        name="column",
    )(at, got)


def unpack_kernel(got_ref, conv_ref, gain_ref, bias_ref, embed_ref, wide):
    channels = gain_ref.shape[1]
    blocks = channels // LANES
    half = CHUNKS // 2
    wide[...] = got_ref[...].astype(F32)
    for r in range(half):
        block, latent = r // LATENT, r % LATENT
        for position in range(TAPS):
            at = position * channels + block * LANES
            conv_ref[latent : latent + 1, at : at + LANES] = wide[r, position : position + 1, :]
        lanes = slice((r // 2) * LANES, (r // 2 + 1) * LANES)
        line = (r % 2) * SUB
        embed_ref[line : line + SUB, lanes] = wide[half + r, 0:SUB, :]
        lanes = slice((r % blocks) * LANES, (r % blocks + 1) * LANES)
        if r < blocks:
            gain_ref[:, lanes] = wide[half + r, SUB : SUB + 1, :]
        elif r < 2 * blocks:
            bias_ref[:, lanes] = wide[half + r, SUB : SUB + 1, :]


def unpack(got, channels, width):
    return pl.pallas_call(
        unpack_kernel,
        out_shape=(
            jax.ShapeDtypeStruct((LATENT, TAPS * channels), F32),
            jax.ShapeDtypeStruct((1, channels), F32),
            jax.ShapeDtypeStruct((1, channels), F32),
            jax.ShapeDtypeStruct((PATCH * PATCH * LATENT, width), F32),
        ),
        in_specs=[vmem()],
        out_specs=(vmem(),) * 4,
        scratch_shapes=[pltpu.VMEM(got.shape, F32)],
        compiler_params=params(),
        name="unpack",
    )(got)


def device(x, zhi, core, zlo, y):
    return ((x * ZHI + zhi) * CORES + core) * (ZLO * YS) + zlo * YS + y


BOTH = ("rows", "batch")
PLANE = [
    [device(x, h, c, d, y) for x in range(XS) for y in range(YS) for c in range(CORES)]
    for h in range(ZHI)
    for d in range(ZLO)
]
SHEET = [
    [device(x, h, c, d, y) for x in range(XS) for y in range(YS)]
    for h in range(ZHI)
    for d in range(ZLO)
    for c in range(CORES)
]
COLUMN = [
    [device(x, h, c, d, y) for h in range(ZHI) for d in range(ZLO)]
    for x in range(XS)
    for y in range(YS)
    for c in range(CORES)
]


def exchanged(value, groups):
    return lax.all_to_all(value, BOTH, 0, 0, axis_index_groups=groups, tiled=True)


def moved(value, where):
    pairs = []
    for x in range(XS):
        for zhi in range(ZHI):
            for core in range(CORES):
                for zlo in range(ZLO):
                    for y in range(YS):
                        a, b, c, d, e = where(x, zhi, core, zlo, y)
                        pairs.append((device(x, zhi, core, zlo, y), device(a, b, c, d, e)))
    return lax.ppermute(value, ("rows", "batch"), pairs)


def crossed(shard):
    y = lax.axis_index("batch") % YS
    part = shard.shape[0] // YS
    mine = lax.dynamic_slice_in_dim(shard, y * part, part, axis=0)
    return mine, moved(mine, lambda x, h, c, d, y: (x, 1 - h, c, ZLO - 1 - d, y))


def sheet(part):
    return lax.all_gather(part, BOTH, axis_index_groups=SHEET, tiled=True)


def swapped(value):
    return moved(value, lambda x, h, c, d, y: (x, h, 1 - c, d, y))


def neighbours(up, down):
    count = lax.axis_size("rows")
    forward = [(i, i + 1) for i in range(count - 1)]
    backward = [(b, a) for a, b in forward]
    return lax.ppermute(up, "rows", backward), lax.ppermute(down, "rows", forward)


def shards(
    features,
    norm_gain,
    norm_bias,
    conv_weight,
    embed_weight,
    embed_bias,
    proj_in,
    proj_in_bias,
    proj_out,
    proj_out_bias,
    targets,
):
    images, height, across, channels = features.shape
    width, align = embed_weight.shape[1], proj_out.shape[1]
    peers = lax.axis_size("rows")
    members = peers * height * across * (channels // GROUPS)
    flat = features.reshape(images, height * across, channels)
    gain, bias = norm_gain.reshape(1, channels), norm_bias.reshape(1, channels)
    depth = proj_in.shape[0]
    shard = jnp.concatenate(
        [proj_in] + [proj_out[at : at + depth] for at in range(0, proj_out.shape[0], depth)], axis=1
    )
    mine, far = crossed(shard)
    own = sheet(mine)
    taps = conv_weight.reshape(LATENT, TAPS, channels).transpose(1, 0, 2)
    taps = jnp.pad(taps, ((0, 0), (0, SUB - LATENT), (0, 0))).reshape(TAPS * SUB, channels)
    taps_full = jnp.pad(taps, ((0, LANES - TAPS * SUB), (0, 0)))
    spread = jnp.pad(
        embed_weight.reshape(PATCH * PATCH, LATENT, width), ((0, 0), (0, SUB - LATENT), (0, 0))
    ).reshape(PATCH * PATCH * SUB, width)

    sums = group_stats(flat, peers)
    far, _ = lax.optimization_barrier((far, sums))
    cross = sheet(far)
    stats = lax.all_to_all(sums, "rows", 0, 0, tiled=True)
    lat, up, down, mean, inv = conv_forward(stats, flat, gain, bias, taps, across, members)
    above, below = neighbours(up, down)
    own, cross, lat = lax.optimization_barrier((own, cross, lat))
    pieces = [own, cross, swapped(own), swapped(cross)]
    rows, batch = lax.axis_index("rows"), lax.axis_index("batch")
    at = jnp.stack([(rows // CORES) % ZHI, rows % CORES, batch % YS, batch // YS])
    at = at.astype(jnp.int32)
    target = targets.reshape(-1, align)
    embed_part, grad_lat = projector(
        at, lat, below, above, target, spread, embed_bias.reshape(1, -1),
        proj_in_bias.reshape(1, -1), proj_out_bias.reshape(1, -1), pieces, across,
    )
    after, before = neighbours(grad_lat, grad_lat)
    send, grad_shift = conv_backward(
        grad_lat, before, after, flat, mean, inv, gain, bias, taps_full, embed_part, across
    )
    plane = exchanged(send, PLANE)
    column = exchanged(plane_total(at, plane), COLUMN)
    chunks, got = column_total(at, column)
    everything = exchanged(chunks, PLANE)
    grad_features = feature_grad(got, flat, mean, inv, gain, grad_shift, members)
    grad_conv, grad_gain, grad_bias, grad_embed = unpack(everything, channels, width)
    return (
        grad_features.reshape(features.shape),
        grad_conv,
        grad_gain.reshape(channels),
        grad_bias.reshape(channels),
        grad_embed,
    )


def solution(mesh):
    in_specs = (
        P("batch", "rows", None, None),
        P(),
        P(),
        P(),
        P(),
        P(),
        P("rows", None),
        P(),
        P("rows", None),
        P(),
        P("batch", "rows", None, None),
    )
    out_specs = (P("batch", "rows", None, None), P(), P(), P(), P())
    return jax.shard_map(shards, mesh=mesh, in_specs=in_specs, out_specs=out_specs, check_vma=False)
```

```python
import jax
import jax.numpy as jnp
from jax import lax
from jax.experimental import pallas as pl
from jax.experimental.pallas import tpu as pltpu
from jax.sharding import PartitionSpec as P

GROUPS = 32
LATENT = 4
PATCH = 2
EPS_NORM = 1e-06
EPS_UNIT = 1e-06

XS, ZHI, CORES, ZLO, YS = 4, 2, 2, 8, 4

HIGH = lax.Precision.HIGHEST
F32 = jnp.float32
BF16 = jnp.bfloat16
TAPS = 9
SUB = 8
LANES = 128
STAT_ROWS = 16
CHUNKS, CHUNK_ROWS, ALL_ROWS = 32, 16, 32
CONV_COST = 20_000_000_000
PART = 16


def params(limit_mb=48):
    return pltpu.CompilerParams(vmem_limit_bytes=limit_mb << 20)


def vmem():
    return pl.BlockSpec(memory_space=pltpu.VMEM)


def sigmoid(v):
    return 0.5 + 0.5 * jnp.tanh(0.5 * v)


def nt(a, b, precision=None):
    return lax.dot_general(
        a, b, (((1,), (1,)), ((), ())), preferred_element_type=F32, precision=precision
    )


def nn(a, b, precision=None):
    return lax.dot_general(
        a, b, (((1,), (0,)), ((), ())), preferred_element_type=F32, precision=precision
    )


def iota(shape, dim):
    return lax.broadcasted_iota(jnp.int32, shape, dim)


def to_groups(channels, per_group, offset):
    shape = (channels, LANES)
    return (iota(shape, 0) // per_group + offset == iota(shape, 1)).astype(F32)


def from_groups(channels, per_group, offset):
    shape = (LANES, channels)
    return (iota(shape, 1) // per_group + offset == iota(shape, 0)).astype(F32)


def pack_stats(total):
    lane = iota((SUB, LANES), 1)
    return jnp.where(lane < LANES // 2, total[:SUB], pltpu.roll(total[SUB:], LANES // 2, 1))


def unpack_stats(packed):
    return jnp.concatenate([packed, pltpu.roll(packed, LANES // 2, 1)], axis=0)


def parts(v):
    top = v.astype(BF16)
    return top, (v - top.astype(F32)).astype(BF16)


def halves(packed):
    top = packed.astype(BF16).astype(F32)
    return jnp.concatenate([top, packed - top], axis=0).astype(BF16)


def stats_kernel(f_ref, out_ref, sums, squares):
    images, _, channels = f_ref.shape
    sums[...] = jnp.zeros_like(sums)
    squares[...] = jnp.zeros_like(squares)
    for i in range(images):
        v = f_ref[i].astype(F32)
        sums[i : i + 1, :] = jnp.sum(v, axis=0, keepdims=True)
        squares[i : i + 1, :] = jnp.sum(v * v, axis=0, keepdims=True)
    per_group = channels // GROUPS
    total = nn(sums[...], to_groups(channels, per_group, 0), HIGH) + nn(
        squares[...], to_groups(channels, per_group, GROUPS), HIGH
    )
    packed = pack_stats(total)
    for r in range(out_ref.shape[0]):
        out_ref[r] = packed


def group_stats(features, peers):
    channels = features.shape[-1]
    return pl.pallas_call(
        stats_kernel,
        out_shape=jax.ShapeDtypeStruct((peers, SUB, LANES), F32),
        in_specs=[vmem()],
        out_specs=vmem(),
        scratch_shapes=[pltpu.VMEM((STAT_ROWS, channels), F32)] * 2,
        compiler_params=params(),
        name="stats",
    )(features)


def lane_masks(shape, across):
    lane = iota(shape, 1)
    return lane % across, (lane // across) % 2


def roll(v, shift):
    return pltpu.roll(v, shift % v.shape[1], 1)


def conv_kernel(
    across, members, st_ref, f_ref, gain_ref, bias_ref, k_ref,
    lat_ref, up_ref, down_ref, mean_ref, inv_ref, act,
):
    images, cells, channels = f_ref.shape
    per_group = channels // GROUPS
    total = unpack_stats(jnp.sum(st_ref[...], axis=0))
    mean = nn(total, from_groups(channels, per_group, 0), HIGH) * (1.0 / members)
    square = nn(total, from_groups(channels, per_group, GROUPS), HIGH) * (1.0 / members)
    inv = lax.rsqrt(jnp.maximum(square - mean * mean, 0.0) + EPS_NORM)
    mean_ref[...] = mean
    inv_ref[...] = inv
    gain, bias = gain_ref[...], bias_ref[...]
    for i in range(images):
        v = f_ref[i].astype(F32)
        shifted = (v - mean[i : i + 1]) * inv[i : i + 1] * gain + bias
        act[i * cells : (i + 1) * cells, :] = (shifted * sigmoid(shifted)).astype(BF16)
    taps = nt(k_ref[...], act[...])
    shape = (SUB, images * cells)
    col, row = lane_masks(shape, across)

    def tap(position):
        return taps[position * SUB : (position + 1) * SUB]

    def line(dy):
        low = jnp.where(col > 0, roll(tap(3 * dy), 1), 0.0)
        high = jnp.where(col < across - 1, roll(tap(3 * dy + 2), -1), 0.0)
        return tap(3 * dy + 1) + low + high

    first, middle, last = line(0), line(1), line(2)
    last_up, first_down = roll(last, -across), roll(first, across)
    lat_ref[...] = middle + jnp.where(row == 0, last_up, first_down)
    up_ref[...] = jnp.where(row == 1, roll(last, across), 0.0)
    down_ref[...] = jnp.where(row == 0, roll(first, -across), 0.0)


def conv_forward(stats, features, gain, bias, kernel_rows, across, members):
    images, cells, channels = features.shape
    line = jax.ShapeDtypeStruct((SUB, images * cells), F32)
    stat = jax.ShapeDtypeStruct((STAT_ROWS, channels), F32)
    return pl.pallas_call(
        lambda *refs: conv_kernel(across, members, *refs),
        out_shape=(line, line, line, stat, stat),
        in_specs=[vmem()] * 5,
        out_specs=(vmem(),) * 5,
        scratch_shapes=[pltpu.VMEM((images * cells, channels), BF16)],
        compiler_params=params(),
        cost_estimate=pl.CostEstimate(
            flops=CONV_COST, bytes_accessed=features.size * 2, transcendentals=features.size
        ),
        name="conv",
    )(stats, features, gain, bias, kernel_rows)


def mlp_kernel(
    across, width, hidden, align, at_ref, lat_ref, below_ref, above_ref, target_ref,
    ew_ref, eb_ref, pib_ref, pob_ref,
    own_near, own_far, cross_near, cross_far, own_near_other, own_far_other,
    cross_near_other, cross_far_other,
    embed_ref, gl_ref, w_in, w_out, pre, emb, acc, grad_emb, sems,
):
    zhi, core, x = at_ref[0], at_ref[1], at_ref[4]
    depth = width // (XS * ZHI * CORES)
    slab = hidden // (XS * ZHI * CORES)
    rows = ew_ref.shape[0]
    copies = []
    own, own_other = (own_near, own_far), (own_near_other, own_far_other)
    cross, cross_other = (cross_near, cross_far), (cross_near_other, cross_far_other)

    def place(piece, at, source_x, of_zhi, of_core, half=0, count=1):
        shard = lax.rem(source_x, XS) * (ZHI * CORES) + of_zhi * CORES + of_core
        size = depth // count
        lines = pl.ds(at, size)

        def put(columns, into):
            copy = pltpu.make_async_copy(piece.at[lines, columns], into, sems.at[len(copies)])
            copy.start()
            copies.append(copy)

        begin = pl.multiple_of(shard * depth + half * size, size)
        put(pl.ds(0, hidden), w_in.at[pl.ds(begin, size), :])
        for part in range(slab // depth):
            begin = pl.multiple_of(shard * slab + part * depth + half * size, size)
            put(pl.ds(hidden + part * align, align), w_out.at[pl.ds(begin, size), :])

    for of_zhi, by_core in (
        (zhi, ((core, own), (1 - core, own_other))),
        (1 - zhi, ((core, cross), (1 - core, cross_other))),
    ):
        for of_core, (near, opposite) in by_core:
            for k, step in enumerate((0, 1, XS - 1)):
                place(near, k * depth, x + step, of_zhi, of_core)
            for half in range(2):
                place(opposite, half * depth // 2, x + 2, of_zhi, of_core, half, 2)

    lat = lat_ref[...] + below_ref[...] + above_ref[...]
    top = lat.astype(BF16)
    rest = lat - top.astype(F32)
    mid = rest.astype(BF16)
    low_part = (rest - mid.astype(F32)).astype(BF16)
    split = jnp.concatenate(
        [top.astype(F32), mid.astype(F32), low_part.astype(F32)], axis=0
    ).astype(BF16)
    cells = lat.shape[1]
    tokens = target_ref.shape[0]
    room = 256
    cols = across // PATCH

    def selection(u, v):
        shape = (cells, room)
        token = iota(shape, 1)
        lane = (token // cols) * (PATCH * across) + u * across + (token % cols) * PATCH + v
        return jnp.where((lane == iota(shape, 0)) & (token < tokens), 1.0, 0.0).astype(BF16)

    picks = [selection(u, v) for u in range(PATCH) for v in range(PATCH)]
    lines = []
    for pick in picks:
        got = nn(split, pick)
        lines.append(got[0:SUB] + got[SUB : 2 * SUB] + got[2 * SUB :])
    patches_t = jnp.concatenate(lines, axis=0)
    patches = patches_t.T
    ew_top, ew_low = parts(ew_ref[...])
    p_top, p_low = parts(patches[:tokens])
    embedded = nn(p_top, ew_top) + nn(p_low, ew_top) + nn(p_top, ew_low)
    emb[...] = (embedded + eb_ref[...]).astype(BF16)

    for copy in copies:
        copy.wait()

    step = 512
    acc[...] = jnp.zeros_like(acc)

    @pl.loop(0, hidden // step)
    def _(tile):
        at = pl.ds(pl.multiple_of(tile * step, step), step)
        h = nn(emb[...], w_in[:, at]) + pib_ref[:, at]
        pre[:, at] = h
        acc[...] += nn((h * sigmoid(h)).astype(BF16), w_out[at, :])

    projected = acc[...] + pob_ref[...]
    target = target_ref[...].astype(F32)
    unit_target = target * lax.rsqrt(jnp.sum(target * target, axis=1, keepdims=True) + EPS_UNIT)
    inv_len = lax.rsqrt(jnp.sum(projected * projected, axis=1, keepdims=True) + EPS_UNIT)
    unit_proj = projected * inv_len
    cosine = jnp.sum(unit_proj * unit_target, axis=1, keepdims=True)
    grad_out = (-inv_len * (unit_target - cosine * unit_proj)).astype(BF16)
    grad_emb[...] = jnp.zeros_like(grad_emb)

    @pl.loop(0, hidden // step)
    def _(tile):
        at = pl.ds(pl.multiple_of(tile * step, step), step)
        back = nt(grad_out, w_out[at, :])
        h = pre[:, at]
        sig = sigmoid(h)
        grad_hidden = (back * (sig * (1.0 + h * (1.0 - sig)))).astype(BF16)
        grad_emb[0:tokens, :] += nt(grad_hidden, w_in[:, at])

    grad = grad_emb[...]
    g_top, g_low = parts(grad)
    t_top, t_low = parts(patches_t)
    both = nn(jnp.concatenate([t_top, t_low], axis=0), g_top)
    embed_ref[...] = both[:rows] + both[rows:] + nn(t_top, g_low)
    both = nt(jnp.concatenate([ew_top, ew_low], axis=0), g_top)
    grad_patch = both[:rows] + both[rows:] + nt(ew_top, g_low)
    total = jnp.zeros((SUB, cells), F32)
    for position, pick in enumerate(picks):
        part = grad_patch[position * SUB : (position + 1) * SUB].astype(BF16)
        total = total + nt(part, pick)
    gl_ref[...] = total


def projector(at, lat, below, above, target, ew, eb, pib, pob, pieces, across):
    rows, width = ew.shape
    hidden, align = pib.shape[1], pob.shape[1]
    tokens = target.shape[0]
    flops = 2 * tokens * (2 * width * hidden + 2 * hidden * align)
    return pl.pallas_call(
        lambda *refs: mlp_kernel(across, width, hidden, align, *refs),
        out_shape=(
            jax.ShapeDtypeStruct((rows, width), F32),
            jax.ShapeDtypeStruct(lat.shape, F32),
        ),
        in_specs=[pl.BlockSpec(memory_space=pltpu.SMEM)]
        + [vmem()] * 8
        + [pl.BlockSpec(memory_space=pltpu.HBM)] * len(pieces),
        out_specs=(vmem(), vmem()),
        scratch_shapes=[
            pltpu.VMEM((width, hidden), BF16),
            pltpu.VMEM((hidden, align), BF16),
            pltpu.VMEM((tokens, hidden), F32),
            pltpu.VMEM((tokens, width), BF16),
            pltpu.VMEM((tokens, align), F32),
            pltpu.VMEM((256, width), F32),
            pltpu.SemaphoreType.DMA((60,)),
        ],
        compiler_params=params(),
        cost_estimate=pl.CostEstimate(
            flops=flops, bytes_accessed=8 << 20, transcendentals=2 * tokens * hidden
        ),
        name="projector",
    )(at, lat, below, above, target, ew, eb, pib, pob, *pieces)


def back_kernel(
    across, gl_ref, before_ref, after_ref, f_ref, mean_ref, inv_ref, gain_ref, bias_ref,
    k_ref, embed_ref, send_ref, gs_ref, act, grads_t, by_bias, by_gain, pack,
):
    images, cells, channels = f_ref.shape
    per_group = channels // GROUPS
    gl, before, after = gl_ref[...], before_ref[...], after_ref[...]
    col, row = lane_masks(gl.shape, across)
    lines = (
        jnp.where(row == 0, roll(gl, -across), roll(after, across)),
        gl,
        jnp.where(row == 0, roll(before, -across), roll(gl, across)),
    )
    parts = []
    for g in lines:
        parts.append(jnp.where(col < across - 1, roll(g, -1), 0.0))
        parts.append(g)
        parts.append(jnp.where(col > 0, roll(g, 1), 0.0))
    parts.append(jnp.zeros((LANES - TAPS * SUB, gl.shape[1]), F32))
    grads = jnp.concatenate(parts, axis=0)
    grads_t[...] = grads.T.astype(BF16)
    gain, bias = gain_ref[...], bias_ref[...]
    by_bias[...] = jnp.zeros_like(by_bias)
    by_gain[...] = jnp.zeros_like(by_gain)
    for i in range(images):
        at = slice(i * cells, (i + 1) * cells)
        v = f_ref[i].astype(F32)
        normed = (v - mean_ref[i : i + 1, :]) * inv_ref[i : i + 1, :]
        shifted = normed * gain + bias
        sig = sigmoid(shifted)
        act[at, :] = (shifted * sig).astype(BF16)
        grad_active = nn(grads_t[at, :], k_ref[...])
        gs = grad_active * (sig * (1.0 + shifted * (1.0 - sig)))
        gs_ref[i] = gs
        by_bias[i : i + 1, :] = jnp.sum(gs, axis=0, keepdims=True)
        by_gain[i : i + 1, :] = jnp.sum(gs * normed, axis=0, keepdims=True)
    conv = nn(grads.astype(BF16), act[...])
    stat = nn(by_bias[...] * gain, to_groups(channels, per_group, 0), HIGH) + nn(
        by_gain[...] * gain, to_groups(channels, per_group, GROUPS), HIGH
    )
    bias_part = jnp.sum(by_bias[...], axis=0, keepdims=True)
    gain_part = jnp.sum(by_gain[...], axis=0, keepdims=True)
    packed = halves(pack_stats(stat))
    for r in range(CHUNKS):
        send_ref[r, CHUNK_ROWS:ALL_ROWS, :] = packed
    blocks = channels // LANES
    half = CHUNKS // 2
    pack[...] = jnp.zeros_like(pack)
    for r in range(half):
        block, latent = r // LATENT, r % LATENT
        lanes = slice(block * LANES, (block + 1) * LANES)
        for position in range(TAPS):
            line = position * SUB + latent
            pack[r, position : position + 1, :] = conv[line : line + 1, lanes]
        lanes = slice((r // 2) * LANES, (r // 2 + 1) * LANES)
        for part in range(2):
            line = (r % 2) * 2 * SUB + part * SUB
            pack[half + r, part * LATENT : (part + 1) * LATENT, :] = embed_ref[
                line : line + LATENT, lanes
            ]
        if r < 2 * blocks:
            one = gain_part if r < blocks else bias_part
            lanes = slice((r % blocks) * LANES, (r % blocks + 1) * LANES)
            pack[half + r, SUB : SUB + 1, :] = one[:, lanes]
    for r in range(CHUNKS):
        send_ref[r, 0:CHUNK_ROWS, :] = pack[r].astype(BF16)


def conv_backward(gl, before, after, features, mean, inv, gain, bias, kernel_rows, embed, across):
    images, cells, channels = features.shape
    return pl.pallas_call(
        lambda *refs: back_kernel(across, *refs),
        out_shape=(
            jax.ShapeDtypeStruct((CHUNKS, ALL_ROWS, LANES), BF16),
            jax.ShapeDtypeStruct((images, cells, channels), F32),
        ),
        in_specs=[vmem()] * 10,
        out_specs=(vmem(),) * 2,
        scratch_shapes=[
            pltpu.VMEM((images * cells, channels), BF16),
            pltpu.VMEM((images * cells, LANES), BF16),
            pltpu.VMEM((STAT_ROWS, channels), F32),
            pltpu.VMEM((STAT_ROWS, channels), F32),
            pltpu.VMEM((CHUNKS, CHUNK_ROWS, LANES), F32),
        ],
        compiler_params=params(),
        name="back",
    )(gl, before, after, features, mean, inv, gain, bias, kernel_rows, embed)


def last_kernel(members, got_ref, f_ref, mean_ref, inv_ref, gain_ref, gs_ref, out_ref):
    images, _, channels = f_ref.shape
    per_group = channels // GROUPS
    total = unpack_stats(got_ref[...])
    first = nn(total, from_groups(channels, per_group, 0), HIGH) * (1.0 / members)
    second = nn(total, from_groups(channels, per_group, GROUPS), HIGH) * (1.0 / members)
    gain = gain_ref[...]
    for i in range(images):
        v = f_ref[i].astype(F32)
        inv = inv_ref[i : i + 1, :]
        normed = (v - mean_ref[i : i + 1, :]) * inv
        out = inv * (gs_ref[i] * gain - first[i : i + 1] - normed * second[i : i + 1])
        out_ref[i] = out.astype(BF16)


def feature_grad(got, features, mean, inv, gain, grad_shift, members):
    return pl.pallas_call(
        lambda *refs: last_kernel(members, *refs),
        out_shape=jax.ShapeDtypeStruct(features.shape, BF16),
        in_specs=[vmem()] * 6,
        out_specs=vmem(),
        compiler_params=params(),
        cost_estimate=pl.CostEstimate(
            flops=10 * features.size, bytes_accessed=8 * features.size, transcendentals=0
        ),
        name="last",
    )(got, features, mean, inv, gain, grad_shift)


def plane_kernel(at_ref, got_ref, out_ref):
    chunk = jnp.zeros((CHUNK_ROWS, LANES), F32)
    stat = jnp.zeros((SUB, LANES), F32)
    for r in range(CHUNKS):
        chunk = chunk + got_ref[r, 0:CHUNK_ROWS, :].astype(F32)
        pair = got_ref[r, CHUNK_ROWS:ALL_ROWS, :].astype(F32)
        stat = stat + jnp.where(at_ref[2] == (r // CORES) % YS, pair[:SUB] + pair[SUB:], 0.0)
    chunk, stat = chunk.astype(BF16), halves(stat)
    for r in range(out_ref.shape[0]):
        out_ref[r, 0:CHUNK_ROWS, :] = chunk
        out_ref[r, CHUNK_ROWS:ALL_ROWS, :] = stat


def plane_total(at, got):
    return pl.pallas_call(
        plane_kernel,
        out_shape=jax.ShapeDtypeStruct((ZHI * ZLO, ALL_ROWS, LANES), BF16),
        in_specs=[pl.BlockSpec(memory_space=pltpu.SMEM), vmem()],
        out_specs=vmem(),
        compiler_params=params(),
        name="plane",
    )(at, got)


def column_kernel(at_ref, got_ref, out_ref, stat_ref):
    chunk = jnp.zeros((CHUNK_ROWS, LANES), F32)
    stat = jnp.zeros((SUB, LANES), F32)
    for r in range(ZHI * ZLO):
        chunk = chunk + got_ref[r, 0:CHUNK_ROWS, :].astype(F32)
        pair = got_ref[r, CHUNK_ROWS:ALL_ROWS, :].astype(F32)
        stat = stat + jnp.where(at_ref[3] == r % ZLO, pair[:SUB] + pair[SUB:], 0.0)
    chunk = chunk.astype(BF16)
    for r in range(out_ref.shape[0]):
        out_ref[r] = chunk
    stat_ref[...] = stat


def column_total(at, got):
    return pl.pallas_call(
        column_kernel,
        out_shape=(
            jax.ShapeDtypeStruct((CHUNKS, CHUNK_ROWS, LANES), BF16),
            jax.ShapeDtypeStruct((SUB, LANES), F32),
        ),
        in_specs=[pl.BlockSpec(memory_space=pltpu.SMEM), vmem()],
        out_specs=(vmem(), vmem()),
        compiler_params=params(),
        name="column",
    )(at, got)


def unpack_kernel(got_ref, conv_ref, gain_ref, bias_ref, embed_ref, wide):
    channels = gain_ref.shape[1]
    blocks = channels // LANES
    half = CHUNKS // 2
    wide[...] = got_ref[...].astype(F32)
    for r in range(half):
        block, latent = r // LATENT, r % LATENT
        for position in range(TAPS):
            at = position * channels + block * LANES
            conv_ref[latent : latent + 1, at : at + LANES] = wide[r, position : position + 1, :]
        lanes = slice((r // 2) * LANES, (r // 2 + 1) * LANES)
        line = (r % 2) * SUB
        embed_ref[line : line + SUB, lanes] = wide[half + r, 0:SUB, :]
        lanes = slice((r % blocks) * LANES, (r % blocks + 1) * LANES)
        if r < blocks:
            gain_ref[:, lanes] = wide[half + r, SUB : SUB + 1, :]
        elif r < 2 * blocks:
            bias_ref[:, lanes] = wide[half + r, SUB : SUB + 1, :]


def unpack(got, channels, width):
    return pl.pallas_call(
        unpack_kernel,
        out_shape=(
            jax.ShapeDtypeStruct((LATENT, TAPS * channels), F32),
            jax.ShapeDtypeStruct((1, channels), F32),
            jax.ShapeDtypeStruct((1, channels), F32),
            jax.ShapeDtypeStruct((PATCH * PATCH * LATENT, width), F32),
        ),
        in_specs=[vmem()],
        out_specs=(vmem(),) * 4,
        scratch_shapes=[pltpu.VMEM(got.shape, F32)],
        compiler_params=params(),
        name="unpack",
    )(got)


def device(x, zhi, core, zlo, y):
    return ((x * ZHI + zhi) * CORES + core) * (ZLO * YS) + zlo * YS + y


BOTH = ("rows", "batch")
PLANE = [
    [device(x, h, c, d, y) for x in range(XS) for y in range(YS) for c in range(CORES)]
    for h in range(ZHI)
    for d in range(ZLO)
]
COLUMN = [
    [device(x, h, c, d, y) for h in range(ZHI) for d in range(ZLO)]
    for x in range(XS)
    for y in range(YS)
    for c in range(CORES)
]


def exchanged(value, groups):
    return lax.all_to_all(value, BOTH, 0, 0, axis_index_groups=groups, tiled=True)


def moved(value, where):
    pairs = []
    for x in range(XS):
        for zhi in range(ZHI):
            for core in range(CORES):
                for zlo in range(ZLO):
                    for y in range(YS):
                        a, b, c, d, e = where(x, zhi, core, zlo, y)
                        pairs.append((device(x, zhi, core, zlo, y), device(a, b, c, d, e)))
    return lax.ppermute(value, ("rows", "batch"), pairs)


def crossed(shard):
    y = lax.axis_index("batch") % YS
    mine = lax.dynamic_slice_in_dim(shard, y * PART, PART, axis=0)
    return moved(mine, lambda x, h, c, d, y: (x, 1 - h, c, ZLO - 1 - d, y))


def along_y(part):
    y = lax.axis_index("batch") % YS
    other = moved(part, lambda x, h, c, d, y: (x, h, c, d, y ^ 1))
    even = y % 2 == 0
    pair = jnp.concatenate([jnp.where(even, part, other), jnp.where(even, other, part)], axis=0)
    far = moved(pair, lambda x, h, c, d, y: (x, h, c, d, YS - 1 - y))
    low = y < 2
    return jnp.concatenate([jnp.where(low, pair, far), jnp.where(low, far, pair)], axis=0)


def from_next(value):
    return moved(value, lambda x, h, c, d, y: ((x + XS - 1) % XS, h, c, d, y))


def from_last(value):
    return moved(value, lambda x, h, c, d, y: ((x + 1) % XS, h, c, d, y))


def along_x(shard):
    half = shard.shape[0] // 2
    plus, minus = from_next(shard), from_last(shard)
    near = jnp.concatenate([shard, plus, minus], axis=0)
    opposite = jnp.concatenate([from_next(plus[:half]), from_last(minus[half:])], axis=0)
    return near, opposite


def swapped(value):
    return moved(value, lambda x, h, c, d, y: (x, h, 1 - c, d, y))


def neighbours(up, down):
    count = lax.axis_size("rows")
    forward = [(i, i + 1) for i in range(count - 1)]
    backward = [(b, a) for a, b in forward]
    return lax.ppermute(up, "rows", backward), lax.ppermute(down, "rows", forward)


def shards(
    features,
    norm_gain,
    norm_bias,
    conv_weight,
    embed_weight,
    embed_bias,
    proj_in,
    proj_in_bias,
    proj_out,
    proj_out_bias,
    targets,
):
    images, height, across, channels = features.shape
    width, align = embed_weight.shape[1], proj_out.shape[1]
    peers = lax.axis_size("rows")
    members = peers * height * across * (channels // GROUPS)
    flat = features.reshape(images, height * across, channels)
    gain, bias = norm_gain.reshape(1, channels), norm_bias.reshape(1, channels)
    depth = proj_in.shape[0]
    shard = jnp.concatenate(
        [proj_in] + [proj_out[at : at + depth] for at in range(0, proj_out.shape[0], depth)], axis=1
    )
    far = crossed(shard)
    own_near, own_far = along_x(shard)
    taps = conv_weight.reshape(LATENT, TAPS, channels).transpose(1, 0, 2)
    taps = jnp.pad(taps, ((0, 0), (0, SUB - LATENT), (0, 0))).reshape(TAPS * SUB, channels)
    taps_full = jnp.pad(taps, ((0, LANES - TAPS * SUB), (0, 0)))
    spread = jnp.pad(
        embed_weight.reshape(PATCH * PATCH, LATENT, width), ((0, 0), (0, SUB - LATENT), (0, 0))
    ).reshape(PATCH * PATCH * SUB, width)

    sums = group_stats(flat, peers)
    stats = lax.all_to_all(sums, "rows", 0, 0, tiled=True)
    cross = along_y(far)
    cross_near, cross_far = along_x(cross)
    lat, up, down, mean, inv = conv_forward(stats, flat, gain, bias, taps, across, members)
    above, below = neighbours(up, down)
    own_near, own_far, above, below = lax.optimization_barrier((own_near, own_far, above, below))
    pieces = [own_near, own_far, cross_near, cross_far]
    pieces = pieces + [swapped(v) for v in pieces]
    rows, batch = lax.axis_index("rows"), lax.axis_index("batch")
    at = jnp.stack([(rows // CORES) % ZHI, rows % CORES, batch % YS, batch // YS, rows // (ZHI * CORES)])
    at = at.astype(jnp.int32)
    target = targets.reshape(-1, align)
    embed_part, grad_lat = projector(
        at, lat, below, above, target, spread, embed_bias.reshape(1, -1),
        proj_in_bias.reshape(1, -1), proj_out_bias.reshape(1, -1), pieces, across,
    )
    after, before = neighbours(grad_lat, grad_lat)
    send, grad_shift = conv_backward(
        grad_lat, before, after, flat, mean, inv, gain, bias, taps_full, embed_part, across
    )
    plane = exchanged(send, PLANE)
    column = exchanged(plane_total(at, plane), COLUMN)
    chunks, got = column_total(at, column)
    everything = exchanged(chunks, PLANE)
    grad_features = feature_grad(got, flat, mean, inv, gain, grad_shift, members)
    grad_conv, grad_gain, grad_bias, grad_embed = unpack(everything, channels, width)
    return (
        grad_features.reshape(features.shape),
        grad_conv,
        grad_gain.reshape(channels),
        grad_bias.reshape(channels),
        grad_embed,
    )


def solution(mesh):
    in_specs = (
        P("batch", "rows", None, None),
        P(),
        P(),
        P(),
        P(),
        P(),
        P("rows", None),
        P(),
        P("rows", None),
        P(),
        P("batch", "rows", None, None),
    )
    out_specs = (P("batch", "rows", None, None), P(), P(), P(), P())
    return jax.shard_map(shards, mesh=mesh, in_specs=in_specs, out_specs=out_specs, check_vma=False)
```

```python
import jax
import jax.numpy as jnp
from jax import lax
from jax.experimental import pallas as pl
from jax.experimental.pallas import tpu as pltpu
from jax.sharding import PartitionSpec as P

GROUPS = 32
LATENT = 4
PATCH = 2
EPS_NORM = 1e-06
EPS_UNIT = 1e-06

XS, ZHI, CORES, ZLO, YS = 4, 2, 2, 8, 4

HIGH = lax.Precision.HIGHEST
F32 = jnp.float32
BF16 = jnp.bfloat16
TAPS = 9
SUB = 8
LANES = 128
STAT_ROWS = 16
CHUNKS, CHUNK_ROWS, ALL_ROWS = 32, 16, 32
CONV_COST = 20_000_000_000
PART = 16


def params(limit_mb=12):
    return pltpu.CompilerParams(vmem_limit_bytes=limit_mb << 20)


def vmem():
    return pl.BlockSpec(memory_space=pltpu.VMEM)


def sigmoid(v):
    return 0.5 + 0.5 * jnp.tanh(0.5 * v)


def nt(a, b, precision=None):
    return lax.dot_general(
        a, b, (((1,), (1,)), ((), ())), preferred_element_type=F32, precision=precision
    )


def nn(a, b, precision=None):
    return lax.dot_general(
        a, b, (((1,), (0,)), ((), ())), preferred_element_type=F32, precision=precision
    )


def iota(shape, dim):
    return lax.broadcasted_iota(jnp.int32, shape, dim)


def to_groups(channels, per_group, offset):
    shape = (channels, LANES)
    return (iota(shape, 0) // per_group + offset == iota(shape, 1)).astype(F32)


def from_groups(channels, per_group, offset):
    shape = (LANES, channels)
    return (iota(shape, 1) // per_group + offset == iota(shape, 0)).astype(F32)


def pack_stats(total):
    lane = iota((SUB, LANES), 1)
    return jnp.where(lane < LANES // 2, total[:SUB], pltpu.roll(total[SUB:], LANES // 2, 1))


def unpack_stats(packed):
    return jnp.concatenate([packed, pltpu.roll(packed, LANES // 2, 1)], axis=0)


def parts(v):
    top = v.astype(BF16)
    return top, (v - top.astype(F32)).astype(BF16)


def halves(packed):
    top = packed.astype(BF16).astype(F32)
    return jnp.concatenate([top, packed - top], axis=0).astype(BF16)


def stats_kernel(f_ref, out_ref, sums, squares):
    images, _, channels = f_ref.shape
    sums[...] = jnp.zeros_like(sums)
    squares[...] = jnp.zeros_like(squares)
    for i in range(images):
        v = f_ref[i].astype(F32)
        sums[i : i + 1, :] = jnp.sum(v, axis=0, keepdims=True)
        squares[i : i + 1, :] = jnp.sum(v * v, axis=0, keepdims=True)
    per_group = channels // GROUPS
    total = nn(sums[...], to_groups(channels, per_group, 0), HIGH) + nn(
        squares[...], to_groups(channels, per_group, GROUPS), HIGH
    )
    packed = pack_stats(total)
    for r in range(out_ref.shape[0]):
        out_ref[r] = packed


def group_stats(features, peers):
    channels = features.shape[-1]
    return pl.pallas_call(
        stats_kernel,
        out_shape=jax.ShapeDtypeStruct((peers, SUB, LANES), F32),
        in_specs=[vmem()],
        out_specs=vmem(),
        scratch_shapes=[pltpu.VMEM((STAT_ROWS, channels), F32)] * 2,
        compiler_params=params(),
        name="stats",
    )(features)


def lane_masks(shape, across):
    lane = iota(shape, 1)
    return lane % across, (lane // across) % 2


def roll(v, shift):
    return pltpu.roll(v, shift % v.shape[1], 1)


def conv_kernel(
    across, members, st_ref, f_ref, gain_ref, bias_ref, k_ref,
    lat_ref, up_ref, down_ref, mean_ref, inv_ref, act,
):
    images, cells, channels = f_ref.shape
    per_group = channels // GROUPS
    total = unpack_stats(jnp.sum(st_ref[...], axis=0))
    mean = nn(total, from_groups(channels, per_group, 0), HIGH) * (1.0 / members)
    square = nn(total, from_groups(channels, per_group, GROUPS), HIGH) * (1.0 / members)
    inv = lax.rsqrt(jnp.maximum(square - mean * mean, 0.0) + EPS_NORM)
    mean_ref[...] = mean
    inv_ref[...] = inv
    gain, bias = gain_ref[...], bias_ref[...]
    for i in range(images):
        v = f_ref[i].astype(F32)
        shifted = (v - mean[i : i + 1]) * inv[i : i + 1] * gain + bias
        act[i * cells : (i + 1) * cells, :] = (shifted * sigmoid(shifted)).astype(BF16)
    taps = nt(k_ref[...], act[...])
    shape = (SUB, images * cells)
    col, row = lane_masks(shape, across)

    def tap(position):
        return taps[position * SUB : (position + 1) * SUB]

    def line(dy):
        low = jnp.where(col > 0, roll(tap(3 * dy), 1), 0.0)
        high = jnp.where(col < across - 1, roll(tap(3 * dy + 2), -1), 0.0)
        return tap(3 * dy + 1) + low + high

    first, middle, last = line(0), line(1), line(2)
    last_up, first_down = roll(last, -across), roll(first, across)
    lat_ref[...] = middle + jnp.where(row == 0, last_up, first_down)
    up_ref[...] = jnp.where(row == 1, roll(last, across), 0.0)
    down_ref[...] = jnp.where(row == 0, roll(first, -across), 0.0)


def conv_forward(stats, features, gain, bias, kernel_rows, across, members):
    images, cells, channels = features.shape
    line = jax.ShapeDtypeStruct((SUB, images * cells), F32)
    stat = jax.ShapeDtypeStruct((STAT_ROWS, channels), F32)
    return pl.pallas_call(
        lambda *refs: conv_kernel(across, members, *refs),
        out_shape=(line, line, line, stat, stat),
        in_specs=[vmem()] * 5,
        out_specs=(vmem(),) * 5,
        scratch_shapes=[pltpu.VMEM((images * cells, channels), BF16)],
        compiler_params=params(),
        cost_estimate=pl.CostEstimate(
            flops=CONV_COST, bytes_accessed=features.size * 2, transcendentals=features.size
        ),
        name="conv",
    )(stats, features, gain, bias, kernel_rows)


def mlp_kernel(
    across, width, hidden, align, at_ref, lat_ref, below_ref, above_ref, target_ref,
    ew_ref, eb_ref, pib_ref, pob_ref,
    own_near, own_far, cross_near, cross_far, own_near_other, own_far_other,
    cross_near_other, cross_far_other,
    embed_ref, gl_ref, w_in, w_out, pre, emb, acc, grad_emb, sems,
):
    zhi, core, x = at_ref[0], at_ref[1], at_ref[4]
    depth = width // (XS * ZHI * CORES)
    slab = hidden // (XS * ZHI * CORES)
    taken = PATCH * PATCH
    rows = taken * SUB
    copies = []
    own, own_other = (own_near, own_far), (own_near_other, own_far_other)
    cross, cross_other = (cross_near, cross_far), (cross_near_other, cross_far_other)

    def place(piece, at, source_x, of_zhi, of_core, half=0, count=1):
        shard = lax.rem(source_x, XS) * (ZHI * CORES) + of_zhi * CORES + of_core
        size = depth // count
        lines = pl.ds(at, size)

        def put(columns, into):
            copy = pltpu.make_async_copy(piece.at[lines, columns], into, sems.at[len(copies)])
            copy.start()
            copies.append(copy)

        begin = pl.multiple_of(shard * depth + half * size, size)
        put(pl.ds(0, hidden), w_in.at[pl.ds(begin, size), :])
        for part in range(slab // depth):
            begin = pl.multiple_of(shard * slab + part * depth + half * size, size)
            put(pl.ds(hidden + part * align, align), w_out.at[pl.ds(begin, size), :])

    for of_zhi, by_core in (
        (zhi, ((core, own), (1 - core, own_other))),
        (1 - zhi, ((core, cross), (1 - core, cross_other))),
    ):
        for of_core, (near, opposite) in by_core:
            for k, step in enumerate((0, 1, XS - 1)):
                place(near, k * depth, x + step, of_zhi, of_core)
            for half in range(2):
                place(opposite, half * depth // 2, x + 2, of_zhi, of_core, half, 2)

    lat = lat_ref[...] + below_ref[...] + above_ref[...]
    top = lat.astype(BF16)
    rest = lat - top.astype(F32)
    mid = rest.astype(BF16)
    low_part = (rest - mid.astype(F32)).astype(BF16)
    split = jnp.concatenate(
        [top.astype(F32), mid.astype(F32), low_part.astype(F32)], axis=0
    ).astype(BF16)
    cells = lat.shape[1]
    tokens = target_ref.shape[0]
    room = 256
    cols = across // PATCH

    def selection(u, v):
        shape = (cells, room)
        token = iota(shape, 1)
        lane = (token // cols) * (PATCH * across) + u * across + (token % cols) * PATCH + v
        return jnp.where((lane == iota(shape, 0)) & (token < tokens), 1.0, 0.0).astype(BF16)

    picks = [selection(u, v) for u in range(PATCH) for v in range(PATCH)]
    lines = []
    for pick in picks:
        got = nn(split, pick)
        lines.append(got[0:SUB] + got[SUB : 2 * SUB] + got[2 * SUB :])
    patches_t = jnp.concatenate(lines, axis=0)
    patches = patches_t.T
    empty = jnp.zeros((SUB - LATENT, width), F32)
    spread = []
    for k in range(taken):
        spread += [ew_ref[k * LATENT : (k + 1) * LATENT, :], empty]
    ew_top, ew_low = parts(jnp.concatenate(spread, axis=0))
    p_top, p_low = parts(patches[:tokens])
    embedded = nn(p_top, ew_top) + nn(p_low, ew_top) + nn(p_top, ew_low)
    emb[...] = (embedded + eb_ref[...]).astype(BF16)

    for copy in copies:
        copy.wait()

    step = 512
    acc[...] = jnp.zeros_like(acc)

    @pl.loop(0, hidden // step)
    def _(tile):
        at = pl.ds(pl.multiple_of(tile * step, step), step)
        h = nn(emb[...], w_in[:, at]) + pib_ref[:, at]
        pre[:, at] = h
        acc[...] += nn((h * sigmoid(h)).astype(BF16), w_out[at, :])

    projected = acc[...] + pob_ref[...]
    target = target_ref[...].astype(F32)
    unit_target = target * lax.rsqrt(jnp.sum(target * target, axis=1, keepdims=True) + EPS_UNIT)
    inv_len = lax.rsqrt(jnp.sum(projected * projected, axis=1, keepdims=True) + EPS_UNIT)
    unit_proj = projected * inv_len
    cosine = jnp.sum(unit_proj * unit_target, axis=1, keepdims=True)
    grad_out = (-inv_len * (unit_target - cosine * unit_proj)).astype(BF16)
    grad_emb[...] = jnp.zeros_like(grad_emb)

    @pl.loop(0, hidden // step)
    def _(tile):
        at = pl.ds(pl.multiple_of(tile * step, step), step)
        back = nt(grad_out, w_out[at, :])
        h = pre[:, at]
        sig = sigmoid(h)
        grad_hidden = (back * (sig * (1.0 + h * (1.0 - sig)))).astype(BF16)
        grad_emb[0:tokens, :] += nt(grad_hidden, w_in[:, at])

    grad = grad_emb[...]
    g_top, g_low = parts(grad)
    t_top, t_low = parts(patches_t)
    both = nn(jnp.concatenate([t_top, t_low], axis=0), g_top)
    embed_ref[...] = both[:rows] + both[rows:] + nn(t_top, g_low)
    both = nt(jnp.concatenate([ew_top, ew_low], axis=0), g_top)
    grad_patch = both[:rows] + both[rows:] + nt(ew_top, g_low)
    total = jnp.zeros((SUB, cells), F32)
    for position, pick in enumerate(picks):
        part = grad_patch[position * SUB : (position + 1) * SUB].astype(BF16)
        total = total + nt(part, pick)
    gl_ref[...] = total


def projector(at, lat, below, above, target, ew, eb, pib, pob, pieces, across):
    rows, width = PATCH * PATCH * SUB, ew.shape[1]
    hidden, align = pib.shape[1], pob.shape[1]
    tokens = target.shape[0]
    flops = 2 * tokens * (2 * width * hidden + 2 * hidden * align)
    return pl.pallas_call(
        lambda *refs: mlp_kernel(across, width, hidden, align, *refs),
        out_shape=(
            jax.ShapeDtypeStruct((rows, width), F32),
            jax.ShapeDtypeStruct(lat.shape, F32),
        ),
        in_specs=[pl.BlockSpec(memory_space=pltpu.SMEM)]
        + [vmem()] * 8
        + [pl.BlockSpec(memory_space=pl.ANY)] * len(pieces),
        out_specs=(vmem(), vmem()),
        scratch_shapes=[
            pltpu.VMEM((width, hidden), BF16),
            pltpu.VMEM((hidden, align), BF16),
            pltpu.VMEM((tokens, hidden), F32),
            pltpu.VMEM((tokens, width), BF16),
            pltpu.VMEM((tokens, align), F32),
            pltpu.VMEM((256, width), F32),
            pltpu.SemaphoreType.DMA((60,)),
        ],
        compiler_params=params(32),
        cost_estimate=pl.CostEstimate(
            flops=flops, bytes_accessed=8 << 20, transcendentals=2 * tokens * hidden
        ),
        name="projector",
    )(at, lat, below, above, target, ew, eb, pib, pob, *pieces)


def back_kernel(
    across, gl_ref, before_ref, after_ref, f_ref, mean_ref, inv_ref, gain_ref, bias_ref,
    k_ref, embed_ref, send_ref, gs_ref, act, grads_t, by_bias, by_gain, pack,
):
    images, cells, channels = f_ref.shape
    per_group = channels // GROUPS
    gl, before, after = gl_ref[...], before_ref[...], after_ref[...]
    col, row = lane_masks(gl.shape, across)
    lines = (
        jnp.where(row == 0, roll(gl, -across), roll(after, across)),
        gl,
        jnp.where(row == 0, roll(before, -across), roll(gl, across)),
    )
    parts = []
    for g in lines:
        parts.append(jnp.where(col < across - 1, roll(g, -1), 0.0))
        parts.append(g)
        parts.append(jnp.where(col > 0, roll(g, 1), 0.0))
    parts.append(jnp.zeros((LANES - TAPS * SUB, gl.shape[1]), F32))
    grads = jnp.concatenate(parts, axis=0)
    grads_t[...] = grads.T.astype(BF16)
    gain, bias = gain_ref[...], bias_ref[...]
    by_bias[...] = jnp.zeros_like(by_bias)
    by_gain[...] = jnp.zeros_like(by_gain)
    for i in range(images):
        at = slice(i * cells, (i + 1) * cells)
        v = f_ref[i].astype(F32)
        normed = (v - mean_ref[i : i + 1, :]) * inv_ref[i : i + 1, :]
        shifted = normed * gain + bias
        sig = sigmoid(shifted)
        act[at, :] = (shifted * sig).astype(BF16)
        grad_active = nn(grads_t[at, :], k_ref[...])
        gs = grad_active * (sig * (1.0 + shifted * (1.0 - sig)))
        gs_ref[i] = gs
        by_bias[i : i + 1, :] = jnp.sum(gs, axis=0, keepdims=True)
        by_gain[i : i + 1, :] = jnp.sum(gs * normed, axis=0, keepdims=True)
    conv = nn(grads.astype(BF16), act[...])
    stat = nn(by_bias[...] * gain, to_groups(channels, per_group, 0), HIGH) + nn(
        by_gain[...] * gain, to_groups(channels, per_group, GROUPS), HIGH
    )
    bias_part = jnp.sum(by_bias[...], axis=0, keepdims=True)
    gain_part = jnp.sum(by_gain[...], axis=0, keepdims=True)
    packed = halves(pack_stats(stat))
    for r in range(CHUNKS):
        send_ref[r, CHUNK_ROWS:ALL_ROWS, :] = packed
    blocks = channels // LANES
    half = CHUNKS // 2
    pack[...] = jnp.zeros_like(pack)
    for r in range(half):
        block, latent = r // LATENT, r % LATENT
        lanes = slice(block * LANES, (block + 1) * LANES)
        for position in range(TAPS):
            line = position * SUB + latent
            pack[r, position : position + 1, :] = conv[line : line + 1, lanes]
        lanes = slice((r // 2) * LANES, (r // 2 + 1) * LANES)
        for part in range(2):
            line = (r % 2) * 2 * SUB + part * SUB
            pack[half + r, part * LATENT : (part + 1) * LATENT, :] = embed_ref[
                line : line + LATENT, lanes
            ]
        if r < 2 * blocks:
            one = gain_part if r < blocks else bias_part
            lanes = slice((r % blocks) * LANES, (r % blocks + 1) * LANES)
            pack[half + r, SUB : SUB + 1, :] = one[:, lanes]
    for r in range(CHUNKS):
        send_ref[r, 0:CHUNK_ROWS, :] = pack[r].astype(BF16)


def conv_backward(gl, before, after, features, mean, inv, gain, bias, kernel_rows, embed, across):
    images, cells, channels = features.shape
    return pl.pallas_call(
        lambda *refs: back_kernel(across, *refs),
        out_shape=(
            jax.ShapeDtypeStruct((CHUNKS, ALL_ROWS, LANES), BF16),
            jax.ShapeDtypeStruct((images, cells, channels), F32),
        ),
        in_specs=[vmem()] * 10,
        out_specs=(vmem(),) * 2,
        scratch_shapes=[
            pltpu.VMEM((images * cells, channels), BF16),
            pltpu.VMEM((images * cells, LANES), BF16),
            pltpu.VMEM((STAT_ROWS, channels), F32),
            pltpu.VMEM((STAT_ROWS, channels), F32),
            pltpu.VMEM((CHUNKS, CHUNK_ROWS, LANES), F32),
        ],
        compiler_params=params(),
        name="back",
    )(gl, before, after, features, mean, inv, gain, bias, kernel_rows, embed)


def last_kernel(members, got_ref, f_ref, mean_ref, inv_ref, gain_ref, gs_ref, out_ref):
    images, _, channels = f_ref.shape
    per_group = channels // GROUPS
    total = unpack_stats(got_ref[...])
    first = nn(total, from_groups(channels, per_group, 0), HIGH) * (1.0 / members)
    second = nn(total, from_groups(channels, per_group, GROUPS), HIGH) * (1.0 / members)
    gain = gain_ref[...]
    for i in range(images):
        v = f_ref[i].astype(F32)
        inv = inv_ref[i : i + 1, :]
        normed = (v - mean_ref[i : i + 1, :]) * inv
        out = inv * (gs_ref[i] * gain - first[i : i + 1] - normed * second[i : i + 1])
        out_ref[i] = out.astype(BF16)


def feature_grad(got, features, mean, inv, gain, grad_shift, members):
    return pl.pallas_call(
        lambda *refs: last_kernel(members, *refs),
        out_shape=jax.ShapeDtypeStruct(features.shape, BF16),
        in_specs=[vmem()] * 6,
        out_specs=vmem(),
        compiler_params=params(),
        cost_estimate=pl.CostEstimate(
            flops=10 * features.size, bytes_accessed=8 * features.size, transcendentals=0
        ),
        name="last",
    )(got, features, mean, inv, gain, grad_shift)


def plane_kernel(at_ref, got_ref, out_ref):
    chunk = jnp.zeros((CHUNK_ROWS, LANES), F32)
    stat = jnp.zeros((SUB, LANES), F32)
    for r in range(CHUNKS):
        chunk = chunk + got_ref[r, 0:CHUNK_ROWS, :].astype(F32)
        pair = got_ref[r, CHUNK_ROWS:ALL_ROWS, :].astype(F32)
        stat = stat + jnp.where(at_ref[2] == (r // CORES) % YS, pair[:SUB] + pair[SUB:], 0.0)
    chunk, stat = chunk.astype(BF16), halves(stat)
    for r in range(out_ref.shape[0]):
        out_ref[r, 0:CHUNK_ROWS, :] = chunk
        out_ref[r, CHUNK_ROWS:ALL_ROWS, :] = stat


def plane_total(at, got):
    return pl.pallas_call(
        plane_kernel,
        out_shape=jax.ShapeDtypeStruct((ZHI * ZLO, ALL_ROWS, LANES), BF16),
        in_specs=[pl.BlockSpec(memory_space=pltpu.SMEM), vmem()],
        out_specs=vmem(),
        compiler_params=params(),
        name="plane",
    )(at, got)


def column_kernel(at_ref, got_ref, out_ref, stat_ref):
    chunk = jnp.zeros((CHUNK_ROWS, LANES), F32)
    stat = jnp.zeros((SUB, LANES), F32)
    for r in range(ZHI * ZLO):
        chunk = chunk + got_ref[r, 0:CHUNK_ROWS, :].astype(F32)
        pair = got_ref[r, CHUNK_ROWS:ALL_ROWS, :].astype(F32)
        stat = stat + jnp.where(at_ref[3] == r % ZLO, pair[:SUB] + pair[SUB:], 0.0)
    chunk = chunk.astype(BF16)
    for r in range(out_ref.shape[0]):
        out_ref[r] = chunk
    stat_ref[...] = stat


def column_total(at, got):
    return pl.pallas_call(
        column_kernel,
        out_shape=(
            jax.ShapeDtypeStruct((CHUNKS, CHUNK_ROWS, LANES), BF16),
            jax.ShapeDtypeStruct((SUB, LANES), F32),
        ),
        in_specs=[pl.BlockSpec(memory_space=pltpu.SMEM), vmem()],
        out_specs=(vmem(), vmem()),
        compiler_params=params(),
        name="column",
    )(at, got)


def unpack_kernel(got_ref, conv_ref, gain_ref, bias_ref, embed_ref, wide):
    channels = gain_ref.shape[1]
    blocks = channels // LANES
    half = CHUNKS // 2
    wide[...] = got_ref[...].astype(F32)
    for r in range(half):
        block, latent = r // LATENT, r % LATENT
        for position in range(TAPS):
            at = position * channels + block * LANES
            conv_ref[latent : latent + 1, at : at + LANES] = wide[r, position : position + 1, :]
        lanes = slice((r // 2) * LANES, (r // 2 + 1) * LANES)
        line = (r % 2) * SUB
        embed_ref[line : line + SUB, lanes] = wide[half + r, 0:SUB, :]
        lanes = slice((r % blocks) * LANES, (r % blocks + 1) * LANES)
        if r < blocks:
            gain_ref[:, lanes] = wide[half + r, SUB : SUB + 1, :]
        elif r < 2 * blocks:
            bias_ref[:, lanes] = wide[half + r, SUB : SUB + 1, :]


def unpack(got, channels, width):
    return pl.pallas_call(
        unpack_kernel,
        out_shape=(
            jax.ShapeDtypeStruct((LATENT, TAPS * channels), F32),
            jax.ShapeDtypeStruct((1, channels), F32),
            jax.ShapeDtypeStruct((1, channels), F32),
            jax.ShapeDtypeStruct((PATCH * PATCH * LATENT, width), F32),
        ),
        in_specs=[vmem()],
        out_specs=(vmem(),) * 4,
        scratch_shapes=[pltpu.VMEM(got.shape, F32)],
        compiler_params=params(),
        name="unpack",
    )(got)


def device(x, zhi, core, zlo, y):
    return ((x * ZHI + zhi) * CORES + core) * (ZLO * YS) + zlo * YS + y


BOTH = ("rows", "batch")
PLANE = [
    [device(x, h, c, d, y) for x in range(XS) for y in range(YS) for c in range(CORES)]
    for h in range(ZHI)
    for d in range(ZLO)
]
COLUMN = [
    [device(x, h, c, d, y) for h in range(ZHI) for d in range(ZLO)]
    for x in range(XS)
    for y in range(YS)
    for c in range(CORES)
]


def exchanged(value, groups):
    return lax.all_to_all(value, BOTH, 0, 0, axis_index_groups=groups, tiled=True)


def moved(value, where):
    pairs = []
    for x in range(XS):
        for zhi in range(ZHI):
            for core in range(CORES):
                for zlo in range(ZLO):
                    for y in range(YS):
                        a, b, c, d, e = where(x, zhi, core, zlo, y)
                        pairs.append((device(x, zhi, core, zlo, y), device(a, b, c, d, e)))
    return lax.ppermute(value, ("rows", "batch"), pairs)


def crossed(shard):
    y = lax.axis_index("batch") % YS
    mine = lax.dynamic_slice_in_dim(shard, y * PART, PART, axis=0)
    return moved(mine, lambda x, h, c, d, y: (x, 1 - h, c, ZLO - 1 - d, y))


def along_y(part):
    y = lax.axis_index("batch") % YS
    other = moved(part, lambda x, h, c, d, y: (x, h, c, d, y ^ 1))
    even = y % 2 == 0
    pair = jnp.concatenate([jnp.where(even, part, other), jnp.where(even, other, part)], axis=0)
    far = moved(pair, lambda x, h, c, d, y: (x, h, c, d, YS - 1 - y))
    low = y < 2
    return jnp.concatenate([jnp.where(low, pair, far), jnp.where(low, far, pair)], axis=0)


def from_next(value):
    return moved(value, lambda x, h, c, d, y: ((x + XS - 1) % XS, h, c, d, y))


def from_last(value):
    return moved(value, lambda x, h, c, d, y: ((x + 1) % XS, h, c, d, y))


def along_x(shard):
    half = shard.shape[0] // 2
    plus, minus = from_next(shard), from_last(shard)
    near = jnp.concatenate([shard, plus, minus], axis=0)
    opposite = jnp.concatenate([from_next(plus[:half]), from_last(minus[half:])], axis=0)
    return near, opposite


def swapped(value):
    return moved(value, lambda x, h, c, d, y: (x, h, 1 - c, d, y))


def neighbours(up, down):
    count = lax.axis_size("rows")
    forward = [(i, i + 1) for i in range(count - 1)]
    backward = [(b, a) for a, b in forward]
    return lax.ppermute(up, "rows", backward), lax.ppermute(down, "rows", forward)


def shards(
    features,
    norm_gain,
    norm_bias,
    conv_weight,
    embed_weight,
    embed_bias,
    proj_in,
    proj_in_bias,
    proj_out,
    proj_out_bias,
    targets,
):
    images, height, across, channels = features.shape
    width, align = embed_weight.shape[1], proj_out.shape[1]
    peers = lax.axis_size("rows")
    members = peers * height * across * (channels // GROUPS)
    flat = features.reshape(images, height * across, channels)
    gain, bias = norm_gain.reshape(1, channels), norm_bias.reshape(1, channels)
    depth = proj_in.shape[0]
    shard = jnp.concatenate(
        [proj_in] + [proj_out[at : at + depth] for at in range(0, proj_out.shape[0], depth)], axis=1
    )
    far = crossed(shard)
    own_near, own_far = along_x(shard)
    taps = conv_weight.reshape(LATENT, TAPS, channels).transpose(1, 0, 2)
    taps = jnp.pad(taps, ((0, 0), (0, SUB - LATENT), (0, 0))).reshape(TAPS * SUB, channels)
    taps_full = jnp.pad(taps, ((0, LANES - TAPS * SUB), (0, 0)))

    sums = group_stats(flat, peers)
    stats = lax.all_to_all(sums, "rows", 0, 0, tiled=True)
    far, sums_ = lax.optimization_barrier((far, sums))
    cross = along_y(far)
    cross, own_near, own_far = lax.optimization_barrier((cross, own_near, own_far))
    stats, own_far = lax.optimization_barrier((stats, own_far))
    cross_near, cross_far = along_x(cross)
    lat, up, down, mean, inv = conv_forward(stats, flat, gain, bias, taps, across, members)
    above, below = neighbours(up, down)
    own_near, own_far, above, below = lax.optimization_barrier((own_near, own_far, above, below))
    pieces = [own_near, own_far, cross_near, cross_far]
    pieces = pieces + [swapped(v) for v in pieces]
    rows, batch = lax.axis_index("rows"), lax.axis_index("batch")
    at = jnp.stack([(rows // CORES) % ZHI, rows % CORES, batch % YS, batch // YS, rows // (ZHI * CORES)])
    at = at.astype(jnp.int32)
    target = targets.reshape(-1, align)
    embed_part, grad_lat = projector(
        at, lat, below, above, target, embed_weight, embed_bias.reshape(1, -1),
        proj_in_bias.reshape(1, -1), proj_out_bias.reshape(1, -1), pieces, across,
    )
    after, before = neighbours(grad_lat, grad_lat)
    send, grad_shift = conv_backward(
        grad_lat, before, after, flat, mean, inv, gain, bias, taps_full, embed_part, across
    )
    plane = exchanged(send, PLANE)
    column = exchanged(plane_total(at, plane), COLUMN)
    chunks, got = column_total(at, column)
    everything = exchanged(chunks, PLANE)
    grad_features = feature_grad(got, flat, mean, inv, gain, grad_shift, members)
    grad_conv, grad_gain, grad_bias, grad_embed = unpack(everything, channels, width)
    return (
        grad_features.reshape(features.shape),
        grad_conv,
        grad_gain.reshape(channels),
        grad_bias.reshape(channels),
        grad_embed,
    )


def solution(mesh):
    in_specs = (
        P("batch", "rows", None, None),
        P(),
        P(),
        P(),
        P(),
        P(),
        P("rows", None),
        P(),
        P("rows", None),
        P(),
        P("batch", "rows", None, None),
    )
    out_specs = (P("batch", "rows", None, None), P(), P(), P(), P())
    return jax.shard_map(shards, mesh=mesh, in_specs=in_specs, out_specs=out_specs, check_vma=False)
```

```python
import jax
import jax.numpy as jnp
from jax import lax
from jax.experimental import pallas as pl
from jax.experimental.pallas import tpu as pltpu
from jax.sharding import PartitionSpec as P

GROUPS = 32
LATENT = 4
PATCH = 2
EPS_NORM = 1e-06
EPS_UNIT = 1e-06

XS, ZHI, CORES, ZLO, YS = 4, 2, 2, 8, 4

HIGH = lax.Precision.HIGHEST
F32 = jnp.float32
BF16 = jnp.bfloat16
TAPS = 9
SUB = 8
LANES = 128
STAT_ROWS = 16
CHUNKS, CHUNK_ROWS, ALL_ROWS = 32, 16, 32
CONV_COST = 20_000_000_000
PART = 16


def params(limit_mb=12):
    return pltpu.CompilerParams(vmem_limit_bytes=limit_mb << 20)


def vmem():
    return pl.BlockSpec(memory_space=pltpu.VMEM)


def sigmoid(v):
    return 0.5 + 0.5 * jnp.tanh(0.5 * v)


def nt(a, b, precision=None):
    return lax.dot_general(
        a, b, (((1,), (1,)), ((), ())), preferred_element_type=F32, precision=precision
    )


def nn(a, b, precision=None):
    return lax.dot_general(
        a, b, (((1,), (0,)), ((), ())), preferred_element_type=F32, precision=precision
    )


def iota(shape, dim):
    return lax.broadcasted_iota(jnp.int32, shape, dim)


def to_groups(channels, per_group, offset):
    shape = (channels, LANES)
    return (iota(shape, 0) // per_group + offset == iota(shape, 1)).astype(F32)


def from_groups(channels, per_group, offset):
    shape = (LANES, channels)
    return (iota(shape, 1) // per_group + offset == iota(shape, 0)).astype(F32)


def pack_stats(total):
    lane = iota((SUB, LANES), 1)
    return jnp.where(lane < LANES // 2, total[:SUB], pltpu.roll(total[SUB:], LANES // 2, 1))


def unpack_stats(packed):
    return jnp.concatenate([packed, pltpu.roll(packed, LANES // 2, 1)], axis=0)


def parts(v):
    top = v.astype(BF16)
    return top, (v - top.astype(F32)).astype(BF16)


def halves(packed):
    top = packed.astype(BF16).astype(F32)
    return jnp.concatenate([top, packed - top], axis=0).astype(BF16)


def stats_kernel(f_ref, out_ref, sums, squares):
    images, _, channels = f_ref.shape
    sums[...] = jnp.zeros_like(sums)
    squares[...] = jnp.zeros_like(squares)
    for i in range(images):
        v = f_ref[i].astype(F32)
        sums[i : i + 1, :] = jnp.sum(v, axis=0, keepdims=True)
        squares[i : i + 1, :] = jnp.sum(v * v, axis=0, keepdims=True)
    per_group = channels // GROUPS
    total = nn(sums[...], to_groups(channels, per_group, 0), HIGH) + nn(
        squares[...], to_groups(channels, per_group, GROUPS), HIGH
    )
    packed = pack_stats(total)
    for r in range(out_ref.shape[0]):
        out_ref[r] = packed


def group_stats(features, peers):
    channels = features.shape[-1]
    return pl.pallas_call(
        stats_kernel,
        out_shape=jax.ShapeDtypeStruct((peers, SUB, LANES), F32),
        in_specs=[vmem()],
        out_specs=vmem(),
        scratch_shapes=[pltpu.VMEM((STAT_ROWS, channels), F32)] * 2,
        compiler_params=params(),
        name="stats",
    )(features)


def lane_masks(shape, across):
    lane = iota(shape, 1)
    return lane % across, (lane // across) % 2


def roll(v, shift):
    return pltpu.roll(v, shift % v.shape[1], 1)


def conv_kernel(
    across, members, st_ref, f_ref, gain_ref, bias_ref, k_ref,
    lat_ref, up_ref, down_ref, mean_ref, inv_ref, act,
):
    images, cells, channels = f_ref.shape
    per_group = channels // GROUPS
    total = unpack_stats(jnp.sum(st_ref[...], axis=0))
    mean = nn(total, from_groups(channels, per_group, 0), HIGH) * (1.0 / members)
    square = nn(total, from_groups(channels, per_group, GROUPS), HIGH) * (1.0 / members)
    inv = lax.rsqrt(jnp.maximum(square - mean * mean, 0.0) + EPS_NORM)
    mean_ref[...] = mean
    inv_ref[...] = inv
    gain, bias = gain_ref[...], bias_ref[...]
    for i in range(images):
        v = f_ref[i].astype(F32)
        shifted = (v - mean[i : i + 1]) * inv[i : i + 1] * gain + bias
        act[i * cells : (i + 1) * cells, :] = (shifted * sigmoid(shifted)).astype(BF16)
    taps = nt(k_ref[...], act[...])
    shape = (SUB, images * cells)
    col, row = lane_masks(shape, across)

    def tap(position):
        return taps[position * SUB : (position + 1) * SUB]

    def line(dy):
        low = jnp.where(col > 0, roll(tap(3 * dy), 1), 0.0)
        high = jnp.where(col < across - 1, roll(tap(3 * dy + 2), -1), 0.0)
        return tap(3 * dy + 1) + low + high

    first, middle, last = line(0), line(1), line(2)
    last_up, first_down = roll(last, -across), roll(first, across)
    lat_ref[...] = middle + jnp.where(row == 0, last_up, first_down)
    up_ref[...] = jnp.where(row == 1, roll(last, across), 0.0)
    down_ref[...] = jnp.where(row == 0, roll(first, -across), 0.0)


def conv_forward(stats, features, gain, bias, kernel_rows, across, members):
    images, cells, channels = features.shape
    line = jax.ShapeDtypeStruct((SUB, images * cells), F32)
    stat = jax.ShapeDtypeStruct((STAT_ROWS, channels), F32)
    return pl.pallas_call(
        lambda *refs: conv_kernel(across, members, *refs),
        out_shape=(line, line, line, stat, stat),
        in_specs=[vmem()] * 5,
        out_specs=(vmem(),) * 5,
        scratch_shapes=[pltpu.VMEM((images * cells, channels), BF16)],
        compiler_params=params(),
        cost_estimate=pl.CostEstimate(
            flops=CONV_COST, bytes_accessed=features.size * 2, transcendentals=features.size
        ),
        name="conv",
    )(stats, features, gain, bias, kernel_rows)


def mlp_kernel(
    across, width, hidden, align, at_ref, lat_ref, below_ref, above_ref, target_ref,
    ew_ref, eb_ref, pib_ref, pob_ref,
    own, cross, own_other, cross_other,
    embed_ref, gl_ref, w_in, w_out, pre, emb, acc, grad_emb, sems,
):
    zhi, core = at_ref[0], at_ref[1]
    depth = width // (XS * ZHI * CORES)
    slab = hidden // (XS * ZHI * CORES)
    taken = PATCH * PATCH
    rows = taken * SUB
    copies = []

    for piece, of_zhi, of_core in (
        (own, zhi, core),
        (own_other, zhi, 1 - core),
        (cross, 1 - zhi, core),
        (cross_other, 1 - zhi, 1 - core),
    ):
        for x in range(XS):
            shard = x * (ZHI * CORES) + of_zhi * CORES + of_core
            lines = pl.ds(x * depth, depth)

            def put(columns, into):
                copy = pltpu.make_async_copy(piece.at[lines, columns], into, sems.at[len(copies)])
                copy.start()
                copies.append(copy)

            put(pl.ds(0, hidden), w_in.at[pl.ds(pl.multiple_of(shard * depth, depth), depth), :])
            for part in range(slab // depth):
                begin = pl.multiple_of(shard * slab + part * depth, depth)
                put(pl.ds(hidden + part * align, align), w_out.at[pl.ds(begin, depth), :])

    lat = lat_ref[...] + below_ref[...] + above_ref[...]
    top = lat.astype(BF16)
    rest = lat - top.astype(F32)
    mid = rest.astype(BF16)
    low_part = (rest - mid.astype(F32)).astype(BF16)
    split = jnp.concatenate(
        [top.astype(F32), mid.astype(F32), low_part.astype(F32)], axis=0
    ).astype(BF16)
    cells = lat.shape[1]
    tokens = target_ref.shape[0]
    room = 256
    cols = across // PATCH

    def selection(u, v):
        shape = (cells, room)
        token = iota(shape, 1)
        lane = (token // cols) * (PATCH * across) + u * across + (token % cols) * PATCH + v
        return jnp.where((lane == iota(shape, 0)) & (token < tokens), 1.0, 0.0).astype(BF16)

    picks = [selection(u, v) for u in range(PATCH) for v in range(PATCH)]
    lines = []
    for pick in picks:
        got = nn(split, pick)
        lines.append(got[0:SUB] + got[SUB : 2 * SUB] + got[2 * SUB :])
    patches_t = jnp.concatenate(lines, axis=0)
    patches = patches_t.T
    empty = jnp.zeros((SUB - LATENT, width), F32)
    spread = []
    for k in range(taken):
        spread += [ew_ref[k * LATENT : (k + 1) * LATENT, :], empty]
    ew_top, ew_low = parts(jnp.concatenate(spread, axis=0))
    p_top, p_low = parts(patches[:tokens])
    embedded = nn(p_top, ew_top) + nn(p_low, ew_top) + nn(p_top, ew_low)
    emb[...] = (embedded + eb_ref[...]).astype(BF16)

    for copy in copies:
        copy.wait()

    step = 512
    acc[...] = jnp.zeros_like(acc)

    @pl.loop(0, hidden // step)
    def _(tile):
        at = pl.ds(pl.multiple_of(tile * step, step), step)
        h = nn(emb[...], w_in[:, at]) + pib_ref[:, at]
        pre[:, at] = h
        acc[...] += nn((h * sigmoid(h)).astype(BF16), w_out[at, :])

    projected = acc[...] + pob_ref[...]
    target = target_ref[...].astype(F32)
    unit_target = target * lax.rsqrt(jnp.sum(target * target, axis=1, keepdims=True) + EPS_UNIT)
    inv_len = lax.rsqrt(jnp.sum(projected * projected, axis=1, keepdims=True) + EPS_UNIT)
    unit_proj = projected * inv_len
    cosine = jnp.sum(unit_proj * unit_target, axis=1, keepdims=True)
    grad_out = (-inv_len * (unit_target - cosine * unit_proj)).astype(BF16)
    grad_emb[...] = jnp.zeros_like(grad_emb)

    @pl.loop(0, hidden // step)
    def _(tile):
        at = pl.ds(pl.multiple_of(tile * step, step), step)
        back = nt(grad_out, w_out[at, :])
        h = pre[:, at]
        sig = sigmoid(h)
        grad_hidden = (back * (sig * (1.0 + h * (1.0 - sig)))).astype(BF16)
        grad_emb[0:tokens, :] += nt(grad_hidden, w_in[:, at])

    grad = grad_emb[...]
    g_top, g_low = parts(grad)
    t_top, t_low = parts(patches_t)
    both = nn(jnp.concatenate([t_top, t_low], axis=0), g_top)
    embed_ref[...] = both[:rows] + both[rows:] + nn(t_top, g_low)
    both = nt(jnp.concatenate([ew_top, ew_low], axis=0), g_top)
    grad_patch = both[:rows] + both[rows:] + nt(ew_top, g_low)
    total = jnp.zeros((SUB, cells), F32)
    for position, pick in enumerate(picks):
        part = grad_patch[position * SUB : (position + 1) * SUB].astype(BF16)
        total = total + nt(part, pick)
    gl_ref[...] = total


def projector(at, lat, below, above, target, ew, eb, pib, pob, pieces, across):
    rows, width = PATCH * PATCH * SUB, ew.shape[1]
    hidden, align = pib.shape[1], pob.shape[1]
    tokens = target.shape[0]
    flops = 2 * tokens * (2 * width * hidden + 2 * hidden * align)
    return pl.pallas_call(
        lambda *refs: mlp_kernel(across, width, hidden, align, *refs),
        out_shape=(
            jax.ShapeDtypeStruct((rows, width), F32),
            jax.ShapeDtypeStruct(lat.shape, F32),
        ),
        in_specs=[pl.BlockSpec(memory_space=pltpu.SMEM)]
        + [vmem()] * 8
        + [pl.BlockSpec(memory_space=pltpu.HBM)] * len(pieces),
        out_specs=(vmem(), vmem()),
        scratch_shapes=[
            pltpu.VMEM((width, hidden), BF16),
            pltpu.VMEM((hidden, align), BF16),
            pltpu.VMEM((tokens, hidden), F32),
            pltpu.VMEM((tokens, width), BF16),
            pltpu.VMEM((tokens, align), F32),
            pltpu.VMEM((256, width), F32),
            pltpu.SemaphoreType.DMA((48,)),
        ],
        compiler_params=params(32),
        cost_estimate=pl.CostEstimate(
            flops=flops, bytes_accessed=8 << 20, transcendentals=2 * tokens * hidden
        ),
        name="projector",
    )(at, lat, below, above, target, ew, eb, pib, pob, *pieces)


def back_kernel(
    across, gl_ref, before_ref, after_ref, f_ref, mean_ref, inv_ref, gain_ref, bias_ref,
    k_ref, embed_ref, send_ref, gs_ref, act, grads_t, by_bias, by_gain, pack,
):
    images, cells, channels = f_ref.shape
    per_group = channels // GROUPS
    gl, before, after = gl_ref[...], before_ref[...], after_ref[...]
    col, row = lane_masks(gl.shape, across)
    lines = (
        jnp.where(row == 0, roll(gl, -across), roll(after, across)),
        gl,
        jnp.where(row == 0, roll(before, -across), roll(gl, across)),
    )
    parts = []
    for g in lines:
        parts.append(jnp.where(col < across - 1, roll(g, -1), 0.0))
        parts.append(g)
        parts.append(jnp.where(col > 0, roll(g, 1), 0.0))
    parts.append(jnp.zeros((LANES - TAPS * SUB, gl.shape[1]), F32))
    grads = jnp.concatenate(parts, axis=0)
    grads_t[...] = grads.T.astype(BF16)
    gain, bias = gain_ref[...], bias_ref[...]
    by_bias[...] = jnp.zeros_like(by_bias)
    by_gain[...] = jnp.zeros_like(by_gain)
    for i in range(images):
        at = slice(i * cells, (i + 1) * cells)
        v = f_ref[i].astype(F32)
        normed = (v - mean_ref[i : i + 1, :]) * inv_ref[i : i + 1, :]
        shifted = normed * gain + bias
        sig = sigmoid(shifted)
        act[at, :] = (shifted * sig).astype(BF16)
        grad_active = nn(grads_t[at, :], k_ref[...])
        gs = grad_active * (sig * (1.0 + shifted * (1.0 - sig)))
        gs_ref[i] = gs
        by_bias[i : i + 1, :] = jnp.sum(gs, axis=0, keepdims=True)
        by_gain[i : i + 1, :] = jnp.sum(gs * normed, axis=0, keepdims=True)
    conv = nn(grads.astype(BF16), act[...])
    stat = nn(by_bias[...] * gain, to_groups(channels, per_group, 0), HIGH) + nn(
        by_gain[...] * gain, to_groups(channels, per_group, GROUPS), HIGH
    )
    bias_part = jnp.sum(by_bias[...], axis=0, keepdims=True)
    gain_part = jnp.sum(by_gain[...], axis=0, keepdims=True)
    packed = halves(pack_stats(stat))
    for r in range(CHUNKS):
        send_ref[r, CHUNK_ROWS:ALL_ROWS, :] = packed
    blocks = channels // LANES
    half = CHUNKS // 2
    pack[...] = jnp.zeros_like(pack)
    for r in range(half):
        block, latent = r // LATENT, r % LATENT
        lanes = slice(block * LANES, (block + 1) * LANES)
        for position in range(TAPS):
            line = position * SUB + latent
            pack[r, position : position + 1, :] = conv[line : line + 1, lanes]
        lanes = slice((r // 2) * LANES, (r // 2 + 1) * LANES)
        for part in range(2):
            line = (r % 2) * 2 * SUB + part * SUB
            pack[half + r, part * LATENT : (part + 1) * LATENT, :] = embed_ref[
                line : line + LATENT, lanes
            ]
        if r < 2 * blocks:
            one = gain_part if r < blocks else bias_part
            lanes = slice((r % blocks) * LANES, (r % blocks + 1) * LANES)
            pack[half + r, SUB : SUB + 1, :] = one[:, lanes]
    for r in range(CHUNKS):
        send_ref[r, 0:CHUNK_ROWS, :] = pack[r].astype(BF16)


def conv_backward(gl, before, after, features, mean, inv, gain, bias, kernel_rows, embed, across):
    images, cells, channels = features.shape
    return pl.pallas_call(
        lambda *refs: back_kernel(across, *refs),
        out_shape=(
            jax.ShapeDtypeStruct((CHUNKS, ALL_ROWS, LANES), BF16),
            jax.ShapeDtypeStruct((images, cells, channels), F32),
        ),
        in_specs=[vmem()] * 10,
        out_specs=(vmem(),) * 2,
        scratch_shapes=[
            pltpu.VMEM((images * cells, channels), BF16),
            pltpu.VMEM((images * cells, LANES), BF16),
            pltpu.VMEM((STAT_ROWS, channels), F32),
            pltpu.VMEM((STAT_ROWS, channels), F32),
            pltpu.VMEM((CHUNKS, CHUNK_ROWS, LANES), F32),
        ],
        compiler_params=params(),
        name="back",
    )(gl, before, after, features, mean, inv, gain, bias, kernel_rows, embed)


def last_kernel(members, got_ref, f_ref, mean_ref, inv_ref, gain_ref, gs_ref, out_ref):
    images, _, channels = f_ref.shape
    per_group = channels // GROUPS
    total = unpack_stats(got_ref[...])
    first = nn(total, from_groups(channels, per_group, 0), HIGH) * (1.0 / members)
    second = nn(total, from_groups(channels, per_group, GROUPS), HIGH) * (1.0 / members)
    gain = gain_ref[...]
    for i in range(images):
        v = f_ref[i].astype(F32)
        inv = inv_ref[i : i + 1, :]
        normed = (v - mean_ref[i : i + 1, :]) * inv
        out = inv * (gs_ref[i] * gain - first[i : i + 1] - normed * second[i : i + 1])
        out_ref[i] = out.astype(BF16)


def feature_grad(got, features, mean, inv, gain, grad_shift, members):
    return pl.pallas_call(
        lambda *refs: last_kernel(members, *refs),
        out_shape=jax.ShapeDtypeStruct(features.shape, BF16),
        in_specs=[vmem()] * 6,
        out_specs=vmem(),
        compiler_params=params(),
        cost_estimate=pl.CostEstimate(
            flops=10 * features.size, bytes_accessed=8 * features.size, transcendentals=0
        ),
        name="last",
    )(got, features, mean, inv, gain, grad_shift)


def plane_kernel(at_ref, got_ref, out_ref):
    chunk = jnp.zeros((CHUNK_ROWS, LANES), F32)
    stat = jnp.zeros((SUB, LANES), F32)
    for r in range(CHUNKS):
        chunk = chunk + got_ref[r, 0:CHUNK_ROWS, :].astype(F32)
        pair = got_ref[r, CHUNK_ROWS:ALL_ROWS, :].astype(F32)
        stat = stat + jnp.where(at_ref[2] == (r // CORES) % YS, pair[:SUB] + pair[SUB:], 0.0)
    chunk, stat = chunk.astype(BF16), halves(stat)
    for r in range(out_ref.shape[0]):
        out_ref[r, 0:CHUNK_ROWS, :] = chunk
        out_ref[r, CHUNK_ROWS:ALL_ROWS, :] = stat


def plane_total(at, got):
    return pl.pallas_call(
        plane_kernel,
        out_shape=jax.ShapeDtypeStruct((ZHI * ZLO, ALL_ROWS, LANES), BF16),
        in_specs=[pl.BlockSpec(memory_space=pltpu.SMEM), vmem()],
        out_specs=vmem(),
        compiler_params=params(),
        name="plane",
    )(at, got)


def column_kernel(at_ref, got_ref, out_ref, stat_ref):
    chunk = jnp.zeros((CHUNK_ROWS, LANES), F32)
    stat = jnp.zeros((SUB, LANES), F32)
    for r in range(ZHI * ZLO):
        chunk = chunk + got_ref[r, 0:CHUNK_ROWS, :].astype(F32)
        pair = got_ref[r, CHUNK_ROWS:ALL_ROWS, :].astype(F32)
        stat = stat + jnp.where(at_ref[3] == r % ZLO, pair[:SUB] + pair[SUB:], 0.0)
    chunk = chunk.astype(BF16)
    for r in range(out_ref.shape[0]):
        out_ref[r] = chunk
    stat_ref[...] = stat


def column_total(at, got):
    return pl.pallas_call(
        column_kernel,
        out_shape=(
            jax.ShapeDtypeStruct((CHUNKS, CHUNK_ROWS, LANES), BF16),
            jax.ShapeDtypeStruct((SUB, LANES), F32),
        ),
        in_specs=[pl.BlockSpec(memory_space=pltpu.SMEM), vmem()],
        out_specs=(vmem(), vmem()),
        compiler_params=params(),
        name="column",
    )(at, got)


def unpack_kernel(got_ref, conv_ref, gain_ref, bias_ref, embed_ref, wide):
    channels = gain_ref.shape[1]
    blocks = channels // LANES
    half = CHUNKS // 2
    wide[...] = got_ref[...].astype(F32)
    for r in range(half):
        block, latent = r // LATENT, r % LATENT
        for position in range(TAPS):
            at = position * channels + block * LANES
            conv_ref[latent : latent + 1, at : at + LANES] = wide[r, position : position + 1, :]
        lanes = slice((r // 2) * LANES, (r // 2 + 1) * LANES)
        line = (r % 2) * SUB
        embed_ref[line : line + SUB, lanes] = wide[half + r, 0:SUB, :]
        lanes = slice((r % blocks) * LANES, (r % blocks + 1) * LANES)
        if r < blocks:
            gain_ref[:, lanes] = wide[half + r, SUB : SUB + 1, :]
        elif r < 2 * blocks:
            bias_ref[:, lanes] = wide[half + r, SUB : SUB + 1, :]


def unpack(got, channels, width):
    return pl.pallas_call(
        unpack_kernel,
        out_shape=(
            jax.ShapeDtypeStruct((LATENT, TAPS * channels), F32),
            jax.ShapeDtypeStruct((1, channels), F32),
            jax.ShapeDtypeStruct((1, channels), F32),
            jax.ShapeDtypeStruct((PATCH * PATCH * LATENT, width), F32),
        ),
        in_specs=[vmem()],
        out_specs=(vmem(),) * 4,
        scratch_shapes=[pltpu.VMEM(got.shape, F32)],
        compiler_params=params(),
        name="unpack",
    )(got)


def device(x, zhi, core, zlo, y):
    return ((x * ZHI + zhi) * CORES + core) * (ZLO * YS) + zlo * YS + y


BOTH = ("rows", "batch")
PLANE = [
    [device(x, h, c, d, y) for x in range(XS) for y in range(YS) for c in range(CORES)]
    for h in range(ZHI)
    for d in range(ZLO)
]
ALONG_X = [
    [device(x, h, c, d, y) for x in range(XS)]
    for h in range(ZHI)
    for c in range(CORES)
    for d in range(ZLO)
    for y in range(YS)
]
ALONG_Y = [
    [device(x, h, c, d, y) for y in range(YS)]
    for x in range(XS)
    for h in range(ZHI)
    for c in range(CORES)
    for d in range(ZLO)
]
COLUMN = [
    [device(x, h, c, d, y) for h in range(ZHI) for d in range(ZLO)]
    for x in range(XS)
    for y in range(YS)
    for c in range(CORES)
]


def exchanged(value, groups):
    return lax.all_to_all(value, BOTH, 0, 0, axis_index_groups=groups, tiled=True)


def moved(value, where):
    pairs = []
    for x in range(XS):
        for zhi in range(ZHI):
            for core in range(CORES):
                for zlo in range(ZLO):
                    for y in range(YS):
                        a, b, c, d, e = where(x, zhi, core, zlo, y)
                        pairs.append((device(x, zhi, core, zlo, y), device(a, b, c, d, e)))
    return lax.ppermute(value, ("rows", "batch"), pairs)


def crossed(shard):
    y = lax.axis_index("batch") % YS
    mine = lax.dynamic_slice_in_dim(shard, y * PART, PART, axis=0)
    return moved(mine, lambda x, h, c, d, y: (x, 1 - h, c, ZLO - 1 - d, y))


def gathered(part, groups):
    return lax.all_gather(part, BOTH, axis_index_groups=groups, tiled=True)


def swapped(value):
    return moved(value, lambda x, h, c, d, y: (x, h, 1 - c, d, y))


def neighbours(up, down):
    count = lax.axis_size("rows")
    forward = [(i, i + 1) for i in range(count - 1)]
    backward = [(b, a) for a, b in forward]
    return lax.ppermute(up, "rows", backward), lax.ppermute(down, "rows", forward)


def shards(
    features,
    norm_gain,
    norm_bias,
    conv_weight,
    embed_weight,
    embed_bias,
    proj_in,
    proj_in_bias,
    proj_out,
    proj_out_bias,
    targets,
):
    images, height, across, channels = features.shape
    width, align = embed_weight.shape[1], proj_out.shape[1]
    peers = lax.axis_size("rows")
    members = peers * height * across * (channels // GROUPS)
    flat = features.reshape(images, height * across, channels)
    gain, bias = norm_gain.reshape(1, channels), norm_bias.reshape(1, channels)
    depth = proj_in.shape[0]
    shard = jnp.concatenate(
        [proj_in] + [proj_out[at : at + depth] for at in range(0, proj_out.shape[0], depth)], axis=1
    )
    far = crossed(shard)
    own = gathered(shard, ALONG_X)
    taps = conv_weight.reshape(LATENT, TAPS, channels).transpose(1, 0, 2)
    taps = jnp.pad(taps, ((0, 0), (0, SUB - LATENT), (0, 0))).reshape(TAPS * SUB, channels)
    taps_full = jnp.pad(taps, ((0, LANES - TAPS * SUB), (0, 0)))

    sums = group_stats(flat, peers)
    stats = lax.all_to_all(sums, "rows", 0, 0, tiled=True)
    far, sums_ = lax.optimization_barrier((far, sums))
    cross = gathered(gathered(far, ALONG_Y), ALONG_X)
    lat, up, down, mean, inv = conv_forward(stats, flat, gain, bias, taps, across, members)
    above, below = neighbours(up, down)
    own, above, below = lax.optimization_barrier((own, above, below))
    pieces = [own, cross, swapped(own), swapped(cross)]
    rows, batch = lax.axis_index("rows"), lax.axis_index("batch")
    at = jnp.stack([(rows // CORES) % ZHI, rows % CORES, batch % YS, batch // YS])
    at = at.astype(jnp.int32)
    target = targets.reshape(-1, align)
    embed_part, grad_lat = projector(
        at, lat, below, above, target, embed_weight, embed_bias.reshape(1, -1),
        proj_in_bias.reshape(1, -1), proj_out_bias.reshape(1, -1), pieces, across,
    )
    after, before = neighbours(grad_lat, grad_lat)
    send, grad_shift = conv_backward(
        grad_lat, before, after, flat, mean, inv, gain, bias, taps_full, embed_part, across
    )
    plane = exchanged(send, PLANE)
    column = exchanged(plane_total(at, plane), COLUMN)
    chunks, got = column_total(at, column)
    everything = exchanged(chunks, PLANE)
    grad_features = feature_grad(got, flat, mean, inv, gain, grad_shift, members)
    grad_conv, grad_gain, grad_bias, grad_embed = unpack(everything, channels, width)
    return (
        grad_features.reshape(features.shape),
        grad_conv,
        grad_gain.reshape(channels),
        grad_bias.reshape(channels),
        grad_embed,
    )


def solution(mesh):
    in_specs = (
        P("batch", "rows", None, None),
        P(),
        P(),
        P(),
        P(),
        P(),
        P("rows", None),
        P(),
        P("rows", None),
        P(),
        P("batch", "rows", None, None),
    )
    out_specs = (P("batch", "rows", None, None), P(), P(), P(), P())
    return jax.shard_map(shards, mesh=mesh, in_specs=in_specs, out_specs=out_specs, check_vma=False)
```

```python
import jax
import jax.numpy as jnp
from jax import lax
from jax.experimental import pallas as pl
from jax.experimental.pallas import tpu as pltpu
from jax.sharding import PartitionSpec as P

GROUPS = 32
LATENT = 4
PATCH = 2
EPS_NORM = 1e-06
EPS_UNIT = 1e-06

XS, ZHI, CORES, ZLO, YS = 4, 2, 2, 8, 4

HIGH = lax.Precision.HIGHEST
F32 = jnp.float32
BF16 = jnp.bfloat16
TAPS = 9
SUB = 8
LANES = 128
STAT_ROWS = 16
CHUNKS, CHUNK_ROWS, ALL_ROWS = 32, 16, 32
CONV_COST = 20_000_000_000
PART = 16


def params(limit_mb=12):
    return pltpu.CompilerParams(vmem_limit_bytes=limit_mb << 20)


def vmem():
    return pl.BlockSpec(memory_space=pltpu.VMEM)


def sigmoid(v):
    return 0.5 + 0.5 * jnp.tanh(0.5 * v)


def nt(a, b, precision=None):
    return lax.dot_general(
        a, b, (((1,), (1,)), ((), ())), preferred_element_type=F32, precision=precision
    )


def nn(a, b, precision=None):
    return lax.dot_general(
        a, b, (((1,), (0,)), ((), ())), preferred_element_type=F32, precision=precision
    )


def iota(shape, dim):
    return lax.broadcasted_iota(jnp.int32, shape, dim)


def to_groups(channels, per_group, offset):
    shape = (channels, LANES)
    return (iota(shape, 0) // per_group + offset == iota(shape, 1)).astype(F32)


def from_groups(channels, per_group, offset):
    shape = (LANES, channels)
    return (iota(shape, 1) // per_group + offset == iota(shape, 0)).astype(F32)


def pack_stats(total):
    lane = iota((SUB, LANES), 1)
    return jnp.where(lane < LANES // 2, total[:SUB], pltpu.roll(total[SUB:], LANES // 2, 1))


def unpack_stats(packed):
    return jnp.concatenate([packed, pltpu.roll(packed, LANES // 2, 1)], axis=0)


def parts(v):
    top = v.astype(BF16)
    return top, (v - top.astype(F32)).astype(BF16)


def halves(packed):
    top = packed.astype(BF16).astype(F32)
    return jnp.concatenate([top, packed - top], axis=0).astype(BF16)


def stats_kernel(f_ref, out_ref, sums, squares):
    images, _, channels = f_ref.shape
    sums[...] = jnp.zeros_like(sums)
    squares[...] = jnp.zeros_like(squares)
    for i in range(images):
        v = f_ref[i].astype(F32)
        sums[i : i + 1, :] = jnp.sum(v, axis=0, keepdims=True)
        squares[i : i + 1, :] = jnp.sum(v * v, axis=0, keepdims=True)
    per_group = channels // GROUPS
    total = nn(sums[...], to_groups(channels, per_group, 0), HIGH) + nn(
        squares[...], to_groups(channels, per_group, GROUPS), HIGH
    )
    packed = pack_stats(total)
    for r in range(out_ref.shape[0]):
        out_ref[r] = packed


def group_stats(features, peers):
    channels = features.shape[-1]
    return pl.pallas_call(
        stats_kernel,
        out_shape=jax.ShapeDtypeStruct((peers, SUB, LANES), F32),
        in_specs=[vmem()],
        out_specs=vmem(),
        scratch_shapes=[pltpu.VMEM((STAT_ROWS, channels), F32)] * 2,
        compiler_params=params(),
        name="stats",
    )(features)


def lane_masks(shape, across):
    lane = iota(shape, 1)
    return lane % across, (lane // across) % 2


def roll(v, shift):
    return pltpu.roll(v, shift % v.shape[1], 1)


def conv_kernel(
    across, members, st_ref, f_ref, gain_ref, bias_ref, k_ref,
    lat_ref, up_ref, down_ref, mean_ref, inv_ref, act,
):
    images, cells, channels = f_ref.shape
    per_group = channels // GROUPS
    total = unpack_stats(jnp.sum(st_ref[...], axis=0))
    mean = nn(total, from_groups(channels, per_group, 0), HIGH) * (1.0 / members)
    square = nn(total, from_groups(channels, per_group, GROUPS), HIGH) * (1.0 / members)
    inv = lax.rsqrt(jnp.maximum(square - mean * mean, 0.0) + EPS_NORM)
    mean_ref[...] = mean
    inv_ref[...] = inv
    gain, bias = gain_ref[...], bias_ref[...]
    for i in range(images):
        v = f_ref[i].astype(F32)
        shifted = (v - mean[i : i + 1]) * inv[i : i + 1] * gain + bias
        act[i * cells : (i + 1) * cells, :] = (shifted * sigmoid(shifted)).astype(BF16)
    taps = nt(k_ref[...], act[...])
    shape = (SUB, images * cells)
    col, row = lane_masks(shape, across)

    def tap(position):
        return taps[position * SUB : (position + 1) * SUB]

    def line(dy):
        low = jnp.where(col > 0, roll(tap(3 * dy), 1), 0.0)
        high = jnp.where(col < across - 1, roll(tap(3 * dy + 2), -1), 0.0)
        return tap(3 * dy + 1) + low + high

    first, middle, last = line(0), line(1), line(2)
    last_up, first_down = roll(last, -across), roll(first, across)
    lat_ref[...] = middle + jnp.where(row == 0, last_up, first_down)
    up_ref[...] = jnp.where(row == 1, roll(last, across), 0.0)
    down_ref[...] = jnp.where(row == 0, roll(first, -across), 0.0)


def conv_forward(stats, features, gain, bias, kernel_rows, across, members):
    images, cells, channels = features.shape
    line = jax.ShapeDtypeStruct((SUB, images * cells), F32)
    stat = jax.ShapeDtypeStruct((STAT_ROWS, channels), F32)
    return pl.pallas_call(
        lambda *refs: conv_kernel(across, members, *refs),
        out_shape=(line, line, line, stat, stat),
        in_specs=[vmem()] * 5,
        out_specs=(vmem(),) * 5,
        scratch_shapes=[pltpu.VMEM((images * cells, channels), BF16)],
        compiler_params=params(),
        cost_estimate=pl.CostEstimate(
            flops=CONV_COST, bytes_accessed=features.size * 2, transcendentals=features.size
        ),
        name="conv",
    )(stats, features, gain, bias, kernel_rows)


def mlp_kernel(
    across, width, hidden, align, at_ref, lat_ref, below_ref, above_ref, target_ref,
    ew_ref, eb_ref, pib_ref, pob_ref,
    own, cross, own_other, cross_other,
    embed_ref, gl_ref, w_in, w_out, pre, emb, acc, grad_emb, sems,
):
    zhi, core = at_ref[0], at_ref[1]
    depth = width // (XS * ZHI * CORES)
    slab = hidden // (XS * ZHI * CORES)
    taken = PATCH * PATCH
    rows = taken * SUB
    copies = []

    def place(piece, at, shard, size):
        lines = pl.ds(at, size)

        def put(columns, into):
            copy = pltpu.make_async_copy(piece.at[lines, columns], into, sems.at[len(copies)])
            copy.start()
            copies.append(copy)

        line = pl.multiple_of(shard * depth, size)
        put(pl.ds(0, hidden), w_in.at[pl.ds(line, size), :])
        for part in range(slab // depth):
            line = pl.multiple_of(shard * slab + part * depth, size)
            put(pl.ds(hidden + part * align, align), w_out.at[pl.ds(line, size), :])

    for near, far, of_core in ((own, cross, core), (own_other, cross_other, 1 - core)):
        for x in range(XS):
            shard = x * (ZHI * CORES) + of_core
            for piece, of_zhi in ((near, zhi), (far, 1 - zhi)):
                place(piece, x * depth, shard + of_zhi * CORES, depth)

    lat = lat_ref[...] + below_ref[...] + above_ref[...]
    top = lat.astype(BF16)
    rest = lat - top.astype(F32)
    mid = rest.astype(BF16)
    low_part = (rest - mid.astype(F32)).astype(BF16)
    split = jnp.concatenate(
        [top.astype(F32), mid.astype(F32), low_part.astype(F32)], axis=0
    ).astype(BF16)
    cells = lat.shape[1]
    tokens = target_ref.shape[0]
    room = 256
    cols = across // PATCH

    def selection(u, v):
        shape = (cells, room)
        token = iota(shape, 1)
        lane = (token // cols) * (PATCH * across) + u * across + (token % cols) * PATCH + v
        return jnp.where((lane == iota(shape, 0)) & (token < tokens), 1.0, 0.0).astype(BF16)

    picks = [selection(u, v) for u in range(PATCH) for v in range(PATCH)]
    lines = []
    for pick in picks:
        got = nn(split, pick)
        lines.append(got[0:SUB] + got[SUB : 2 * SUB] + got[2 * SUB :])
    patches_t = jnp.concatenate(lines, axis=0)
    patches = patches_t.T
    empty = jnp.zeros((SUB - LATENT, width), F32)
    spread = []
    for k in range(taken):
        spread += [ew_ref[k * LATENT : (k + 1) * LATENT, :], empty]
    ew_top, ew_low = parts(jnp.concatenate(spread, axis=0))
    p_top, p_low = parts(patches[:tokens])
    embedded = nn(p_top, ew_top) + nn(p_low, ew_top) + nn(p_top, ew_low)
    emb[...] = (embedded + eb_ref[...]).astype(BF16)

    for copy in copies:
        copy.wait()

    step = 512
    acc[...] = jnp.zeros_like(acc)

    @pl.loop(0, hidden // step)
    def _(tile):
        at = pl.ds(pl.multiple_of(tile * step, step), step)
        h = nn(emb[...], w_in[:, at]) + pib_ref[:, at]
        pre[:, at] = h
        acc[...] += nn((h * sigmoid(h)).astype(BF16), w_out[at, :])

    projected = acc[...] + pob_ref[...]
    target = target_ref[...].astype(F32)
    unit_target = target * lax.rsqrt(jnp.sum(target * target, axis=1, keepdims=True) + EPS_UNIT)
    inv_len = lax.rsqrt(jnp.sum(projected * projected, axis=1, keepdims=True) + EPS_UNIT)
    unit_proj = projected * inv_len
    cosine = jnp.sum(unit_proj * unit_target, axis=1, keepdims=True)
    grad_out = (-inv_len * (unit_target - cosine * unit_proj)).astype(BF16)
    grad_emb[...] = jnp.zeros_like(grad_emb)

    @pl.loop(0, hidden // step)
    def _(tile):
        at = pl.ds(pl.multiple_of(tile * step, step), step)
        back = nt(grad_out, w_out[at, :])
        h = pre[:, at]
        sig = sigmoid(h)
        grad_hidden = (back * (sig * (1.0 + h * (1.0 - sig)))).astype(BF16)
        grad_emb[0:tokens, :] += nt(grad_hidden, w_in[:, at])

    grad = grad_emb[...]
    g_top, g_low = parts(grad)
    t_top, t_low = parts(patches_t)
    both = nn(jnp.concatenate([t_top, t_low], axis=0), g_top)
    embed_ref[...] = both[:rows] + both[rows:] + nn(t_top, g_low)
    both = nt(jnp.concatenate([ew_top, ew_low], axis=0), g_top)
    grad_patch = both[:rows] + both[rows:] + nt(ew_top, g_low)
    total = jnp.zeros((SUB, cells), F32)
    for position, pick in enumerate(picks):
        part = grad_patch[position * SUB : (position + 1) * SUB].astype(BF16)
        total = total + nt(part, pick)
    gl_ref[...] = total


def projector(at, lat, below, above, target, ew, eb, pib, pob, pieces, across):
    rows, width = PATCH * PATCH * SUB, ew.shape[1]
    hidden, align = pib.shape[1], pob.shape[1]
    tokens = target.shape[0]
    flops = 2 * tokens * (2 * width * hidden + 2 * hidden * align)
    return pl.pallas_call(
        lambda *refs: mlp_kernel(across, width, hidden, align, *refs),
        out_shape=(
            jax.ShapeDtypeStruct((rows, width), F32),
            jax.ShapeDtypeStruct(lat.shape, F32),
        ),
        in_specs=[pl.BlockSpec(memory_space=pltpu.SMEM)]
        + [vmem()] * 8
        + [pl.BlockSpec(memory_space=pltpu.HBM)] * len(pieces),
        out_specs=(vmem(), vmem()),
        scratch_shapes=[
            pltpu.VMEM((width, hidden), BF16),
            pltpu.VMEM((hidden, align), BF16),
            pltpu.VMEM((tokens, hidden), F32),
            pltpu.VMEM((tokens, width), BF16),
            pltpu.VMEM((tokens, align), F32),
            pltpu.VMEM((256, width), F32),
            pltpu.SemaphoreType.DMA((48,)),
        ],
        compiler_params=params(32),
        cost_estimate=pl.CostEstimate(
            flops=flops, bytes_accessed=8 << 20, transcendentals=2 * tokens * hidden
        ),
        name="projector",
    )(at, lat, below, above, target, ew, eb, pib, pob, *pieces)


def back_kernel(
    across, gl_ref, before_ref, after_ref, f_ref, mean_ref, inv_ref, gain_ref, bias_ref,
    k_ref, embed_ref, send_ref, gs_ref, act, grads_t, by_bias, by_gain, pack,
):
    images, cells, channels = f_ref.shape
    per_group = channels // GROUPS
    gl, before, after = gl_ref[...], before_ref[...], after_ref[...]
    col, row = lane_masks(gl.shape, across)
    lines = (
        jnp.where(row == 0, roll(gl, -across), roll(after, across)),
        gl,
        jnp.where(row == 0, roll(before, -across), roll(gl, across)),
    )
    parts = []
    for g in lines:
        parts.append(jnp.where(col < across - 1, roll(g, -1), 0.0))
        parts.append(g)
        parts.append(jnp.where(col > 0, roll(g, 1), 0.0))
    parts.append(jnp.zeros((LANES - TAPS * SUB, gl.shape[1]), F32))
    grads = jnp.concatenate(parts, axis=0)
    grads_t[...] = grads.T.astype(BF16)
    gain, bias = gain_ref[...], bias_ref[...]
    by_bias[...] = jnp.zeros_like(by_bias)
    by_gain[...] = jnp.zeros_like(by_gain)
    for i in range(images):
        at = slice(i * cells, (i + 1) * cells)
        v = f_ref[i].astype(F32)
        normed = (v - mean_ref[i : i + 1, :]) * inv_ref[i : i + 1, :]
        shifted = normed * gain + bias
        sig = sigmoid(shifted)
        act[at, :] = (shifted * sig).astype(BF16)
        grad_active = nn(grads_t[at, :], k_ref[...])
        gs = grad_active * (sig * (1.0 + shifted * (1.0 - sig)))
        gs_ref[i] = gs
        by_bias[i : i + 1, :] = jnp.sum(gs, axis=0, keepdims=True)
        by_gain[i : i + 1, :] = jnp.sum(gs * normed, axis=0, keepdims=True)
    conv = nn(grads.astype(BF16), act[...])
    stat = nn(by_bias[...] * gain, to_groups(channels, per_group, 0), HIGH) + nn(
        by_gain[...] * gain, to_groups(channels, per_group, GROUPS), HIGH
    )
    bias_part = jnp.sum(by_bias[...], axis=0, keepdims=True)
    gain_part = jnp.sum(by_gain[...], axis=0, keepdims=True)
    packed = halves(pack_stats(stat))
    for r in range(CHUNKS):
        send_ref[r, CHUNK_ROWS:ALL_ROWS, :] = packed
    blocks = channels // LANES
    half = CHUNKS // 2
    pack[...] = jnp.zeros_like(pack)
    for r in range(half):
        block, latent = r // LATENT, r % LATENT
        lanes = slice(block * LANES, (block + 1) * LANES)
        for position in range(TAPS):
            line = position * SUB + latent
            pack[r, position : position + 1, :] = conv[line : line + 1, lanes]
        lanes = slice((r // 2) * LANES, (r // 2 + 1) * LANES)
        for part in range(2):
            line = (r % 2) * 2 * SUB + part * SUB
            pack[half + r, part * LATENT : (part + 1) * LATENT, :] = embed_ref[
                line : line + LATENT, lanes
            ]
        if r < 2 * blocks:
            one = gain_part if r < blocks else bias_part
            lanes = slice((r % blocks) * LANES, (r % blocks + 1) * LANES)
            pack[half + r, SUB : SUB + 1, :] = one[:, lanes]
    for r in range(CHUNKS):
        send_ref[r, 0:CHUNK_ROWS, :] = pack[r].astype(BF16)


def conv_backward(gl, before, after, features, mean, inv, gain, bias, kernel_rows, embed, across):
    images, cells, channels = features.shape
    return pl.pallas_call(
        lambda *refs: back_kernel(across, *refs),
        out_shape=(
            jax.ShapeDtypeStruct((CHUNKS, ALL_ROWS, LANES), BF16),
            jax.ShapeDtypeStruct((images, cells, channels), F32),
        ),
        in_specs=[vmem()] * 10,
        out_specs=(vmem(),) * 2,
        scratch_shapes=[
            pltpu.VMEM((images * cells, channels), BF16),
            pltpu.VMEM((images * cells, LANES), BF16),
            pltpu.VMEM((STAT_ROWS, channels), F32),
            pltpu.VMEM((STAT_ROWS, channels), F32),
            pltpu.VMEM((CHUNKS, CHUNK_ROWS, LANES), F32),
        ],
        compiler_params=params(),
        name="back",
    )(gl, before, after, features, mean, inv, gain, bias, kernel_rows, embed)


def last_kernel(members, got_ref, f_ref, mean_ref, inv_ref, gain_ref, gs_ref, out_ref):
    images, _, channels = f_ref.shape
    per_group = channels // GROUPS
    total = unpack_stats(got_ref[...])
    first = nn(total, from_groups(channels, per_group, 0), HIGH) * (1.0 / members)
    second = nn(total, from_groups(channels, per_group, GROUPS), HIGH) * (1.0 / members)
    gain = gain_ref[...]
    for i in range(images):
        v = f_ref[i].astype(F32)
        inv = inv_ref[i : i + 1, :]
        normed = (v - mean_ref[i : i + 1, :]) * inv
        out = inv * (gs_ref[i] * gain - first[i : i + 1] - normed * second[i : i + 1])
        out_ref[i] = out.astype(BF16)


def feature_grad(got, features, mean, inv, gain, grad_shift, members):
    return pl.pallas_call(
        lambda *refs: last_kernel(members, *refs),
        out_shape=jax.ShapeDtypeStruct(features.shape, BF16),
        in_specs=[vmem()] * 6,
        out_specs=vmem(),
        compiler_params=params(),
        cost_estimate=pl.CostEstimate(
            flops=10 * features.size, bytes_accessed=8 * features.size, transcendentals=0
        ),
        name="last",
    )(got, features, mean, inv, gain, grad_shift)


def plane_kernel(at_ref, got_ref, out_ref):
    chunk = jnp.zeros((CHUNK_ROWS, LANES), F32)
    stat = jnp.zeros((SUB, LANES), F32)
    for r in range(CHUNKS):
        chunk = chunk + got_ref[r, 0:CHUNK_ROWS, :].astype(F32)
        pair = got_ref[r, CHUNK_ROWS:ALL_ROWS, :].astype(F32)
        stat = stat + jnp.where(at_ref[2] == (r // CORES) % YS, pair[:SUB] + pair[SUB:], 0.0)
    chunk, stat = chunk.astype(BF16), halves(stat)
    for r in range(out_ref.shape[0]):
        out_ref[r, 0:CHUNK_ROWS, :] = chunk
        out_ref[r, CHUNK_ROWS:ALL_ROWS, :] = stat


def plane_total(at, got):
    return pl.pallas_call(
        plane_kernel,
        out_shape=jax.ShapeDtypeStruct((ZHI * ZLO, ALL_ROWS, LANES), BF16),
        in_specs=[pl.BlockSpec(memory_space=pltpu.SMEM), vmem()],
        out_specs=vmem(),
        compiler_params=params(),
        name="plane",
    )(at, got)


def column_kernel(at_ref, got_ref, out_ref, stat_ref):
    chunk = jnp.zeros((CHUNK_ROWS, LANES), F32)
    stat = jnp.zeros((SUB, LANES), F32)
    for r in range(ZHI * ZLO):
        chunk = chunk + got_ref[r, 0:CHUNK_ROWS, :].astype(F32)
        pair = got_ref[r, CHUNK_ROWS:ALL_ROWS, :].astype(F32)
        stat = stat + jnp.where(at_ref[3] == r % ZLO, pair[:SUB] + pair[SUB:], 0.0)
    chunk = chunk.astype(BF16)
    for r in range(out_ref.shape[0]):
        out_ref[r] = chunk
    stat_ref[...] = stat


def column_total(at, got):
    return pl.pallas_call(
        column_kernel,
        out_shape=(
            jax.ShapeDtypeStruct((CHUNKS, CHUNK_ROWS, LANES), BF16),
            jax.ShapeDtypeStruct((SUB, LANES), F32),
        ),
        in_specs=[pl.BlockSpec(memory_space=pltpu.SMEM), vmem()],
        out_specs=(vmem(), vmem()),
        compiler_params=params(),
        name="column",
    )(at, got)


def unpack_kernel(got_ref, conv_ref, gain_ref, bias_ref, embed_ref, wide):
    channels = gain_ref.shape[1]
    blocks = channels // LANES
    half = CHUNKS // 2
    wide[...] = got_ref[...].astype(F32)
    for r in range(half):
        block, latent = r // LATENT, r % LATENT
        for position in range(TAPS):
            at = position * channels + block * LANES
            conv_ref[latent : latent + 1, at : at + LANES] = wide[r, position : position + 1, :]
        lanes = slice((r // 2) * LANES, (r // 2 + 1) * LANES)
        line = (r % 2) * SUB
        embed_ref[line : line + SUB, lanes] = wide[half + r, 0:SUB, :]
        lanes = slice((r % blocks) * LANES, (r % blocks + 1) * LANES)
        if r < blocks:
            gain_ref[:, lanes] = wide[half + r, SUB : SUB + 1, :]
        elif r < 2 * blocks:
            bias_ref[:, lanes] = wide[half + r, SUB : SUB + 1, :]


def unpack(got, channels, width):
    return pl.pallas_call(
        unpack_kernel,
        out_shape=(
            jax.ShapeDtypeStruct((LATENT, TAPS * channels), F32),
            jax.ShapeDtypeStruct((1, channels), F32),
            jax.ShapeDtypeStruct((1, channels), F32),
            jax.ShapeDtypeStruct((PATCH * PATCH * LATENT, width), F32),
        ),
        in_specs=[vmem()],
        out_specs=(vmem(),) * 4,
        scratch_shapes=[pltpu.VMEM(got.shape, F32)],
        compiler_params=params(),
        name="unpack",
    )(got)


def device(x, zhi, core, zlo, y):
    return ((x * ZHI + zhi) * CORES + core) * (ZLO * YS) + zlo * YS + y


BOTH = ("rows", "batch")
PLANE = [
    [device(x, h, c, d, y) for x in range(XS) for y in range(YS) for c in range(CORES)]
    for h in range(ZHI)
    for d in range(ZLO)
]
ALONG_X = [
    [device(x, h, c, d, y) for x in range(XS)]
    for h in range(ZHI)
    for c in range(CORES)
    for d in range(ZLO)
    for y in range(YS)
]
ALONG_PAIR = [
    [device(x, h, c, d, 2 * p + k) for x in range(XS) for k in range(2)]
    for h in range(ZHI)
    for c in range(CORES)
    for d in range(ZLO)
    for p in range(YS // 2)
]
COLUMN = [
    [device(x, h, c, d, y) for h in range(ZHI) for d in range(ZLO)]
    for x in range(XS)
    for y in range(YS)
    for c in range(CORES)
]


def exchanged(value, groups):
    return lax.all_to_all(value, BOTH, 0, 0, axis_index_groups=groups, tiled=True)


def moved(value, where):
    pairs = []
    for x in range(XS):
        for zhi in range(ZHI):
            for core in range(CORES):
                for zlo in range(ZLO):
                    for y in range(YS):
                        a, b, c, d, e = where(x, zhi, core, zlo, y)
                        pairs.append((device(x, zhi, core, zlo, y), device(a, b, c, d, e)))
    return lax.ppermute(value, ("rows", "batch"), pairs)


def shard_kernel(at_ref, in_ref, out_ref, shard_ref, half_ref):
    depth, hidden = in_ref.shape
    align = out_ref.shape[1]
    shard_ref[:, 0:hidden] = in_ref[...]
    for part in range(out_ref.shape[0] // depth):
        shard_ref[:, hidden + part * align : hidden + (part + 1) * align] = out_ref[
            part * depth : (part + 1) * depth, :
        ]
    size = half_ref.shape[0]
    begin = pl.multiple_of(lax.rem(at_ref[2], 2) * size, size)
    half_ref[...] = shard_ref[pl.ds(begin, size), :]


def shard_of(at, proj_in, proj_out):
    depth, hidden = proj_in.shape
    columns = hidden + proj_out.size // depth
    return pl.pallas_call(
        shard_kernel,
        out_shape=(
            jax.ShapeDtypeStruct((depth, columns), BF16),
            jax.ShapeDtypeStruct((depth // 2, columns), BF16),
        ),
        in_specs=[pl.BlockSpec(memory_space=pltpu.SMEM), vmem(), vmem()],
        out_specs=(vmem(), vmem()),
        compiler_params=params(),
        name="shard",
    )(at, proj_in, proj_out)


def crossed(half):
    return moved(half, lambda x, h, c, d, y: (x, 1 - h, c, ZLO - 1 - d, y))


def gathered(part, groups):
    return lax.all_gather(part, BOTH, axis_index_groups=groups, tiled=True)


def swapped(value):
    return moved(value, lambda x, h, c, d, y: (x, h, 1 - c, d, y))


def neighbours(up, down):
    count = lax.axis_size("rows")
    forward = [(i, i + 1) for i in range(count - 1)]
    backward = [(b, a) for a, b in forward]
    return lax.ppermute(up, "rows", backward), lax.ppermute(down, "rows", forward)


def shards(
    features,
    norm_gain,
    norm_bias,
    conv_weight,
    embed_weight,
    embed_bias,
    proj_in,
    proj_in_bias,
    proj_out,
    proj_out_bias,
    targets,
):
    images, height, across, channels = features.shape
    width, align = embed_weight.shape[1], proj_out.shape[1]
    peers = lax.axis_size("rows")
    members = peers * height * across * (channels // GROUPS)
    flat = features.reshape(images, height * across, channels)
    gain, bias = norm_gain.reshape(1, channels), norm_bias.reshape(1, channels)
    rows, batch = lax.axis_index("rows"), lax.axis_index("batch")
    at = jnp.stack([(rows // CORES) % ZHI, rows % CORES, batch % YS, batch // YS])
    at = at.astype(jnp.int32)
    shard, half = shard_of(at, proj_in, proj_out)
    own = gathered(shard, ALONG_X)
    taps = conv_weight.reshape(LATENT, TAPS, channels).transpose(1, 0, 2)
    taps = jnp.pad(taps, ((0, 0), (0, SUB - LATENT), (0, 0))).reshape(TAPS * SUB, channels)
    taps_full = jnp.pad(taps, ((0, LANES - TAPS * SUB), (0, 0)))

    sums = group_stats(flat, peers)
    stats = lax.all_to_all(sums, "rows", 0, 0, tiled=True)
    cross, stats = lax.optimization_barrier((crossed(half), stats))
    cross = jnp.broadcast_to(cross[None], (2 * XS, *cross.shape))
    cross = exchanged(cross, ALONG_PAIR).reshape(own.shape)
    lat, up, down, mean, inv = conv_forward(stats, flat, gain, bias, taps, across, members)
    above, below = neighbours(up, down)
    cross, own, above, below = lax.optimization_barrier((cross, own, above, below))
    pieces = [own, cross, swapped(own), swapped(cross)]
    target = targets.reshape(-1, align)
    embed_part, grad_lat = projector(
        at, lat, below, above, target, embed_weight, embed_bias.reshape(1, -1),
        proj_in_bias.reshape(1, -1), proj_out_bias.reshape(1, -1), pieces, across,
    )
    after, before = neighbours(grad_lat, grad_lat)
    send, grad_shift = conv_backward(
        grad_lat, before, after, flat, mean, inv, gain, bias, taps_full, embed_part, across
    )
    plane = exchanged(send, PLANE)
    column = exchanged(plane_total(at, plane), COLUMN)
    chunks, got = column_total(at, column)
    everything = exchanged(chunks, PLANE)
    grad_features = feature_grad(got, flat, mean, inv, gain, grad_shift, members)
    grad_conv, grad_gain, grad_bias, grad_embed = unpack(everything, channels, width)
    return (
        grad_features.reshape(features.shape),
        grad_conv,
        grad_gain.reshape(channels),
        grad_bias.reshape(channels),
        grad_embed,
    )


def solution(mesh):
    in_specs = (
        P("batch", "rows", None, None),
        P(),
        P(),
        P(),
        P(),
        P(),
        P("rows", None),
        P(),
        P("rows", None),
        P(),
        P("batch", "rows", None, None),
    )
    out_specs = (P("batch", "rows", None, None), P(), P(), P(), P())
    return jax.shard_map(shards, mesh=mesh, in_specs=in_specs, out_specs=out_specs, check_vma=False)
```

```python
import jax
import jax.numpy as jnp
from jax import lax
from jax.experimental import pallas as pl
from jax.experimental.pallas import tpu as pltpu
from jax.sharding import PartitionSpec as P

GROUPS = 32
LATENT = 4
PATCH = 2
EPS_NORM = 1e-06
EPS_UNIT = 1e-06

XS, ZHI, CORES, ZLO, YS = 4, 2, 2, 8, 4

HIGH = lax.Precision.HIGHEST
F32 = jnp.float32
BF16 = jnp.bfloat16
TAPS = 9
SUB = 8
LANES = 128
STAT_ROWS = 16
CHUNKS, CHUNK_ROWS, ALL_ROWS = 32, 16, 32
CONV_COST = 20_000_000_000
PART = 16


def params(limit_mb=12):
    return pltpu.CompilerParams(vmem_limit_bytes=limit_mb << 20)


def vmem():
    return pl.BlockSpec(memory_space=pltpu.VMEM)


def sigmoid(v):
    return 0.5 + 0.5 * jnp.tanh(0.5 * v)


def nt(a, b, precision=None):
    return lax.dot_general(
        a, b, (((1,), (1,)), ((), ())), preferred_element_type=F32, precision=precision
    )


def nn(a, b, precision=None):
    return lax.dot_general(
        a, b, (((1,), (0,)), ((), ())), preferred_element_type=F32, precision=precision
    )


def iota(shape, dim):
    return lax.broadcasted_iota(jnp.int32, shape, dim)


def to_groups(channels, per_group, offset):
    shape = (channels, LANES)
    return (iota(shape, 0) // per_group + offset == iota(shape, 1)).astype(F32)


def from_groups(channels, per_group, offset):
    shape = (LANES, channels)
    return (iota(shape, 1) // per_group + offset == iota(shape, 0)).astype(F32)


def pack_stats(total):
    lane = iota((SUB, LANES), 1)
    return jnp.where(lane < LANES // 2, total[:SUB], pltpu.roll(total[SUB:], LANES // 2, 1))


def unpack_stats(packed):
    return jnp.concatenate([packed, pltpu.roll(packed, LANES // 2, 1)], axis=0)


def parts(v):
    top = v.astype(BF16)
    return top, (v - top.astype(F32)).astype(BF16)


def halves(packed):
    top = packed.astype(BF16).astype(F32)
    return jnp.concatenate([top, packed - top], axis=0).astype(BF16)


def stats_kernel(f_ref, out_ref, sums, squares):
    images, _, channels = f_ref.shape
    sums[...] = jnp.zeros_like(sums)
    squares[...] = jnp.zeros_like(squares)
    for i in range(images):
        v = f_ref[i].astype(F32)
        sums[i : i + 1, :] = jnp.sum(v, axis=0, keepdims=True)
        squares[i : i + 1, :] = jnp.sum(v * v, axis=0, keepdims=True)
    per_group = channels // GROUPS
    total = nn(sums[...], to_groups(channels, per_group, 0), HIGH) + nn(
        squares[...], to_groups(channels, per_group, GROUPS), HIGH
    )
    packed = pack_stats(total)
    for r in range(out_ref.shape[0]):
        out_ref[r] = packed


def group_stats(features, peers):
    channels = features.shape[-1]
    return pl.pallas_call(
        stats_kernel,
        out_shape=jax.ShapeDtypeStruct((peers, SUB, LANES), F32),
        in_specs=[vmem()],
        out_specs=vmem(),
        scratch_shapes=[pltpu.VMEM((STAT_ROWS, channels), F32)] * 2,
        compiler_params=params(),
        name="stats",
    )(features)


def lane_masks(shape, across):
    lane = iota(shape, 1)
    return lane % across, (lane // across) % 2


def roll(v, shift):
    return pltpu.roll(v, shift % v.shape[1], 1)


def conv_kernel(
    across, members, st_ref, f_ref, gain_ref, bias_ref, k_ref,
    lat_ref, up_ref, down_ref, mean_ref, inv_ref, act,
):
    images, cells, channels = f_ref.shape
    per_group = channels // GROUPS
    total = unpack_stats(jnp.sum(st_ref[...], axis=0))
    mean = nn(total, from_groups(channels, per_group, 0), HIGH) * (1.0 / members)
    square = nn(total, from_groups(channels, per_group, GROUPS), HIGH) * (1.0 / members)
    inv = lax.rsqrt(jnp.maximum(square - mean * mean, 0.0) + EPS_NORM)
    mean_ref[...] = mean
    inv_ref[...] = inv
    gain, bias = gain_ref[...], bias_ref[...]
    for i in range(images):
        v = f_ref[i].astype(F32)
        shifted = (v - mean[i : i + 1]) * inv[i : i + 1] * gain + bias
        act[i * cells : (i + 1) * cells, :] = (shifted * sigmoid(shifted)).astype(BF16)
    taps = nt(k_ref[...], act[...])
    shape = (SUB, images * cells)
    col, row = lane_masks(shape, across)

    def tap(position):
        return taps[position * SUB : (position + 1) * SUB]

    def line(dy):
        low = jnp.where(col > 0, roll(tap(3 * dy), 1), 0.0)
        high = jnp.where(col < across - 1, roll(tap(3 * dy + 2), -1), 0.0)
        return tap(3 * dy + 1) + low + high

    first, middle, last = line(0), line(1), line(2)
    last_up, first_down = roll(last, -across), roll(first, across)
    lat_ref[...] = middle + jnp.where(row == 0, last_up, first_down)
    up_ref[...] = jnp.where(row == 1, roll(last, across), 0.0)
    down_ref[...] = jnp.where(row == 0, roll(first, -across), 0.0)


def conv_forward(stats, features, gain, bias, kernel_rows, across, members):
    images, cells, channels = features.shape
    line = jax.ShapeDtypeStruct((SUB, images * cells), F32)
    stat = jax.ShapeDtypeStruct((STAT_ROWS, channels), F32)
    return pl.pallas_call(
        lambda *refs: conv_kernel(across, members, *refs),
        out_shape=(line, line, line, stat, stat),
        in_specs=[vmem()] * 5,
        out_specs=(vmem(),) * 5,
        scratch_shapes=[pltpu.VMEM((images * cells, channels), BF16)],
        compiler_params=params(),
        cost_estimate=pl.CostEstimate(
            flops=CONV_COST, bytes_accessed=features.size * 2, transcendentals=features.size
        ),
        name="conv",
    )(stats, features, gain, bias, kernel_rows)


def mlp_kernel(
    across, width, hidden, align, at_ref, lat_ref, below_ref, above_ref, target_ref,
    ew_ref, eb_ref, pib_ref, pob_ref,
    own_near, own_far, cross, own_near_other, own_far_other, cross_other,
    embed_ref, gl_ref, w_in, w_out, pre, emb, acc, grad_emb, sems,
):
    zhi, core, x = at_ref[0], at_ref[1], at_ref[4]
    depth = width // (XS * ZHI * CORES)
    slab = hidden // (XS * ZHI * CORES)
    taken = PATCH * PATCH
    rows = taken * SUB
    copies = []

    def place(piece, at, source_x, of_zhi, of_core, begin=0, size=depth):
        shard = lax.rem(source_x, XS) * (ZHI * CORES) + of_zhi * CORES + of_core
        lines = pl.ds(at, size)

        def put(columns, into):
            copy = pltpu.make_async_copy(piece.at[lines, columns], into, sems.at[len(copies)])
            copy.start()
            copies.append(copy)

        line = pl.multiple_of(shard * depth + begin, size)
        put(pl.ds(0, hidden), w_in.at[pl.ds(line, size), :])
        for part in range(slab // depth):
            line = pl.multiple_of(shard * slab + part * depth + begin, size)
            put(pl.ds(hidden + part * align, align), w_out.at[pl.ds(line, size), :])

    half = depth // 2
    for near, opposite, far, of_core in (
        (own_near, own_far, cross, core),
        (own_near_other, own_far_other, cross_other, 1 - core),
    ):
        for k, step in enumerate((0, 1, XS - 1)):
            place(near, k * depth, x + step, zhi, of_core)
        for begin in (0, half):
            place(opposite, begin, x + 2, zhi, of_core, begin, half)
        for k in range(XS):
            place(far, k * depth, k, 1 - zhi, of_core)

    lat = lat_ref[...] + below_ref[...] + above_ref[...]
    top = lat.astype(BF16)
    rest = lat - top.astype(F32)
    mid = rest.astype(BF16)
    low_part = (rest - mid.astype(F32)).astype(BF16)
    split = jnp.concatenate(
        [top.astype(F32), mid.astype(F32), low_part.astype(F32)], axis=0
    ).astype(BF16)
    cells = lat.shape[1]
    tokens = target_ref.shape[0]
    room = 256
    cols = across // PATCH

    def selection(u, v):
        shape = (cells, room)
        token = iota(shape, 1)
        lane = (token // cols) * (PATCH * across) + u * across + (token % cols) * PATCH + v
        return jnp.where((lane == iota(shape, 0)) & (token < tokens), 1.0, 0.0).astype(BF16)

    picks = [selection(u, v) for u in range(PATCH) for v in range(PATCH)]
    lines = []
    for pick in picks:
        got = nn(split, pick)
        lines.append(got[0:SUB] + got[SUB : 2 * SUB] + got[2 * SUB :])
    patches_t = jnp.concatenate(lines, axis=0)
    patches = patches_t.T
    empty = jnp.zeros((SUB - LATENT, width), F32)
    spread = []
    for k in range(taken):
        spread += [ew_ref[k * LATENT : (k + 1) * LATENT, :], empty]
    ew_top, ew_low = parts(jnp.concatenate(spread, axis=0))
    p_top, p_low = parts(patches[:tokens])
    embedded = nn(p_top, ew_top) + nn(p_low, ew_top) + nn(p_top, ew_low)
    emb[...] = (embedded + eb_ref[...]).astype(BF16)

    for copy in copies:
        copy.wait()

    step = 512
    acc[...] = jnp.zeros_like(acc)

    @pl.loop(0, hidden // step)
    def _(tile):
        at = pl.ds(pl.multiple_of(tile * step, step), step)
        h = nn(emb[...], w_in[:, at]) + pib_ref[:, at]
        pre[:, at] = h
        acc[...] += nn((h * sigmoid(h)).astype(BF16), w_out[at, :])

    projected = acc[...] + pob_ref[...]
    target = target_ref[...].astype(F32)
    unit_target = target * lax.rsqrt(jnp.sum(target * target, axis=1, keepdims=True) + EPS_UNIT)
    inv_len = lax.rsqrt(jnp.sum(projected * projected, axis=1, keepdims=True) + EPS_UNIT)
    unit_proj = projected * inv_len
    cosine = jnp.sum(unit_proj * unit_target, axis=1, keepdims=True)
    grad_out = (-inv_len * (unit_target - cosine * unit_proj)).astype(BF16)
    grad_emb[...] = jnp.zeros_like(grad_emb)

    @pl.loop(0, hidden // step)
    def _(tile):
        at = pl.ds(pl.multiple_of(tile * step, step), step)
        back = nt(grad_out, w_out[at, :])
        h = pre[:, at]
        sig = sigmoid(h)
        grad_hidden = (back * (sig * (1.0 + h * (1.0 - sig)))).astype(BF16)
        grad_emb[0:tokens, :] += nt(grad_hidden, w_in[:, at])

    grad = grad_emb[...]
    g_top, g_low = parts(grad)
    t_top, t_low = parts(patches_t)
    both = nn(jnp.concatenate([t_top, t_low], axis=0), g_top)
    embed_ref[...] = both[:rows] + both[rows:] + nn(t_top, g_low)
    both = nt(jnp.concatenate([ew_top, ew_low], axis=0), g_top)
    grad_patch = both[:rows] + both[rows:] + nt(ew_top, g_low)
    total = jnp.zeros((SUB, cells), F32)
    for position, pick in enumerate(picks):
        part = grad_patch[position * SUB : (position + 1) * SUB].astype(BF16)
        total = total + nt(part, pick)
    gl_ref[...] = total


def projector(at, lat, below, above, target, ew, eb, pib, pob, pieces, across):
    rows, width = PATCH * PATCH * SUB, ew.shape[1]
    hidden, align = pib.shape[1], pob.shape[1]
    tokens = target.shape[0]
    flops = 2 * tokens * (2 * width * hidden + 2 * hidden * align)
    return pl.pallas_call(
        lambda *refs: mlp_kernel(across, width, hidden, align, *refs),
        out_shape=(
            jax.ShapeDtypeStruct((rows, width), F32),
            jax.ShapeDtypeStruct(lat.shape, F32),
        ),
        in_specs=[pl.BlockSpec(memory_space=pltpu.SMEM)]
        + [vmem()] * 8
        + [pl.BlockSpec(memory_space=pltpu.HBM)] * len(pieces),
        out_specs=(vmem(), vmem()),
        scratch_shapes=[
            pltpu.VMEM((width, hidden), BF16),
            pltpu.VMEM((hidden, align), BF16),
            pltpu.VMEM((tokens, hidden), F32),
            pltpu.VMEM((tokens, width), BF16),
            pltpu.VMEM((tokens, align), F32),
            pltpu.VMEM((256, width), F32),
            pltpu.SemaphoreType.DMA((54,)),
        ],
        compiler_params=params(32),
        cost_estimate=pl.CostEstimate(
            flops=flops, bytes_accessed=8 << 20, transcendentals=2 * tokens * hidden
        ),
        name="projector",
    )(at, lat, below, above, target, ew, eb, pib, pob, *pieces)


def back_kernel(
    across, gl_ref, before_ref, after_ref, f_ref, mean_ref, inv_ref, gain_ref, bias_ref,
    k_ref, embed_ref, send_ref, gs_ref, act, grads_t, by_bias, by_gain, pack,
):
    images, cells, channels = f_ref.shape
    per_group = channels // GROUPS
    gl, before, after = gl_ref[...], before_ref[...], after_ref[...]
    col, row = lane_masks(gl.shape, across)
    lines = (
        jnp.where(row == 0, roll(gl, -across), roll(after, across)),
        gl,
        jnp.where(row == 0, roll(before, -across), roll(gl, across)),
    )
    parts = []
    for g in lines:
        parts.append(jnp.where(col < across - 1, roll(g, -1), 0.0))
        parts.append(g)
        parts.append(jnp.where(col > 0, roll(g, 1), 0.0))
    parts.append(jnp.zeros((LANES - TAPS * SUB, gl.shape[1]), F32))
    grads = jnp.concatenate(parts, axis=0)
    grads_t[...] = grads.T.astype(BF16)
    gain, bias = gain_ref[...], bias_ref[...]
    by_bias[...] = jnp.zeros_like(by_bias)
    by_gain[...] = jnp.zeros_like(by_gain)
    for i in range(images):
        at = slice(i * cells, (i + 1) * cells)
        v = f_ref[i].astype(F32)
        normed = (v - mean_ref[i : i + 1, :]) * inv_ref[i : i + 1, :]
        shifted = normed * gain + bias
        sig = sigmoid(shifted)
        act[at, :] = (shifted * sig).astype(BF16)
        grad_active = nn(grads_t[at, :], k_ref[...])
        gs = grad_active * (sig * (1.0 + shifted * (1.0 - sig)))
        gs_ref[i] = gs
        by_bias[i : i + 1, :] = jnp.sum(gs, axis=0, keepdims=True)
        by_gain[i : i + 1, :] = jnp.sum(gs * normed, axis=0, keepdims=True)
    conv = nn(grads.astype(BF16), act[...])
    stat = nn(by_bias[...] * gain, to_groups(channels, per_group, 0), HIGH) + nn(
        by_gain[...] * gain, to_groups(channels, per_group, GROUPS), HIGH
    )
    bias_part = jnp.sum(by_bias[...], axis=0, keepdims=True)
    gain_part = jnp.sum(by_gain[...], axis=0, keepdims=True)
    packed = halves(pack_stats(stat))
    for r in range(CHUNKS):
        send_ref[r, CHUNK_ROWS:ALL_ROWS, :] = packed
    blocks = channels // LANES
    half = CHUNKS // 2
    pack[...] = jnp.zeros_like(pack)
    for r in range(half):
        block, latent = r // LATENT, r % LATENT
        lanes = slice(block * LANES, (block + 1) * LANES)
        for position in range(TAPS):
            line = position * SUB + latent
            pack[r, position : position + 1, :] = conv[line : line + 1, lanes]
        lanes = slice((r // 2) * LANES, (r // 2 + 1) * LANES)
        for part in range(2):
            line = (r % 2) * 2 * SUB + part * SUB
            pack[half + r, part * LATENT : (part + 1) * LATENT, :] = embed_ref[
                line : line + LATENT, lanes
            ]
        if r < 2 * blocks:
            one = gain_part if r < blocks else bias_part
            lanes = slice((r % blocks) * LANES, (r % blocks + 1) * LANES)
            pack[half + r, SUB : SUB + 1, :] = one[:, lanes]
    for r in range(CHUNKS):
        send_ref[r, 0:CHUNK_ROWS, :] = pack[r].astype(BF16)


def conv_backward(gl, before, after, features, mean, inv, gain, bias, kernel_rows, embed, across):
    images, cells, channels = features.shape
    return pl.pallas_call(
        lambda *refs: back_kernel(across, *refs),
        out_shape=(
            jax.ShapeDtypeStruct((CHUNKS, ALL_ROWS, LANES), BF16),
            jax.ShapeDtypeStruct((images, cells, channels), F32),
        ),
        in_specs=[vmem()] * 10,
        out_specs=(vmem(),) * 2,
        scratch_shapes=[
            pltpu.VMEM((images * cells, channels), BF16),
            pltpu.VMEM((images * cells, LANES), BF16),
            pltpu.VMEM((STAT_ROWS, channels), F32),
            pltpu.VMEM((STAT_ROWS, channels), F32),
            pltpu.VMEM((CHUNKS, CHUNK_ROWS, LANES), F32),
        ],
        compiler_params=params(),
        name="back",
    )(gl, before, after, features, mean, inv, gain, bias, kernel_rows, embed)


def last_kernel(members, got_ref, f_ref, mean_ref, inv_ref, gain_ref, gs_ref, out_ref):
    images, _, channels = f_ref.shape
    per_group = channels // GROUPS
    total = unpack_stats(got_ref[...])
    first = nn(total, from_groups(channels, per_group, 0), HIGH) * (1.0 / members)
    second = nn(total, from_groups(channels, per_group, GROUPS), HIGH) * (1.0 / members)
    gain = gain_ref[...]
    for i in range(images):
        v = f_ref[i].astype(F32)
        inv = inv_ref[i : i + 1, :]
        normed = (v - mean_ref[i : i + 1, :]) * inv
        out = inv * (gs_ref[i] * gain - first[i : i + 1] - normed * second[i : i + 1])
        out_ref[i] = out.astype(BF16)


def feature_grad(got, features, mean, inv, gain, grad_shift, members):
    return pl.pallas_call(
        lambda *refs: last_kernel(members, *refs),
        out_shape=jax.ShapeDtypeStruct(features.shape, BF16),
        in_specs=[vmem()] * 6,
        out_specs=vmem(),
        compiler_params=params(),
        cost_estimate=pl.CostEstimate(
            flops=10 * features.size, bytes_accessed=8 * features.size, transcendentals=0
        ),
        name="last",
    )(got, features, mean, inv, gain, grad_shift)


def plane_kernel(at_ref, got_ref, out_ref):
    chunk = jnp.zeros((CHUNK_ROWS, LANES), F32)
    stat = jnp.zeros((SUB, LANES), F32)
    for r in range(CHUNKS):
        chunk = chunk + got_ref[r, 0:CHUNK_ROWS, :].astype(F32)
        pair = got_ref[r, CHUNK_ROWS:ALL_ROWS, :].astype(F32)
        stat = stat + jnp.where(at_ref[2] == (r // CORES) % YS, pair[:SUB] + pair[SUB:], 0.0)
    chunk, stat = chunk.astype(BF16), halves(stat)
    for r in range(out_ref.shape[0]):
        out_ref[r, 0:CHUNK_ROWS, :] = chunk
        out_ref[r, CHUNK_ROWS:ALL_ROWS, :] = stat


def plane_total(at, got):
    return pl.pallas_call(
        plane_kernel,
        out_shape=jax.ShapeDtypeStruct((ZHI * ZLO, ALL_ROWS, LANES), BF16),
        in_specs=[pl.BlockSpec(memory_space=pltpu.SMEM), vmem()],
        out_specs=vmem(),
        compiler_params=params(),
        name="plane",
    )(at, got)


def column_kernel(at_ref, got_ref, out_ref, stat_ref):
    chunk = jnp.zeros((CHUNK_ROWS, LANES), F32)
    stat = jnp.zeros((SUB, LANES), F32)
    for r in range(ZHI * ZLO):
        chunk = chunk + got_ref[r, 0:CHUNK_ROWS, :].astype(F32)
        pair = got_ref[r, CHUNK_ROWS:ALL_ROWS, :].astype(F32)
        stat = stat + jnp.where(at_ref[3] == r % ZLO, pair[:SUB] + pair[SUB:], 0.0)
    chunk = chunk.astype(BF16)
    for r in range(out_ref.shape[0]):
        out_ref[r] = chunk
    stat_ref[...] = stat


def column_total(at, got):
    return pl.pallas_call(
        column_kernel,
        out_shape=(
            jax.ShapeDtypeStruct((CHUNKS, CHUNK_ROWS, LANES), BF16),
            jax.ShapeDtypeStruct((SUB, LANES), F32),
        ),
        in_specs=[pl.BlockSpec(memory_space=pltpu.SMEM), vmem()],
        out_specs=(vmem(), vmem()),
        compiler_params=params(),
        name="column",
    )(at, got)


def unpack_kernel(got_ref, conv_ref, gain_ref, bias_ref, embed_ref, wide):
    channels = gain_ref.shape[1]
    blocks = channels // LANES
    half = CHUNKS // 2
    wide[...] = got_ref[...].astype(F32)
    for r in range(half):
        block, latent = r // LATENT, r % LATENT
        for position in range(TAPS):
            at = position * channels + block * LANES
            conv_ref[latent : latent + 1, at : at + LANES] = wide[r, position : position + 1, :]
        lanes = slice((r // 2) * LANES, (r // 2 + 1) * LANES)
        line = (r % 2) * SUB
        embed_ref[line : line + SUB, lanes] = wide[half + r, 0:SUB, :]
        lanes = slice((r % blocks) * LANES, (r % blocks + 1) * LANES)
        if r < blocks:
            gain_ref[:, lanes] = wide[half + r, SUB : SUB + 1, :]
        elif r < 2 * blocks:
            bias_ref[:, lanes] = wide[half + r, SUB : SUB + 1, :]


def unpack(got, channels, width):
    return pl.pallas_call(
        unpack_kernel,
        out_shape=(
            jax.ShapeDtypeStruct((LATENT, TAPS * channels), F32),
            jax.ShapeDtypeStruct((1, channels), F32),
            jax.ShapeDtypeStruct((1, channels), F32),
            jax.ShapeDtypeStruct((PATCH * PATCH * LATENT, width), F32),
        ),
        in_specs=[vmem()],
        out_specs=(vmem(),) * 4,
        scratch_shapes=[pltpu.VMEM(got.shape, F32)],
        compiler_params=params(),
        name="unpack",
    )(got)


def device(x, zhi, core, zlo, y):
    return ((x * ZHI + zhi) * CORES + core) * (ZLO * YS) + zlo * YS + y


BOTH = ("rows", "batch")
PLANE = [
    [device(x, h, c, d, y) for x in range(XS) for y in range(YS) for c in range(CORES)]
    for h in range(ZHI)
    for d in range(ZLO)
]
SHEET = [
    [device(x, h, c, d, y) for x in range(XS) for y in range(YS)]
    for h in range(ZHI)
    for d in range(ZLO)
    for c in range(CORES)
]
COLUMN = [
    [device(x, h, c, d, y) for h in range(ZHI) for d in range(ZLO)]
    for x in range(XS)
    for y in range(YS)
    for c in range(CORES)
]


def exchanged(value, groups):
    return lax.all_to_all(value, BOTH, 0, 0, axis_index_groups=groups, tiled=True)


def moved(value, where):
    pairs = []
    for x in range(XS):
        for zhi in range(ZHI):
            for core in range(CORES):
                for zlo in range(ZLO):
                    for y in range(YS):
                        a, b, c, d, e = where(x, zhi, core, zlo, y)
                        pairs.append((device(x, zhi, core, zlo, y), device(a, b, c, d, e)))
    return lax.ppermute(value, ("rows", "batch"), pairs)


def shard_kernel(at_ref, in_ref, out_ref, shard_ref, part_ref):
    depth, hidden = in_ref.shape
    align = out_ref.shape[1]
    shard_ref[:, 0:hidden] = in_ref[...]
    for part in range(out_ref.shape[0] // depth):
        shard_ref[:, hidden + part * align : hidden + (part + 1) * align] = out_ref[
            part * depth : (part + 1) * depth, :
        ]
    size = part_ref.shape[0]
    begin = pl.multiple_of(at_ref[2] * size, size)
    part_ref[...] = shard_ref[pl.ds(begin, size), :]


def shard_of(at, proj_in, proj_out):
    depth, hidden = proj_in.shape
    columns = hidden + proj_out.size // depth
    return pl.pallas_call(
        shard_kernel,
        out_shape=(
            jax.ShapeDtypeStruct((depth, columns), BF16),
            jax.ShapeDtypeStruct((depth // YS, columns), BF16),
        ),
        in_specs=[pl.BlockSpec(memory_space=pltpu.SMEM), vmem(), vmem()],
        out_specs=(vmem(), vmem()),
        compiler_params=params(),
        name="shard",
    )(at, proj_in, proj_out)


def crossed(part):
    return moved(part, lambda x, h, c, d, y: (x, 1 - h, c, ZLO - 1 - d, y))


def from_next(value):
    return moved(value, lambda x, h, c, d, y: ((x + XS - 1) % XS, h, c, d, y))


def from_last(value):
    return moved(value, lambda x, h, c, d, y: ((x + 1) % XS, h, c, d, y))


def along_x(shard):
    half = shard.shape[0] // 2
    plus, minus = from_next(shard), from_last(shard)
    near = jnp.concatenate([shard, plus, minus], axis=0)
    opposite = jnp.concatenate([from_next(plus[:half]), from_last(minus[half:])], axis=0)
    return near, opposite


def swapped(value):
    return moved(value, lambda x, h, c, d, y: (x, h, 1 - c, d, y))


def neighbours(up, down):
    count = lax.axis_size("rows")
    forward = [(i, i + 1) for i in range(count - 1)]
    backward = [(b, a) for a, b in forward]
    return lax.ppermute(up, "rows", backward), lax.ppermute(down, "rows", forward)


def shards(
    features,
    norm_gain,
    norm_bias,
    conv_weight,
    embed_weight,
    embed_bias,
    proj_in,
    proj_in_bias,
    proj_out,
    proj_out_bias,
    targets,
):
    images, height, across, channels = features.shape
    width, align = embed_weight.shape[1], proj_out.shape[1]
    peers = lax.axis_size("rows")
    members = peers * height * across * (channels // GROUPS)
    flat = features.reshape(images, height * across, channels)
    gain, bias = norm_gain.reshape(1, channels), norm_bias.reshape(1, channels)
    rows, batch = lax.axis_index("rows"), lax.axis_index("batch")
    at = jnp.stack([(rows // CORES) % ZHI, rows % CORES, batch % YS, batch // YS, rows // (ZHI * CORES)])
    at = at.astype(jnp.int32)
    shard, part = shard_of(at, proj_in, proj_out)
    own_near, own_far = along_x(shard)
    taps = conv_weight.reshape(LATENT, TAPS, channels).transpose(1, 0, 2)
    taps = jnp.pad(taps, ((0, 0), (0, SUB - LATENT), (0, 0))).reshape(TAPS * SUB, channels)
    taps_full = jnp.pad(taps, ((0, LANES - TAPS * SUB), (0, 0)))

    sums = group_stats(flat, peers)
    stats = lax.all_to_all(sums, "rows", 0, 0, tiled=True)
    cross, stats = lax.optimization_barrier((crossed(part), stats))
    cross = jnp.broadcast_to(cross[None], (XS * YS, *cross.shape))
    cross = exchanged(cross, SHEET).reshape(-1, shard.shape[1])
    lat, up, down, mean, inv = conv_forward(stats, flat, gain, bias, taps, across, members)
    above, below = neighbours(up, down)
    cross, own_near, own_far, above, below = lax.optimization_barrier((cross, own_near, own_far, above, below))
    pieces = [own_near, own_far, cross]
    pieces = pieces + [swapped(v) for v in pieces]
    target = targets.reshape(-1, align)
    embed_part, grad_lat = projector(
        at, lat, below, above, target, embed_weight, embed_bias.reshape(1, -1),
        proj_in_bias.reshape(1, -1), proj_out_bias.reshape(1, -1), pieces, across,
    )
    after, before = neighbours(grad_lat, grad_lat)
    send, grad_shift = conv_backward(
        grad_lat, before, after, flat, mean, inv, gain, bias, taps_full, embed_part, across
    )
    plane = exchanged(send, PLANE)
    column = exchanged(plane_total(at, plane), COLUMN)
    chunks, got = column_total(at, column)
    everything = exchanged(chunks, PLANE)
    grad_features = feature_grad(got, flat, mean, inv, gain, grad_shift, members)
    grad_conv, grad_gain, grad_bias, grad_embed = unpack(everything, channels, width)
    return (
        grad_features.reshape(features.shape),
        grad_conv,
        grad_gain.reshape(channels),
        grad_bias.reshape(channels),
        grad_embed,
    )


def solution(mesh):
    in_specs = (
        P("batch", "rows", None, None),
        P(),
        P(),
        P(),
        P(),
        P(),
        P("rows", None),
        P(),
        P("rows", None),
        P(),
        P("batch", "rows", None, None),
    )
    out_specs = (P("batch", "rows", None, None), P(), P(), P(), P())
    return jax.shard_map(shards, mesh=mesh, in_specs=in_specs, out_specs=out_specs, check_vma=False)
```

```python
import jax
import jax.numpy as jnp
from jax import lax
from jax.experimental import pallas as pl
from jax.experimental.pallas import tpu as pltpu
from jax.sharding import PartitionSpec as P

GROUPS = 32
LATENT = 4
PATCH = 2
EPS_NORM = 1e-06
EPS_UNIT = 1e-06

XS, ZHI, CORES, ZLO, YS = 4, 2, 2, 8, 4

HIGH = lax.Precision.HIGHEST
F32 = jnp.float32
BF16 = jnp.bfloat16
TAPS = 9
SUB = 8
LANES = 128
STAT_ROWS = 16
CHUNKS, CHUNK_ROWS, ALL_ROWS = 32, 16, 32
CONV_COST = 20_000_000_000
PART = 16


def params(limit_mb=12):
    return pltpu.CompilerParams(vmem_limit_bytes=limit_mb << 20)


def vmem():
    return pl.BlockSpec(memory_space=pltpu.VMEM)


def sigmoid(v):
    return 0.5 + 0.5 * jnp.tanh(0.5 * v)


def nt(a, b, precision=None):
    return lax.dot_general(
        a, b, (((1,), (1,)), ((), ())), preferred_element_type=F32, precision=precision
    )


def nn(a, b, precision=None):
    return lax.dot_general(
        a, b, (((1,), (0,)), ((), ())), preferred_element_type=F32, precision=precision
    )


def iota(shape, dim):
    return lax.broadcasted_iota(jnp.int32, shape, dim)


def to_groups(channels, per_group, offset):
    shape = (channels, LANES)
    return (iota(shape, 0) // per_group + offset == iota(shape, 1)).astype(F32)


def from_groups(channels, per_group, offset):
    shape = (LANES, channels)
    return (iota(shape, 1) // per_group + offset == iota(shape, 0)).astype(F32)


def pack_stats(total):
    lane = iota((SUB, LANES), 1)
    return jnp.where(lane < LANES // 2, total[:SUB], pltpu.roll(total[SUB:], LANES // 2, 1))


def unpack_stats(packed):
    return jnp.concatenate([packed, pltpu.roll(packed, LANES // 2, 1)], axis=0)


def parts(v):
    top = v.astype(BF16)
    return top, (v - top.astype(F32)).astype(BF16)


def halves(packed):
    top = packed.astype(BF16).astype(F32)
    return jnp.concatenate([top, packed - top], axis=0).astype(BF16)


def stats_kernel(f_ref, out_ref, sums, squares):
    images, _, channels = f_ref.shape
    sums[...] = jnp.zeros_like(sums)
    squares[...] = jnp.zeros_like(squares)
    for i in range(images):
        v = f_ref[i].astype(F32)
        sums[i : i + 1, :] = jnp.sum(v, axis=0, keepdims=True)
        squares[i : i + 1, :] = jnp.sum(v * v, axis=0, keepdims=True)
    per_group = channels // GROUPS
    total = nn(sums[...], to_groups(channels, per_group, 0), HIGH) + nn(
        squares[...], to_groups(channels, per_group, GROUPS), HIGH
    )
    packed = pack_stats(total)
    for r in range(out_ref.shape[0]):
        out_ref[r] = packed


def group_stats(features, peers):
    channels = features.shape[-1]
    return pl.pallas_call(
        stats_kernel,
        out_shape=jax.ShapeDtypeStruct((peers, SUB, LANES), F32),
        in_specs=[vmem()],
        out_specs=vmem(),
        scratch_shapes=[pltpu.VMEM((STAT_ROWS, channels), F32)] * 2,
        compiler_params=params(),
        name="stats",
    )(features)


def lane_masks(shape, across):
    lane = iota(shape, 1)
    return lane % across, (lane // across) % 2


def roll(v, shift):
    return pltpu.roll(v, shift % v.shape[1], 1)


def conv_kernel(
    across, members, st_ref, f_ref, gain_ref, bias_ref, k_ref,
    lat_ref, up_ref, down_ref, mean_ref, inv_ref, act,
):
    images, cells, channels = f_ref.shape
    per_group = channels // GROUPS
    total = unpack_stats(jnp.sum(st_ref[...], axis=0))
    mean = nn(total, from_groups(channels, per_group, 0), HIGH) * (1.0 / members)
    square = nn(total, from_groups(channels, per_group, GROUPS), HIGH) * (1.0 / members)
    inv = lax.rsqrt(jnp.maximum(square - mean * mean, 0.0) + EPS_NORM)
    mean_ref[...] = mean
    inv_ref[...] = inv
    gain, bias = gain_ref[...], bias_ref[...]
    for i in range(images):
        v = f_ref[i].astype(F32)
        shifted = (v - mean[i : i + 1]) * inv[i : i + 1] * gain + bias
        act[i * cells : (i + 1) * cells, :] = (shifted * sigmoid(shifted)).astype(BF16)
    taps = nt(k_ref[...], act[...])
    shape = (SUB, images * cells)
    col, row = lane_masks(shape, across)

    def tap(position):
        return taps[position * SUB : (position + 1) * SUB]

    def line(dy):
        low = jnp.where(col > 0, roll(tap(3 * dy), 1), 0.0)
        high = jnp.where(col < across - 1, roll(tap(3 * dy + 2), -1), 0.0)
        return tap(3 * dy + 1) + low + high

    first, middle, last = line(0), line(1), line(2)
    last_up, first_down = roll(last, -across), roll(first, across)
    lat_ref[...] = middle + jnp.where(row == 0, last_up, first_down)
    up_ref[...] = jnp.where(row == 1, roll(last, across), 0.0)
    down_ref[...] = jnp.where(row == 0, roll(first, -across), 0.0)


def conv_forward(stats, features, gain, bias, kernel_rows, across, members):
    images, cells, channels = features.shape
    line = jax.ShapeDtypeStruct((SUB, images * cells), F32)
    stat = jax.ShapeDtypeStruct((STAT_ROWS, channels), F32)
    return pl.pallas_call(
        lambda *refs: conv_kernel(across, members, *refs),
        out_shape=(line, line, line, stat, stat),
        in_specs=[vmem()] * 5,
        out_specs=(vmem(),) * 5,
        scratch_shapes=[pltpu.VMEM((images * cells, channels), BF16)],
        compiler_params=params(),
        cost_estimate=pl.CostEstimate(
            flops=CONV_COST, bytes_accessed=features.size * 2, transcendentals=features.size
        ),
        name="conv",
    )(stats, features, gain, bias, kernel_rows)


def mlp_kernel(
    across, width, hidden, align, at_ref, lat_ref, below_ref, above_ref, target_ref,
    ew_ref, eb_ref, pib_ref, pob_ref,
    own_near, own_far, cross, own_near_other, own_far_other, cross_other,
    embed_ref, gl_ref, w_in, w_out, pre, emb, acc, grad_emb, sems,
):
    zhi, core, x = at_ref[0], at_ref[1], at_ref[4]
    depth = width // (XS * ZHI * CORES)
    slab = hidden // (XS * ZHI * CORES)
    taken = PATCH * PATCH
    rows = taken * SUB
    copies = []

    def place(piece, at, source_x, of_zhi, of_core, begin=0, size=depth):
        shard = lax.rem(source_x, XS) * (ZHI * CORES) + of_zhi * CORES + of_core
        lines = pl.ds(at, size)

        def put(columns, into):
            copy = pltpu.make_async_copy(piece.at[lines, columns], into, sems.at[len(copies)])
            copy.start()
            copies.append(copy)

        line = pl.multiple_of(shard * depth + begin, size)
        put(pl.ds(0, hidden), w_in.at[pl.ds(line, size), :])
        for part in range(slab // depth):
            line = pl.multiple_of(shard * slab + part * depth + begin, size)
            put(pl.ds(hidden + part * align, align), w_out.at[pl.ds(line, size), :])

    half = depth // 2
    for near, opposite, far, of_core in (
        (own_near, own_far, cross, core),
        (own_near_other, own_far_other, cross_other, 1 - core),
    ):
        for k, step in enumerate((0, 1, XS - 1)):
            place(near, k * depth, x + step, zhi, of_core)
        for begin in (0, half):
            place(opposite, begin, x + 2, zhi, of_core, begin, half)
        for k in range(XS):
            place(far, k * depth, k, 1 - zhi, of_core)

    lat = lat_ref[...] + below_ref[...] + above_ref[...]
    top = lat.astype(BF16)
    rest = lat - top.astype(F32)
    mid = rest.astype(BF16)
    low_part = (rest - mid.astype(F32)).astype(BF16)
    split = jnp.concatenate(
        [top.astype(F32), mid.astype(F32), low_part.astype(F32)], axis=0
    ).astype(BF16)
    cells = lat.shape[1]
    tokens = target_ref.shape[0]
    room = 256
    cols = across // PATCH

    def selection(u, v):
        shape = (cells, room)
        token = iota(shape, 1)
        lane = (token // cols) * (PATCH * across) + u * across + (token % cols) * PATCH + v
        return jnp.where((lane == iota(shape, 0)) & (token < tokens), 1.0, 0.0).astype(BF16)

    picks = [selection(u, v) for u in range(PATCH) for v in range(PATCH)]
    lines = []
    for pick in picks:
        got = nn(split, pick)
        lines.append(got[0:SUB] + got[SUB : 2 * SUB] + got[2 * SUB :])
    patches_t = jnp.concatenate(lines, axis=0)
    patches = patches_t.T
    empty = jnp.zeros((SUB - LATENT, width), F32)
    spread = []
    for k in range(taken):
        spread += [ew_ref[k * LATENT : (k + 1) * LATENT, :], empty]
    ew_top, ew_low = parts(jnp.concatenate(spread, axis=0))
    p_top, p_low = parts(patches[:tokens])
    embedded = nn(p_top, ew_top) + nn(p_low, ew_top) + nn(p_top, ew_low)
    emb[...] = (embedded + eb_ref[...]).astype(BF16)

    for copy in copies:
        copy.wait()

    step = 1024
    acc[...] = jnp.zeros_like(acc)

    for tile in range(hidden // step):
        at = pl.ds(pl.multiple_of(tile * step, step), step)
        h = nn(emb[...], w_in[:, at]) + pib_ref[:, at]
        pre[:, at] = h
        acc[...] += nn((h * sigmoid(h)).astype(BF16), w_out[at, :])

    projected = acc[...] + pob_ref[...]
    target = target_ref[...].astype(F32)
    unit_target = target * lax.rsqrt(jnp.sum(target * target, axis=1, keepdims=True) + EPS_UNIT)
    inv_len = lax.rsqrt(jnp.sum(projected * projected, axis=1, keepdims=True) + EPS_UNIT)
    unit_proj = projected * inv_len
    cosine = jnp.sum(unit_proj * unit_target, axis=1, keepdims=True)
    grad_out = (-inv_len * (unit_target - cosine * unit_proj)).astype(BF16)
    grad_emb[...] = jnp.zeros_like(grad_emb)

    for tile in range(hidden // step):
        at = pl.ds(pl.multiple_of(tile * step, step), step)
        back = nt(grad_out, w_out[at, :])
        h = pre[:, at]
        sig = sigmoid(h)
        grad_hidden = (back * (sig * (1.0 + h * (1.0 - sig)))).astype(BF16)
        grad_emb[0:tokens, :] += nt(grad_hidden, w_in[:, at])

    grad = grad_emb[...]
    g_top, g_low = parts(grad)
    t_top, t_low = parts(patches_t)
    both = nn(jnp.concatenate([t_top, t_low], axis=0), g_top)
    embed_ref[...] = both[:rows] + both[rows:] + nn(t_top, g_low)
    both = nt(jnp.concatenate([ew_top, ew_low], axis=0), g_top)
    grad_patch = both[:rows] + both[rows:] + nt(ew_top, g_low)
    total = jnp.zeros((SUB, cells), F32)
    for position, pick in enumerate(picks):
        part = grad_patch[position * SUB : (position + 1) * SUB].astype(BF16)
        total = total + nt(part, pick)
    gl_ref[...] = total


def projector(at, lat, below, above, target, ew, eb, pib, pob, pieces, across):
    rows, width = PATCH * PATCH * SUB, ew.shape[1]
    hidden, align = pib.shape[1], pob.shape[1]
    tokens = target.shape[0]
    flops = 2 * tokens * (2 * width * hidden + 2 * hidden * align)
    return pl.pallas_call(
        lambda *refs: mlp_kernel(across, width, hidden, align, *refs),
        out_shape=(
            jax.ShapeDtypeStruct((rows, width), F32),
            jax.ShapeDtypeStruct(lat.shape, F32),
        ),
        in_specs=[pl.BlockSpec(memory_space=pltpu.SMEM)]
        + [vmem()] * 8
        + [pl.BlockSpec(memory_space=pltpu.HBM)] * len(pieces),
        out_specs=(vmem(), vmem()),
        scratch_shapes=[
            pltpu.VMEM((width, hidden), BF16),
            pltpu.VMEM((hidden, align), BF16),
            pltpu.VMEM((tokens, hidden), F32),
            pltpu.VMEM((tokens, width), BF16),
            pltpu.VMEM((tokens, align), F32),
            pltpu.VMEM((256, width), F32),
            pltpu.SemaphoreType.DMA((54,)),
        ],
        compiler_params=params(32),
        cost_estimate=pl.CostEstimate(
            flops=flops, bytes_accessed=8 << 20, transcendentals=2 * tokens * hidden
        ),
        name="projector",
    )(at, lat, below, above, target, ew, eb, pib, pob, *pieces)


def back_kernel(
    across, gl_ref, before_ref, after_ref, f_ref, mean_ref, inv_ref, gain_ref, bias_ref,
    k_ref, embed_ref, send_ref, gs_ref, act, grads_t, by_bias, by_gain, pack,
):
    images, cells, channels = f_ref.shape
    per_group = channels // GROUPS
    gl, before, after = gl_ref[...], before_ref[...], after_ref[...]
    col, row = lane_masks(gl.shape, across)
    lines = (
        jnp.where(row == 0, roll(gl, -across), roll(after, across)),
        gl,
        jnp.where(row == 0, roll(before, -across), roll(gl, across)),
    )
    parts = []
    for g in lines:
        parts.append(jnp.where(col < across - 1, roll(g, -1), 0.0))
        parts.append(g)
        parts.append(jnp.where(col > 0, roll(g, 1), 0.0))
    parts.append(jnp.zeros((LANES - TAPS * SUB, gl.shape[1]), F32))
    grads = jnp.concatenate(parts, axis=0)
    grads_t[...] = grads.T.astype(BF16)
    gain, bias = gain_ref[...], bias_ref[...]
    by_bias[...] = jnp.zeros_like(by_bias)
    by_gain[...] = jnp.zeros_like(by_gain)
    for i in range(images):
        at = slice(i * cells, (i + 1) * cells)
        v = f_ref[i].astype(F32)
        normed = (v - mean_ref[i : i + 1, :]) * inv_ref[i : i + 1, :]
        shifted = normed * gain + bias
        sig = sigmoid(shifted)
        act[at, :] = (shifted * sig).astype(BF16)
        grad_active = nn(grads_t[at, :], k_ref[...])
        gs = grad_active * (sig * (1.0 + shifted * (1.0 - sig)))
        gs_ref[i] = gs
        by_bias[i : i + 1, :] = jnp.sum(gs, axis=0, keepdims=True)
        by_gain[i : i + 1, :] = jnp.sum(gs * normed, axis=0, keepdims=True)
    conv = nn(grads.astype(BF16), act[...])
    stat = nn(by_bias[...] * gain, to_groups(channels, per_group, 0), HIGH) + nn(
        by_gain[...] * gain, to_groups(channels, per_group, GROUPS), HIGH
    )
    bias_part = jnp.sum(by_bias[...], axis=0, keepdims=True)
    gain_part = jnp.sum(by_gain[...], axis=0, keepdims=True)
    packed = halves(pack_stats(stat))
    for r in range(CHUNKS):
        send_ref[r, CHUNK_ROWS:ALL_ROWS, :] = packed
    blocks = channels // LANES
    half = CHUNKS // 2
    pack[...] = jnp.zeros_like(pack)
    for r in range(half):
        block, latent = r // LATENT, r % LATENT
        lanes = slice(block * LANES, (block + 1) * LANES)
        for position in range(TAPS):
            line = position * SUB + latent
            pack[r, position : position + 1, :] = conv[line : line + 1, lanes]
        lanes = slice((r // 2) * LANES, (r // 2 + 1) * LANES)
        for part in range(2):
            line = (r % 2) * 2 * SUB + part * SUB
            pack[half + r, part * LATENT : (part + 1) * LATENT, :] = embed_ref[
                line : line + LATENT, lanes
            ]
        if r < 2 * blocks:
            one = gain_part if r < blocks else bias_part
            lanes = slice((r % blocks) * LANES, (r % blocks + 1) * LANES)
            pack[half + r, SUB : SUB + 1, :] = one[:, lanes]
    for r in range(CHUNKS):
        send_ref[r, 0:CHUNK_ROWS, :] = pack[r].astype(BF16)


def conv_backward(gl, before, after, features, mean, inv, gain, bias, kernel_rows, embed, across):
    images, cells, channels = features.shape
    return pl.pallas_call(
        lambda *refs: back_kernel(across, *refs),
        out_shape=(
            jax.ShapeDtypeStruct((CHUNKS, ALL_ROWS, LANES), BF16),
            jax.ShapeDtypeStruct((images, cells, channels), F32),
        ),
        in_specs=[vmem()] * 10,
        out_specs=(vmem(),) * 2,
        scratch_shapes=[
            pltpu.VMEM((images * cells, channels), BF16),
            pltpu.VMEM((images * cells, LANES), BF16),
            pltpu.VMEM((STAT_ROWS, channels), F32),
            pltpu.VMEM((STAT_ROWS, channels), F32),
            pltpu.VMEM((CHUNKS, CHUNK_ROWS, LANES), F32),
        ],
        compiler_params=params(),
        name="back",
    )(gl, before, after, features, mean, inv, gain, bias, kernel_rows, embed)


def last_kernel(members, got_ref, f_ref, mean_ref, inv_ref, gain_ref, gs_ref, out_ref):
    images, _, channels = f_ref.shape
    per_group = channels // GROUPS
    total = unpack_stats(got_ref[...])
    first = nn(total, from_groups(channels, per_group, 0), HIGH) * (1.0 / members)
    second = nn(total, from_groups(channels, per_group, GROUPS), HIGH) * (1.0 / members)
    gain = gain_ref[...]
    for i in range(images):
        v = f_ref[i].astype(F32)
        inv = inv_ref[i : i + 1, :]
        normed = (v - mean_ref[i : i + 1, :]) * inv
        out = inv * (gs_ref[i] * gain - first[i : i + 1] - normed * second[i : i + 1])
        out_ref[i] = out.astype(BF16)


def feature_grad(got, features, mean, inv, gain, grad_shift, members):
    return pl.pallas_call(
        lambda *refs: last_kernel(members, *refs),
        out_shape=jax.ShapeDtypeStruct(features.shape, BF16),
        in_specs=[vmem()] * 6,
        out_specs=vmem(),
        compiler_params=params(),
        cost_estimate=pl.CostEstimate(
            flops=10 * features.size, bytes_accessed=8 * features.size, transcendentals=0
        ),
        name="last",
    )(got, features, mean, inv, gain, grad_shift)


def plane_kernel(at_ref, got_ref, out_ref):
    chunk = jnp.zeros((CHUNK_ROWS, LANES), F32)
    stat = jnp.zeros((SUB, LANES), F32)
    for r in range(CHUNKS):
        chunk = chunk + got_ref[r, 0:CHUNK_ROWS, :].astype(F32)
        pair = got_ref[r, CHUNK_ROWS:ALL_ROWS, :].astype(F32)
        stat = stat + jnp.where(at_ref[2] == (r // CORES) % YS, pair[:SUB] + pair[SUB:], 0.0)
    chunk, stat = chunk.astype(BF16), halves(stat)
    for r in range(out_ref.shape[0]):
        out_ref[r, 0:CHUNK_ROWS, :] = chunk
        out_ref[r, CHUNK_ROWS:ALL_ROWS, :] = stat


def plane_total(at, got):
    return pl.pallas_call(
        plane_kernel,
        out_shape=jax.ShapeDtypeStruct((ZHI * ZLO, ALL_ROWS, LANES), BF16),
        in_specs=[pl.BlockSpec(memory_space=pltpu.SMEM), vmem()],
        out_specs=vmem(),
        compiler_params=params(),
        name="plane",
    )(at, got)


def column_kernel(at_ref, got_ref, out_ref, stat_ref):
    chunk = jnp.zeros((CHUNK_ROWS, LANES), F32)
    stat = jnp.zeros((SUB, LANES), F32)
    for r in range(ZHI * ZLO):
        chunk = chunk + got_ref[r, 0:CHUNK_ROWS, :].astype(F32)
        pair = got_ref[r, CHUNK_ROWS:ALL_ROWS, :].astype(F32)
        stat = stat + jnp.where(at_ref[3] == r % ZLO, pair[:SUB] + pair[SUB:], 0.0)
    chunk = chunk.astype(BF16)
    for r in range(out_ref.shape[0]):
        out_ref[r] = chunk
    stat_ref[...] = stat


def column_total(at, got):
    return pl.pallas_call(
        column_kernel,
        out_shape=(
            jax.ShapeDtypeStruct((CHUNKS, CHUNK_ROWS, LANES), BF16),
            jax.ShapeDtypeStruct((SUB, LANES), F32),
        ),
        in_specs=[pl.BlockSpec(memory_space=pltpu.SMEM), vmem()],
        out_specs=(vmem(), vmem()),
        compiler_params=params(),
        name="column",
    )(at, got)


def unpack_kernel(got_ref, conv_ref, gain_ref, bias_ref, embed_ref, wide):
    channels = gain_ref.shape[1]
    blocks = channels // LANES
    half = CHUNKS // 2
    wide[...] = got_ref[...].astype(F32)
    for r in range(half):
        block, latent = r // LATENT, r % LATENT
        for position in range(TAPS):
            at = position * channels + block * LANES
            conv_ref[latent : latent + 1, at : at + LANES] = wide[r, position : position + 1, :]
        lanes = slice((r // 2) * LANES, (r // 2 + 1) * LANES)
        line = (r % 2) * SUB
        embed_ref[line : line + SUB, lanes] = wide[half + r, 0:SUB, :]
        lanes = slice((r % blocks) * LANES, (r % blocks + 1) * LANES)
        if r < blocks:
            gain_ref[:, lanes] = wide[half + r, SUB : SUB + 1, :]
        elif r < 2 * blocks:
            bias_ref[:, lanes] = wide[half + r, SUB : SUB + 1, :]


def unpack(got, channels, width):
    return pl.pallas_call(
        unpack_kernel,
        out_shape=(
            jax.ShapeDtypeStruct((LATENT, TAPS * channels), F32),
            jax.ShapeDtypeStruct((1, channels), F32),
            jax.ShapeDtypeStruct((1, channels), F32),
            jax.ShapeDtypeStruct((PATCH * PATCH * LATENT, width), F32),
        ),
        in_specs=[vmem()],
        out_specs=(vmem(),) * 4,
        scratch_shapes=[pltpu.VMEM(got.shape, F32)],
        compiler_params=params(),
        name="unpack",
    )(got)


def device(x, zhi, core, zlo, y):
    return ((x * ZHI + zhi) * CORES + core) * (ZLO * YS) + zlo * YS + y


BOTH = ("rows", "batch")
PLANE = [
    [device(x, h, c, d, y) for x in range(XS) for y in range(YS) for c in range(CORES)]
    for h in range(ZHI)
    for d in range(ZLO)
]
SHEET = [
    [device(x, h, c, d, y) for x in range(XS) for y in range(YS)]
    for h in range(ZHI)
    for d in range(ZLO)
    for c in range(CORES)
]
COLUMN = [
    [device(x, h, c, d, y) for h in range(ZHI) for d in range(ZLO)]
    for x in range(XS)
    for y in range(YS)
    for c in range(CORES)
]


def exchanged(value, groups):
    return lax.all_to_all(value, BOTH, 0, 0, axis_index_groups=groups, tiled=True)


def moved(value, where):
    pairs = []
    for x in range(XS):
        for zhi in range(ZHI):
            for core in range(CORES):
                for zlo in range(ZLO):
                    for y in range(YS):
                        a, b, c, d, e = where(x, zhi, core, zlo, y)
                        pairs.append((device(x, zhi, core, zlo, y), device(a, b, c, d, e)))
    return lax.ppermute(value, ("rows", "batch"), pairs)


def shard_kernel(at_ref, in_ref, out_ref, shard_ref, part_ref):
    depth, hidden = in_ref.shape
    align = out_ref.shape[1]
    shard_ref[:, 0:hidden] = in_ref[...]
    for part in range(out_ref.shape[0] // depth):
        shard_ref[:, hidden + part * align : hidden + (part + 1) * align] = out_ref[
            part * depth : (part + 1) * depth, :
        ]
    size = part_ref.shape[0]
    begin = pl.multiple_of(at_ref[2] * size, size)
    part_ref[...] = shard_ref[pl.ds(begin, size), :]


def shard_of(at, proj_in, proj_out):
    depth, hidden = proj_in.shape
    columns = hidden + proj_out.size // depth
    return pl.pallas_call(
        shard_kernel,
        out_shape=(
            jax.ShapeDtypeStruct((depth, columns), BF16),
            jax.ShapeDtypeStruct((depth // YS, columns), BF16),
        ),
        in_specs=[pl.BlockSpec(memory_space=pltpu.SMEM), vmem(), vmem()],
        out_specs=(vmem(), vmem()),
        compiler_params=params(),
        name="shard",
    )(at, proj_in, proj_out)


def crossed(part):
    return moved(part, lambda x, h, c, d, y: (x, 1 - h, c, ZLO - 1 - d, y))


def from_next(value):
    return moved(value, lambda x, h, c, d, y: ((x + XS - 1) % XS, h, c, d, y))


def from_last(value):
    return moved(value, lambda x, h, c, d, y: ((x + 1) % XS, h, c, d, y))


def along_x(shard):
    half = shard.shape[0] // 2
    plus, minus = from_next(shard), from_last(shard)
    near = jnp.concatenate([shard, plus, minus], axis=0)
    opposite = jnp.concatenate([from_next(plus[:half]), from_last(minus[half:])], axis=0)
    return near, opposite


def swapped(value):
    return moved(value, lambda x, h, c, d, y: (x, h, 1 - c, d, y))


def neighbours(up, down):
    count = lax.axis_size("rows")
    forward = [(i, i + 1) for i in range(count - 1)]
    backward = [(b, a) for a, b in forward]
    return lax.ppermute(up, "rows", backward), lax.ppermute(down, "rows", forward)


def shards(
    features,
    norm_gain,
    norm_bias,
    conv_weight,
    embed_weight,
    embed_bias,
    proj_in,
    proj_in_bias,
    proj_out,
    proj_out_bias,
    targets,
):
    images, height, across, channels = features.shape
    width, align = embed_weight.shape[1], proj_out.shape[1]
    peers = lax.axis_size("rows")
    members = peers * height * across * (channels // GROUPS)
    flat = features.reshape(images, height * across, channels)
    gain, bias = norm_gain.reshape(1, channels), norm_bias.reshape(1, channels)
    rows, batch = lax.axis_index("rows"), lax.axis_index("batch")
    at = jnp.stack([(rows // CORES) % ZHI, rows % CORES, batch % YS, batch // YS, rows // (ZHI * CORES)])
    at = at.astype(jnp.int32)
    shard, part = shard_of(at, proj_in, proj_out)
    own_near, own_far = along_x(shard)
    taps = conv_weight.reshape(LATENT, TAPS, channels).transpose(1, 0, 2)
    taps = jnp.pad(taps, ((0, 0), (0, SUB - LATENT), (0, 0))).reshape(TAPS * SUB, channels)
    taps_full = jnp.pad(taps, ((0, LANES - TAPS * SUB), (0, 0)))

    sums = group_stats(flat, peers)
    stats = lax.all_to_all(sums, "rows", 0, 0, tiled=True)
    cross, stats, own_near, own_far = lax.optimization_barrier((crossed(part), stats, own_near, own_far))
    cross = jnp.broadcast_to(cross[None], (XS * YS, *cross.shape))
    cross = exchanged(cross, SHEET).reshape(-1, shard.shape[1])
    lat, up, down, mean, inv = conv_forward(stats, flat, gain, bias, taps, across, members)
    above, below = neighbours(up, down)
    own_near, own_far, above, below = lax.optimization_barrier((own_near, own_far, above, below))
    pieces = [own_near, own_far, cross]
    others = [swapped(own_near), swapped(own_far)]
    cross, others = lax.optimization_barrier((cross, others))
    pieces = [own_near, own_far, cross] + others + [swapped(cross)]
    target = targets.reshape(-1, align)
    embed_part, grad_lat = projector(
        at, lat, below, above, target, embed_weight, embed_bias.reshape(1, -1),
        proj_in_bias.reshape(1, -1), proj_out_bias.reshape(1, -1), pieces, across,
    )
    after, before = neighbours(grad_lat, grad_lat)
    send, grad_shift = conv_backward(
        grad_lat, before, after, flat, mean, inv, gain, bias, taps_full, embed_part, across
    )
    plane = exchanged(send, PLANE)
    column = exchanged(plane_total(at, plane), COLUMN)
    chunks, got = column_total(at, column)
    everything = exchanged(chunks, PLANE)
    grad_features = feature_grad(got, flat, mean, inv, gain, grad_shift, members)
    grad_conv, grad_gain, grad_bias, grad_embed = unpack(everything, channels, width)
    return (
        grad_features.reshape(features.shape),
        grad_conv,
        grad_gain.reshape(channels),
        grad_bias.reshape(channels),
        grad_embed,
    )


def solution(mesh):
    in_specs = (
        P("batch", "rows", None, None),
        P(),
        P(),
        P(),
        P(),
        P(),
        P("rows", None),
        P(),
        P("rows", None),
        P(),
        P("batch", "rows", None, None),
    )
    out_specs = (P("batch", "rows", None, None), P(), P(), P(), P())
    return jax.shard_map(shards, mesh=mesh, in_specs=in_specs, out_specs=out_specs, check_vma=False)
```

```python
import jax
import jax.numpy as jnp
from jax import lax
from jax.experimental import pallas as pl
from jax.experimental.pallas import tpu as pltpu
from jax.sharding import PartitionSpec as P

GROUPS = 32
LATENT = 4
PATCH = 2
EPS_NORM = 1e-06
EPS_UNIT = 1e-06

XS, ZHI, CORES, ZLO, YS = 4, 2, 2, 8, 4

HIGH = lax.Precision.HIGHEST
F32 = jnp.float32
BF16 = jnp.bfloat16
TAPS = 9
SUB = 8
LANES = 128
STAT_ROWS = 16
CHUNKS, CHUNK_ROWS, ALL_ROWS = 32, 16, 32
CONV_COST = 20_000_000_000
PART = 16


def params(limit_mb=12):
    return pltpu.CompilerParams(vmem_limit_bytes=limit_mb << 20)


def vmem():
    return pl.BlockSpec(memory_space=pltpu.VMEM)


def in_hbm(v):
    return pltpu.with_memory_space_constraint(v, pltpu.HBM)


def sigmoid(v):
    return 0.5 + 0.5 * jnp.tanh(0.5 * v)


def nt(a, b, precision=None):
    return lax.dot_general(
        a, b, (((1,), (1,)), ((), ())), preferred_element_type=F32, precision=precision
    )


def nn(a, b, precision=None):
    return lax.dot_general(
        a, b, (((1,), (0,)), ((), ())), preferred_element_type=F32, precision=precision
    )


def iota(shape, dim):
    return lax.broadcasted_iota(jnp.int32, shape, dim)


def to_groups(channels, per_group, offset):
    shape = (channels, LANES)
    return (iota(shape, 0) // per_group + offset == iota(shape, 1)).astype(F32)


def from_groups(channels, per_group, offset):
    shape = (LANES, channels)
    return (iota(shape, 1) // per_group + offset == iota(shape, 0)).astype(F32)


def pack_stats(total):
    lane = iota((SUB, LANES), 1)
    return jnp.where(lane < LANES // 2, total[:SUB], pltpu.roll(total[SUB:], LANES // 2, 1))


def unpack_stats(packed):
    return jnp.concatenate([packed, pltpu.roll(packed, LANES // 2, 1)], axis=0)


def parts(v):
    top = v.astype(BF16)
    return top, (v - top.astype(F32)).astype(BF16)


def halves(packed):
    top = packed.astype(BF16).astype(F32)
    return jnp.concatenate([top, packed - top], axis=0).astype(BF16)


def stats_kernel(f_ref, out_ref, sums, squares):
    images, _, channels = f_ref.shape
    sums[...] = jnp.zeros_like(sums)
    squares[...] = jnp.zeros_like(squares)
    for i in range(images):
        v = f_ref[i].astype(F32)
        sums[i : i + 1, :] = jnp.sum(v, axis=0, keepdims=True)
        squares[i : i + 1, :] = jnp.sum(v * v, axis=0, keepdims=True)
    per_group = channels // GROUPS
    total = nn(sums[...], to_groups(channels, per_group, 0), HIGH) + nn(
        squares[...], to_groups(channels, per_group, GROUPS), HIGH
    )
    packed = pack_stats(total)
    for r in range(out_ref.shape[0]):
        out_ref[r] = packed


def group_stats(features, peers):
    channels = features.shape[-1]
    return pl.pallas_call(
        stats_kernel,
        out_shape=jax.ShapeDtypeStruct((peers, SUB, LANES), F32),
        in_specs=[vmem()],
        out_specs=vmem(),
        scratch_shapes=[pltpu.VMEM((STAT_ROWS, channels), F32)] * 2,
        compiler_params=params(),
        name="stats",
    )(features)


def lane_masks(shape, across):
    lane = iota(shape, 1)
    return lane % across, (lane // across) % 2


def roll(v, shift):
    return pltpu.roll(v, shift % v.shape[1], 1)


def conv_kernel(
    across, members, st_ref, f_ref, gain_ref, bias_ref, k_ref,
    lat_ref, up_ref, down_ref, mean_ref, inv_ref, act,
):
    images, cells, channels = f_ref.shape
    per_group = channels // GROUPS
    total = unpack_stats(jnp.sum(st_ref[...], axis=0))
    mean = nn(total, from_groups(channels, per_group, 0), HIGH) * (1.0 / members)
    square = nn(total, from_groups(channels, per_group, GROUPS), HIGH) * (1.0 / members)
    inv = lax.rsqrt(jnp.maximum(square - mean * mean, 0.0) + EPS_NORM)
    mean_ref[...] = mean
    inv_ref[...] = inv
    gain, bias = gain_ref[...], bias_ref[...]
    for i in range(images):
        v = f_ref[i].astype(F32)
        shifted = (v - mean[i : i + 1]) * inv[i : i + 1] * gain + bias
        act[i * cells : (i + 1) * cells, :] = (shifted * sigmoid(shifted)).astype(BF16)
    taps = nt(k_ref[...], act[...])
    shape = (SUB, images * cells)
    col, row = lane_masks(shape, across)

    def tap(position):
        return taps[position * SUB : (position + 1) * SUB]

    def line(dy):
        low = jnp.where(col > 0, roll(tap(3 * dy), 1), 0.0)
        high = jnp.where(col < across - 1, roll(tap(3 * dy + 2), -1), 0.0)
        return tap(3 * dy + 1) + low + high

    first, middle, last = line(0), line(1), line(2)
    last_up, first_down = roll(last, -across), roll(first, across)
    lat_ref[...] = middle + jnp.where(row == 0, last_up, first_down)
    up_ref[...] = jnp.where(row == 1, roll(last, across), 0.0)
    down_ref[...] = jnp.where(row == 0, roll(first, -across), 0.0)


def conv_forward(stats, features, gain, bias, kernel_rows, across, members):
    images, cells, channels = features.shape
    line = jax.ShapeDtypeStruct((SUB, images * cells), F32)
    stat = jax.ShapeDtypeStruct((STAT_ROWS, channels), F32)
    return pl.pallas_call(
        lambda *refs: conv_kernel(across, members, *refs),
        out_shape=(line, line, line, stat, stat),
        in_specs=[vmem()] * 5,
        out_specs=(vmem(),) * 5,
        scratch_shapes=[pltpu.VMEM((images * cells, channels), BF16)],
        compiler_params=params(),
        cost_estimate=pl.CostEstimate(
            flops=CONV_COST, bytes_accessed=features.size * 2, transcendentals=features.size
        ),
        name="conv",
    )(stats, features, gain, bias, kernel_rows)


def mlp_kernel(
    across, width, hidden, align, at_ref, lat_ref, below_ref, above_ref, target_ref,
    ew_ref, eb_ref, pib_ref, pob_ref,
    own_near, own_far, cross, own_near_other, own_far_other, cross_other,
    embed_ref, gl_ref, w_in, w_out, pre, emb, acc, grad_emb, wanted, sems,
):
    zhi, core, x = at_ref[0], at_ref[1], at_ref[4]
    depth = width // (XS * ZHI * CORES)
    slab = hidden // (XS * ZHI * CORES)
    taken = PATCH * PATCH
    rows = taken * SUB
    copies = [pltpu.make_async_copy(target_ref, wanted, sems.at[0])]
    copies[0].start()

    def place(piece, at, source_x, of_zhi, of_core, begin=0, size=depth):
        shard = lax.rem(source_x, XS) * (ZHI * CORES) + of_zhi * CORES + of_core
        lines = pl.ds(at, size)

        def put(columns, into):
            copy = pltpu.make_async_copy(piece.at[lines, columns], into, sems.at[len(copies)])
            copy.start()
            copies.append(copy)

        line = pl.multiple_of(shard * depth + begin, size)
        put(pl.ds(0, hidden), w_in.at[pl.ds(line, size), :])
        for part in range(slab // depth):
            line = pl.multiple_of(shard * slab + part * depth + begin, size)
            put(pl.ds(hidden + part * align, align), w_out.at[pl.ds(line, size), :])

    half = depth // 2
    for near, opposite, far, of_core in (
        (own_near, own_far, cross, core),
        (own_near_other, own_far_other, cross_other, 1 - core),
    ):
        for k, step in enumerate((0, 1, XS - 1)):
            place(near, k * depth, x + step, zhi, of_core)
        for begin in (0, half):
            place(opposite, begin, x + 2, zhi, of_core, begin, half)
        for k in range(XS):
            place(far, k * depth, k, 1 - zhi, of_core)

    lat = lat_ref[...] + below_ref[...] + above_ref[...]
    top = lat.astype(BF16)
    rest = lat - top.astype(F32)
    mid = rest.astype(BF16)
    low_part = (rest - mid.astype(F32)).astype(BF16)
    split = jnp.concatenate(
        [top.astype(F32), mid.astype(F32), low_part.astype(F32)], axis=0
    ).astype(BF16)
    cells = lat.shape[1]
    tokens = target_ref.shape[0]
    room = 256
    cols = across // PATCH

    def selection(u, v):
        shape = (cells, room)
        token = iota(shape, 1)
        lane = (token // cols) * (PATCH * across) + u * across + (token % cols) * PATCH + v
        return jnp.where((lane == iota(shape, 0)) & (token < tokens), 1.0, 0.0).astype(BF16)

    picks = [selection(u, v) for u in range(PATCH) for v in range(PATCH)]
    lines = []
    for pick in picks:
        got = nn(split, pick)
        lines.append(got[0:SUB] + got[SUB : 2 * SUB] + got[2 * SUB :])
    patches_t = jnp.concatenate(lines, axis=0)
    patches = patches_t.T
    empty = jnp.zeros((SUB - LATENT, width), F32)
    spread = []
    for k in range(taken):
        spread += [ew_ref[k * LATENT : (k + 1) * LATENT, :], empty]
    ew_top, ew_low = parts(jnp.concatenate(spread, axis=0))
    p_top, p_low = parts(patches[:tokens])
    embedded = nn(p_top, ew_top) + nn(p_low, ew_top) + nn(p_top, ew_low)
    emb[...] = (embedded + eb_ref[...]).astype(BF16)

    for copy in copies:
        copy.wait()

    step = 1024
    acc[...] = jnp.zeros_like(acc)

    for tile in range(hidden // step):
        at = pl.ds(pl.multiple_of(tile * step, step), step)
        h = nn(emb[...], w_in[:, at]) + pib_ref[:, at]
        pre[:, at] = h
        acc[...] += nn((h * sigmoid(h)).astype(BF16), w_out[at, :])

    projected = acc[...] + pob_ref[...]
    target = wanted[...].astype(F32)
    unit_target = target * lax.rsqrt(jnp.sum(target * target, axis=1, keepdims=True) + EPS_UNIT)
    inv_len = lax.rsqrt(jnp.sum(projected * projected, axis=1, keepdims=True) + EPS_UNIT)
    unit_proj = projected * inv_len
    cosine = jnp.sum(unit_proj * unit_target, axis=1, keepdims=True)
    grad_out = (-inv_len * (unit_target - cosine * unit_proj)).astype(BF16)
    grad_emb[...] = jnp.zeros_like(grad_emb)

    for tile in range(hidden // step):
        at = pl.ds(pl.multiple_of(tile * step, step), step)
        back = nt(grad_out, w_out[at, :])
        h = pre[:, at]
        sig = sigmoid(h)
        grad_hidden = (back * (sig * (1.0 + h * (1.0 - sig)))).astype(BF16)
        grad_emb[0:tokens, :] += nt(grad_hidden, w_in[:, at])

    grad = grad_emb[...]
    g_top, g_low = parts(grad)
    t_top, t_low = parts(patches_t)
    both = nn(jnp.concatenate([t_top, t_low], axis=0), g_top)
    embed_ref[...] = both[:rows] + both[rows:] + nn(t_top, g_low)
    both = nt(jnp.concatenate([ew_top, ew_low], axis=0), g_top)
    grad_patch = both[:rows] + both[rows:] + nt(ew_top, g_low)
    total = jnp.zeros((SUB, cells), F32)
    for position, pick in enumerate(picks):
        part = grad_patch[position * SUB : (position + 1) * SUB].astype(BF16)
        total = total + nt(part, pick)
    gl_ref[...] = total


def projector(at, lat, below, above, target, ew, eb, pib, pob, pieces, across):
    rows, width = PATCH * PATCH * SUB, ew.shape[1]
    hidden, align = pib.shape[1], pob.shape[1]
    tokens = target.shape[0]
    flops = 2 * tokens * (2 * width * hidden + 2 * hidden * align)
    return pl.pallas_call(
        lambda *refs: mlp_kernel(across, width, hidden, align, *refs),
        out_shape=(
            jax.ShapeDtypeStruct((rows, width), F32),
            jax.ShapeDtypeStruct(lat.shape, F32),
        ),
        in_specs=[pl.BlockSpec(memory_space=pltpu.SMEM)]
        + [vmem()] * 3
        + [pl.BlockSpec(memory_space=pltpu.HBM)]
        + [vmem()] * 4
        + [pl.BlockSpec(memory_space=pltpu.HBM)] * len(pieces),
        out_specs=(vmem(), vmem()),
        scratch_shapes=[
            pltpu.VMEM((width, hidden), BF16),
            pltpu.VMEM((hidden, align), BF16),
            pltpu.VMEM((tokens, hidden), F32),
            pltpu.VMEM((tokens, width), BF16),
            pltpu.VMEM((tokens, align), F32),
            pltpu.VMEM((256, width), F32),
            pltpu.VMEM((tokens, align), BF16),
            pltpu.SemaphoreType.DMA((55,)),
        ],
        compiler_params=params(32),
        cost_estimate=pl.CostEstimate(
            flops=flops, bytes_accessed=8 << 20, transcendentals=2 * tokens * hidden
        ),
        name="projector",
    )(at, lat, below, above, in_hbm(target), ew, eb, pib, pob, in_hbm(pieces[0]), *pieces[1:])


def back_kernel(
    across, gl_ref, before_ref, after_ref, f_ref, mean_ref, inv_ref, gain_ref, bias_ref,
    k_ref, embed_ref, send_ref, gs_ref, act, grads_t, by_bias, by_gain, pack,
):
    images, cells, channels = f_ref.shape
    per_group = channels // GROUPS
    gl, before, after = gl_ref[...], before_ref[...], after_ref[...]
    col, row = lane_masks(gl.shape, across)
    lines = (
        jnp.where(row == 0, roll(gl, -across), roll(after, across)),
        gl,
        jnp.where(row == 0, roll(before, -across), roll(gl, across)),
    )
    parts = []
    for g in lines:
        parts.append(jnp.where(col < across - 1, roll(g, -1), 0.0))
        parts.append(g)
        parts.append(jnp.where(col > 0, roll(g, 1), 0.0))
    parts.append(jnp.zeros((LANES - TAPS * SUB, gl.shape[1]), F32))
    grads = jnp.concatenate(parts, axis=0)
    grads_t[...] = grads.T.astype(BF16)
    gain, bias = gain_ref[...], bias_ref[...]
    by_bias[...] = jnp.zeros_like(by_bias)
    by_gain[...] = jnp.zeros_like(by_gain)
    for i in range(images):
        at = slice(i * cells, (i + 1) * cells)
        v = f_ref[i].astype(F32)
        normed = (v - mean_ref[i : i + 1, :]) * inv_ref[i : i + 1, :]
        shifted = normed * gain + bias
        sig = sigmoid(shifted)
        act[at, :] = (shifted * sig).astype(BF16)
        grad_active = nn(grads_t[at, :], k_ref[...])
        gs = grad_active * (sig * (1.0 + shifted * (1.0 - sig)))
        gs_ref[i] = gs
        by_bias[i : i + 1, :] = jnp.sum(gs, axis=0, keepdims=True)
        by_gain[i : i + 1, :] = jnp.sum(gs * normed, axis=0, keepdims=True)
    conv = nn(grads.astype(BF16), act[...])
    stat = nn(by_bias[...] * gain, to_groups(channels, per_group, 0), HIGH) + nn(
        by_gain[...] * gain, to_groups(channels, per_group, GROUPS), HIGH
    )
    bias_part = jnp.sum(by_bias[...], axis=0, keepdims=True)
    gain_part = jnp.sum(by_gain[...], axis=0, keepdims=True)
    packed = halves(pack_stats(stat))
    for r in range(CHUNKS):
        send_ref[r, CHUNK_ROWS:ALL_ROWS, :] = packed
    blocks = channels // LANES
    half = CHUNKS // 2
    pack[...] = jnp.zeros_like(pack)
    for r in range(half):
        block, latent = r // LATENT, r % LATENT
        lanes = slice(block * LANES, (block + 1) * LANES)
        for position in range(TAPS):
            line = position * SUB + latent
            pack[r, position : position + 1, :] = conv[line : line + 1, lanes]
        lanes = slice((r // 2) * LANES, (r // 2 + 1) * LANES)
        for part in range(2):
            line = (r % 2) * 2 * SUB + part * SUB
            pack[half + r, part * LATENT : (part + 1) * LATENT, :] = embed_ref[
                line : line + LATENT, lanes
            ]
        if r < 2 * blocks:
            one = gain_part if r < blocks else bias_part
            lanes = slice((r % blocks) * LANES, (r % blocks + 1) * LANES)
            pack[half + r, SUB : SUB + 1, :] = one[:, lanes]
    for r in range(CHUNKS):
        send_ref[r, 0:CHUNK_ROWS, :] = pack[r].astype(BF16)


def conv_backward(gl, before, after, features, mean, inv, gain, bias, kernel_rows, embed, across):
    images, cells, channels = features.shape
    return pl.pallas_call(
        lambda *refs: back_kernel(across, *refs),
        out_shape=(
            jax.ShapeDtypeStruct((CHUNKS, ALL_ROWS, LANES), BF16),
            jax.ShapeDtypeStruct((images, cells, channels), F32),
        ),
        in_specs=[vmem()] * 10,
        out_specs=(vmem(),) * 2,
        scratch_shapes=[
            pltpu.VMEM((images * cells, channels), BF16),
            pltpu.VMEM((images * cells, LANES), BF16),
            pltpu.VMEM((STAT_ROWS, channels), F32),
            pltpu.VMEM((STAT_ROWS, channels), F32),
            pltpu.VMEM((CHUNKS, CHUNK_ROWS, LANES), F32),
        ],
        compiler_params=params(),
        name="back",
    )(gl, before, after, features, mean, inv, gain, bias, kernel_rows, embed)


def last_kernel(members, got_ref, f_ref, mean_ref, inv_ref, gain_ref, gs_ref, out_ref):
    images, _, channels = f_ref.shape
    per_group = channels // GROUPS
    total = unpack_stats(got_ref[...])
    first = nn(total, from_groups(channels, per_group, 0), HIGH) * (1.0 / members)
    second = nn(total, from_groups(channels, per_group, GROUPS), HIGH) * (1.0 / members)
    gain = gain_ref[...]
    for i in range(images):
        v = f_ref[i].astype(F32)
        inv = inv_ref[i : i + 1, :]
        normed = (v - mean_ref[i : i + 1, :]) * inv
        out = inv * (gs_ref[i] * gain - first[i : i + 1] - normed * second[i : i + 1])
        out_ref[i] = out.astype(BF16)


def feature_grad(got, features, mean, inv, gain, grad_shift, members):
    return pl.pallas_call(
        lambda *refs: last_kernel(members, *refs),
        out_shape=jax.ShapeDtypeStruct(features.shape, BF16),
        in_specs=[vmem()] * 6,
        out_specs=vmem(),
        compiler_params=params(),
        cost_estimate=pl.CostEstimate(
            flops=10 * features.size, bytes_accessed=8 * features.size, transcendentals=0
        ),
        name="last",
    )(got, features, mean, inv, gain, grad_shift)


def plane_kernel(at_ref, got_ref, out_ref):
    chunk = jnp.zeros((CHUNK_ROWS, LANES), F32)
    stat = jnp.zeros((SUB, LANES), F32)
    for r in range(CHUNKS):
        chunk = chunk + got_ref[r, 0:CHUNK_ROWS, :].astype(F32)
        pair = got_ref[r, CHUNK_ROWS:ALL_ROWS, :].astype(F32)
        stat = stat + jnp.where(at_ref[2] == (r // CORES) % YS, pair[:SUB] + pair[SUB:], 0.0)
    chunk, stat = chunk.astype(BF16), halves(stat)
    for r in range(out_ref.shape[0]):
        out_ref[r, 0:CHUNK_ROWS, :] = chunk
        out_ref[r, CHUNK_ROWS:ALL_ROWS, :] = stat


def plane_total(at, got):
    return pl.pallas_call(
        plane_kernel,
        out_shape=jax.ShapeDtypeStruct((ZHI * ZLO, ALL_ROWS, LANES), BF16),
        in_specs=[pl.BlockSpec(memory_space=pltpu.SMEM), vmem()],
        out_specs=vmem(),
        compiler_params=params(),
        name="plane",
    )(at, got)


def column_kernel(at_ref, got_ref, out_ref, stat_ref):
    chunk = jnp.zeros((CHUNK_ROWS, LANES), F32)
    stat = jnp.zeros((SUB, LANES), F32)
    for r in range(ZHI * ZLO):
        chunk = chunk + got_ref[r, 0:CHUNK_ROWS, :].astype(F32)
        pair = got_ref[r, CHUNK_ROWS:ALL_ROWS, :].astype(F32)
        stat = stat + jnp.where(at_ref[3] == r % ZLO, pair[:SUB] + pair[SUB:], 0.0)
    chunk = chunk.astype(BF16)
    for r in range(out_ref.shape[0]):
        out_ref[r] = chunk
    stat_ref[...] = stat


def column_total(at, got):
    return pl.pallas_call(
        column_kernel,
        out_shape=(
            jax.ShapeDtypeStruct((CHUNKS, CHUNK_ROWS, LANES), BF16),
            jax.ShapeDtypeStruct((SUB, LANES), F32),
        ),
        in_specs=[pl.BlockSpec(memory_space=pltpu.SMEM), vmem()],
        out_specs=(vmem(), vmem()),
        compiler_params=params(),
        name="column",
    )(at, got)


def unpack_kernel(got_ref, conv_ref, gain_ref, bias_ref, embed_ref, wide):
    channels = gain_ref.shape[1]
    blocks = channels // LANES
    half = CHUNKS // 2
    wide[...] = got_ref[...].astype(F32)
    for r in range(half):
        block, latent = r // LATENT, r % LATENT
        for position in range(TAPS):
            at = position * channels + block * LANES
            conv_ref[latent : latent + 1, at : at + LANES] = wide[r, position : position + 1, :]
        lanes = slice((r // 2) * LANES, (r // 2 + 1) * LANES)
        line = (r % 2) * SUB
        embed_ref[line : line + SUB, lanes] = wide[half + r, 0:SUB, :]
        lanes = slice((r % blocks) * LANES, (r % blocks + 1) * LANES)
        if r < blocks:
            gain_ref[:, lanes] = wide[half + r, SUB : SUB + 1, :]
        elif r < 2 * blocks:
            bias_ref[:, lanes] = wide[half + r, SUB : SUB + 1, :]


def unpack(got, channels, width):
    return pl.pallas_call(
        unpack_kernel,
        out_shape=(
            jax.ShapeDtypeStruct((LATENT, TAPS * channels), F32),
            jax.ShapeDtypeStruct((1, channels), F32),
            jax.ShapeDtypeStruct((1, channels), F32),
            jax.ShapeDtypeStruct((PATCH * PATCH * LATENT, width), F32),
        ),
        in_specs=[vmem()],
        out_specs=(vmem(),) * 4,
        scratch_shapes=[pltpu.VMEM(got.shape, F32)],
        compiler_params=params(),
        name="unpack",
    )(got)


def device(x, zhi, core, zlo, y):
    return ((x * ZHI + zhi) * CORES + core) * (ZLO * YS) + zlo * YS + y


BOTH = ("rows", "batch")
PLANE = [
    [device(x, h, c, d, y) for x in range(XS) for y in range(YS) for c in range(CORES)]
    for h in range(ZHI)
    for d in range(ZLO)
]
SHEET = [
    [device(x, h, c, d, y) for x in range(XS) for y in range(YS)]
    for h in range(ZHI)
    for d in range(ZLO)
    for c in range(CORES)
]
COLUMN = [
    [device(x, h, c, d, y) for h in range(ZHI) for d in range(ZLO)]
    for x in range(XS)
    for y in range(YS)
    for c in range(CORES)
]


def exchanged(value, groups):
    return lax.all_to_all(value, BOTH, 0, 0, axis_index_groups=groups, tiled=True)


def moved(value, where):
    pairs = []
    for x in range(XS):
        for zhi in range(ZHI):
            for core in range(CORES):
                for zlo in range(ZLO):
                    for y in range(YS):
                        a, b, c, d, e = where(x, zhi, core, zlo, y)
                        pairs.append((device(x, zhi, core, zlo, y), device(a, b, c, d, e)))
    return lax.ppermute(value, ("rows", "batch"), pairs)


def shard_kernel(at_ref, in_ref, out_ref, shard_ref, part_ref, sems):
    depth, hidden = in_ref.shape
    align = out_ref.shape[1]
    size = part_ref.shape[0]
    begin = pl.multiple_of(at_ref[2] * size, size)
    copies = []

    def put(source, lines, into, columns):
        copy = pltpu.make_async_copy(
            source.at[lines], into.at[:, columns], sems.at[len(copies)]
        )
        copy.start()
        copies.append(copy)

    for into, first, count in ((part_ref, begin, size), (shard_ref, 0, depth)):
        put(in_ref, pl.ds(first, count), into, pl.ds(0, hidden))
        for part in range(out_ref.shape[0] // depth):
            lines = pl.ds(part * depth + first, count)
            put(out_ref, lines, into, pl.ds(hidden + part * align, align))
    for copy in copies:
        copy.wait()


def shard_of(at, proj_in, proj_out):
    depth, hidden = proj_in.shape
    columns = hidden + proj_out.size // depth
    return pl.pallas_call(
        shard_kernel,
        out_shape=(
            jax.ShapeDtypeStruct((depth, columns), BF16),
            jax.ShapeDtypeStruct((depth // YS, columns), BF16),
        ),
        in_specs=[pl.BlockSpec(memory_space=pltpu.SMEM)]
        + [pl.BlockSpec(memory_space=pltpu.HBM)] * 2,
        out_specs=(vmem(), vmem()),
        scratch_shapes=[pltpu.SemaphoreType.DMA((6,))],
        compiler_params=params(),
        name="shard",
    )(at, in_hbm(proj_in), in_hbm(proj_out))


def crossed(part):
    return moved(part, lambda x, h, c, d, y: (x, 1 - h, c, ZLO - 1 - d, y))


def from_next(value):
    return moved(value, lambda x, h, c, d, y: ((x + XS - 1) % XS, h, c, d, y))


def from_last(value):
    return moved(value, lambda x, h, c, d, y: ((x + 1) % XS, h, c, d, y))


def along_x(shard):
    half = shard.shape[0] // 2
    plus, minus = from_next(shard), from_last(shard)
    near = jnp.concatenate([shard, plus, minus], axis=0)
    opposite = jnp.concatenate([from_next(plus[:half]), from_last(minus[half:])], axis=0)
    return near, opposite


def swapped(value):
    return moved(value, lambda x, h, c, d, y: (x, h, 1 - c, d, y))


def neighbours(up, down):
    count = lax.axis_size("rows")
    forward = [(i, i + 1) for i in range(count - 1)]
    backward = [(b, a) for a, b in forward]
    return lax.ppermute(up, "rows", backward), lax.ppermute(down, "rows", forward)


def shards(
    features,
    norm_gain,
    norm_bias,
    conv_weight,
    embed_weight,
    embed_bias,
    proj_in,
    proj_in_bias,
    proj_out,
    proj_out_bias,
    targets,
):
    images, height, across, channels = features.shape
    width, align = embed_weight.shape[1], proj_out.shape[1]
    peers = lax.axis_size("rows")
    members = peers * height * across * (channels // GROUPS)
    flat = features.reshape(images, height * across, channels)
    gain, bias = norm_gain.reshape(1, channels), norm_bias.reshape(1, channels)
    rows, batch = lax.axis_index("rows"), lax.axis_index("batch")
    at = jnp.stack([(rows // CORES) % ZHI, rows % CORES, batch % YS, batch // YS, rows // (ZHI * CORES)])
    at = at.astype(jnp.int32)
    shard, part = shard_of(at, proj_in, proj_out)
    own_near, own_far = along_x(shard)
    taps = conv_weight.reshape(LATENT, TAPS, channels).transpose(1, 0, 2)
    taps = jnp.pad(taps, ((0, 0), (0, SUB - LATENT), (0, 0))).reshape(TAPS * SUB, channels)
    taps_full = jnp.pad(taps, ((0, LANES - TAPS * SUB), (0, 0)))

    sums = group_stats(flat, peers)
    stats = lax.all_to_all(sums, "rows", 0, 0, tiled=True)
    cross, stats = lax.optimization_barrier((crossed(part), stats))
    cross = jnp.broadcast_to(cross[None], (XS * YS, *cross.shape))
    cross = exchanged(cross, SHEET).reshape(-1, shard.shape[1])
    lat, up, down, mean, inv = conv_forward(stats, flat, gain, bias, taps, across, members)
    above, below = neighbours(up, down)
    cross, own_near, own_far, above, below = lax.optimization_barrier((cross, own_near, own_far, above, below))
    pieces = [own_near, own_far, cross]
    pieces = pieces + [swapped(v) for v in pieces]
    target = targets.reshape(-1, align)
    embed_part, grad_lat = projector(
        at, lat, below, above, target, embed_weight, embed_bias.reshape(1, -1),
        proj_in_bias.reshape(1, -1), proj_out_bias.reshape(1, -1), pieces, across,
    )
    after, before = neighbours(grad_lat, grad_lat)
    send, grad_shift = conv_backward(
        grad_lat, before, after, flat, mean, inv, gain, bias, taps_full, embed_part, across
    )
    plane = exchanged(send, PLANE)
    column = exchanged(plane_total(at, plane), COLUMN)
    chunks, got = column_total(at, column)
    everything = exchanged(chunks, PLANE)
    grad_features = feature_grad(got, flat, mean, inv, gain, grad_shift, members)
    grad_conv, grad_gain, grad_bias, grad_embed = unpack(everything, channels, width)
    return (
        grad_features.reshape(features.shape),
        grad_conv,
        grad_gain.reshape(channels),
        grad_bias.reshape(channels),
        grad_embed,
    )


def solution(mesh):
    in_specs = (
        P("batch", "rows", None, None),
        P(),
        P(),
        P(),
        P(),
        P(),
        P("rows", None),
        P(),
        P("rows", None),
        P(),
        P("batch", "rows", None, None),
    )
    out_specs = (P("batch", "rows", None, None), P(), P(), P(), P())
    return jax.shard_map(shards, mesh=mesh, in_specs=in_specs, out_specs=out_specs, check_vma=False)
```

```python
import jax
import jax.numpy as jnp
from jax import lax
from jax.experimental import pallas as pl
from jax.experimental.pallas import tpu as pltpu
from jax.sharding import PartitionSpec as P

GROUPS = 32
LATENT = 4
PATCH = 2
EPS_NORM = 1e-06
EPS_UNIT = 1e-06

XS, ZHI, CORES, ZLO, YS = 4, 2, 2, 8, 4

HIGH = lax.Precision.HIGHEST
F32 = jnp.float32
BF16 = jnp.bfloat16
TAPS = 9
SUB = 8
LANES = 128
STAT_ROWS = 16
CHUNKS, CHUNK_ROWS, ALL_ROWS = 32, 16, 32
CONV_COST = 20_000_000_000
PART = 16


def params(limit_mb=12):
    return pltpu.CompilerParams(vmem_limit_bytes=limit_mb << 20)


def vmem():
    return pl.BlockSpec(memory_space=pltpu.VMEM)


def in_hbm(v):
    return pltpu.with_memory_space_constraint(v, pltpu.HBM)


def sigmoid(v):
    return 0.5 + 0.5 * jnp.tanh(0.5 * v)


def nt(a, b, precision=None):
    return lax.dot_general(
        a, b, (((1,), (1,)), ((), ())), preferred_element_type=F32, precision=precision
    )


def nn(a, b, precision=None):
    return lax.dot_general(
        a, b, (((1,), (0,)), ((), ())), preferred_element_type=F32, precision=precision
    )


def iota(shape, dim):
    return lax.broadcasted_iota(jnp.int32, shape, dim)


def to_groups(channels, per_group, offset):
    shape = (channels, LANES)
    return (iota(shape, 0) // per_group + offset == iota(shape, 1)).astype(F32)


def from_groups(channels, per_group, offset):
    shape = (LANES, channels)
    return (iota(shape, 1) // per_group + offset == iota(shape, 0)).astype(F32)


def pack_stats(total):
    lane = iota((SUB, LANES), 1)
    return jnp.where(lane < LANES // 2, total[:SUB], pltpu.roll(total[SUB:], LANES // 2, 1))


def unpack_stats(packed):
    return jnp.concatenate([packed, pltpu.roll(packed, LANES // 2, 1)], axis=0)


def parts(v):
    top = v.astype(BF16)
    return top, (v - top.astype(F32)).astype(BF16)


def halves(packed):
    top = packed.astype(BF16).astype(F32)
    return jnp.concatenate([top, packed - top], axis=0).astype(BF16)


def stats_kernel(f_ref, out_ref, sums, squares):
    images, _, channels = f_ref.shape
    sums[...] = jnp.zeros_like(sums)
    squares[...] = jnp.zeros_like(squares)
    for i in range(images):
        v = f_ref[i].astype(F32)
        sums[i : i + 1, :] = jnp.sum(v, axis=0, keepdims=True)
        squares[i : i + 1, :] = jnp.sum(v * v, axis=0, keepdims=True)
    per_group = channels // GROUPS
    total = nn(sums[...], to_groups(channels, per_group, 0), HIGH) + nn(
        squares[...], to_groups(channels, per_group, GROUPS), HIGH
    )
    packed = pack_stats(total)
    for r in range(out_ref.shape[0]):
        out_ref[r] = packed


def group_stats(features, peers):
    channels = features.shape[-1]
    return pl.pallas_call(
        stats_kernel,
        out_shape=jax.ShapeDtypeStruct((peers, SUB, LANES), F32),
        in_specs=[vmem()],
        out_specs=vmem(),
        scratch_shapes=[pltpu.VMEM((STAT_ROWS, channels), F32)] * 2,
        compiler_params=params(),
        name="stats",
    )(features)


def lane_masks(shape, across):
    lane = iota(shape, 1)
    return lane % across, (lane // across) % 2


def roll(v, shift):
    return pltpu.roll(v, shift % v.shape[1], 1)


def conv_kernel(
    across, members, at_ref, st_ref, f_ref, gain_ref, bias_ref, k_ref,
    lat_ref, far_ref, near_ref, mean_ref, inv_ref, act,
):
    images, cells, channels = f_ref.shape
    per_group = channels // GROUPS
    total = unpack_stats(jnp.sum(st_ref[...], axis=0))
    mean = nn(total, from_groups(channels, per_group, 0), HIGH) * (1.0 / members)
    square = nn(total, from_groups(channels, per_group, GROUPS), HIGH) * (1.0 / members)
    inv = lax.rsqrt(jnp.maximum(square - mean * mean, 0.0) + EPS_NORM)
    mean_ref[...] = mean
    inv_ref[...] = inv
    gain, bias = gain_ref[...], bias_ref[...]
    for i in range(images):
        v = f_ref[i].astype(F32)
        shifted = (v - mean[i : i + 1]) * inv[i : i + 1] * gain + bias
        act[i * cells : (i + 1) * cells, :] = (shifted * sigmoid(shifted)).astype(BF16)
    taps = nt(k_ref[...], act[...])
    shape = (SUB, images * cells)
    col, row = lane_masks(shape, across)

    def tap(position):
        return taps[position * SUB : (position + 1) * SUB]

    def line(dy):
        low = jnp.where(col > 0, roll(tap(3 * dy), 1), 0.0)
        high = jnp.where(col < across - 1, roll(tap(3 * dy + 2), -1), 0.0)
        return tap(3 * dy + 1) + low + high

    first, middle, last = line(0), line(1), line(2)
    last_up, first_down = roll(last, -across), roll(first, across)
    lat_ref[...] = middle + jnp.where(row == 0, last_up, first_down)
    up = jnp.where(row == 1, roll(last, across), 0.0)
    down = jnp.where(row == 0, roll(first, -across), 0.0)
    upper = at_ref[1] == 1
    far_ref[...] = jnp.where(upper, down, up)
    near_ref[...] = jnp.where(upper, up, down)


def conv_forward(at, stats, features, gain, bias, kernel_rows, across, members):
    images, cells, channels = features.shape
    line = jax.ShapeDtypeStruct((SUB, images * cells), F32)
    stat = jax.ShapeDtypeStruct((STAT_ROWS, channels), F32)
    return pl.pallas_call(
        lambda *refs: conv_kernel(across, members, *refs),
        out_shape=(line, line, line, stat, stat),
        in_specs=[pl.BlockSpec(memory_space=pltpu.SMEM)] + [vmem()] * 5,
        out_specs=(vmem(),) * 5,
        scratch_shapes=[pltpu.VMEM((images * cells, channels), BF16)],
        compiler_params=params(),
        cost_estimate=pl.CostEstimate(
            flops=CONV_COST, bytes_accessed=features.size * 2, transcendentals=features.size
        ),
        name="conv",
    )(at, stats, features, gain, bias, kernel_rows)


def mlp_kernel(
    across, width, hidden, align, at_ref, lat_ref, below_ref, above_ref, target_ref,
    ew_ref, eb_ref, pib_ref, pob_ref,
    own_near, own_far, cross, own_near_other, own_far_other, cross_other,
    embed_ref, gl_ref, w_in, w_out, pre, emb, acc, grad_emb, wanted, sems,
):
    zhi, core, x = at_ref[0], at_ref[1], at_ref[4]
    depth = width // (XS * ZHI * CORES)
    slab = hidden // (XS * ZHI * CORES)
    taken = PATCH * PATCH
    rows = taken * SUB
    copies = [pltpu.make_async_copy(target_ref, wanted, sems.at[0])]
    copies[0].start()

    def place(piece, at, source_x, of_zhi, of_core, begin=0, size=depth):
        shard = lax.rem(source_x, XS) * (ZHI * CORES) + of_zhi * CORES + of_core
        lines = pl.ds(at, size)

        def put(columns, into):
            copy = pltpu.make_async_copy(piece.at[lines, columns], into, sems.at[len(copies)])
            copy.start()
            copies.append(copy)

        line = pl.multiple_of(shard * depth + begin, size)
        put(pl.ds(0, hidden), w_in.at[pl.ds(line, size), :])
        for part in range(slab // depth):
            line = pl.multiple_of(shard * slab + part * depth + begin, size)
            put(pl.ds(hidden + part * align, align), w_out.at[pl.ds(line, size), :])

    half = depth // 2
    for near, opposite, far, of_core in (
        (own_near, own_far, cross, core),
        (own_near_other, own_far_other, cross_other, 1 - core),
    ):
        for k, step in enumerate((0, 1, XS - 1)):
            place(near, k * depth, x + step, zhi, of_core)
        for begin in (0, half):
            place(opposite, begin, x + 2, zhi, of_core, begin, half)
        for k in range(XS):
            place(far, k * depth, k, 1 - zhi, of_core)

    lat = lat_ref[...] + below_ref[...] + above_ref[...]
    top = lat.astype(BF16)
    rest = lat - top.astype(F32)
    mid = rest.astype(BF16)
    low_part = (rest - mid.astype(F32)).astype(BF16)
    split = jnp.concatenate(
        [top.astype(F32), mid.astype(F32), low_part.astype(F32)], axis=0
    ).astype(BF16)
    cells = lat.shape[1]
    tokens = target_ref.shape[0]
    room = 256
    cols = across // PATCH

    def selection(u, v):
        shape = (cells, room)
        token = iota(shape, 1)
        lane = (token // cols) * (PATCH * across) + u * across + (token % cols) * PATCH + v
        return jnp.where((lane == iota(shape, 0)) & (token < tokens), 1.0, 0.0).astype(BF16)

    picks = [selection(u, v) for u in range(PATCH) for v in range(PATCH)]
    lines = []
    for pick in picks:
        got = nn(split, pick)
        lines.append(got[0:SUB] + got[SUB : 2 * SUB] + got[2 * SUB :])
    patches_t = jnp.concatenate(lines, axis=0)
    patches = patches_t.T
    empty = jnp.zeros((SUB - LATENT, width), F32)
    spread = []
    for k in range(taken):
        spread += [ew_ref[k * LATENT : (k + 1) * LATENT, :], empty]
    ew_top, ew_low = parts(jnp.concatenate(spread, axis=0))
    p_top, p_low = parts(patches[:tokens])
    embedded = nn(p_top, ew_top) + nn(p_low, ew_top) + nn(p_top, ew_low)
    emb[...] = (embedded + eb_ref[...]).astype(BF16)

    for copy in copies:
        copy.wait()

    step = 1024
    acc[...] = jnp.zeros_like(acc)

    for tile in range(hidden // step):
        at = pl.ds(pl.multiple_of(tile * step, step), step)
        h = nn(emb[...], w_in[:, at]) + pib_ref[:, at]
        pre[:, at] = h
        acc[...] += nn((h * sigmoid(h)).astype(BF16), w_out[at, :])

    projected = acc[...] + pob_ref[...]
    target = wanted[...].astype(F32)
    unit_target = target * lax.rsqrt(jnp.sum(target * target, axis=1, keepdims=True) + EPS_UNIT)
    inv_len = lax.rsqrt(jnp.sum(projected * projected, axis=1, keepdims=True) + EPS_UNIT)
    unit_proj = projected * inv_len
    cosine = jnp.sum(unit_proj * unit_target, axis=1, keepdims=True)
    grad_out = (-inv_len * (unit_target - cosine * unit_proj)).astype(BF16)
    grad_emb[...] = jnp.zeros_like(grad_emb)

    for tile in range(hidden // step):
        at = pl.ds(pl.multiple_of(tile * step, step), step)
        back = nt(grad_out, w_out[at, :])
        h = pre[:, at]
        sig = sigmoid(h)
        grad_hidden = (back * (sig * (1.0 + h * (1.0 - sig)))).astype(BF16)
        grad_emb[0:tokens, :] += nt(grad_hidden, w_in[:, at])

    grad = grad_emb[...]
    g_top, g_low = parts(grad)
    t_top, t_low = parts(patches_t)
    both = nn(jnp.concatenate([t_top, t_low], axis=0), g_top)
    embed_ref[...] = both[:rows] + both[rows:] + nn(t_top, g_low)
    both = nt(jnp.concatenate([ew_top, ew_low], axis=0), g_top)
    grad_patch = both[:rows] + both[rows:] + nt(ew_top, g_low)
    total = jnp.zeros((SUB, cells), F32)
    for position, pick in enumerate(picks):
        part = grad_patch[position * SUB : (position + 1) * SUB].astype(BF16)
        total = total + nt(part, pick)
    gl_ref[...] = total


def projector(at, lat, below, above, target, ew, eb, pib, pob, pieces, across):
    rows, width = PATCH * PATCH * SUB, ew.shape[1]
    hidden, align = pib.shape[1], pob.shape[1]
    tokens = target.shape[0]
    flops = 2 * tokens * (2 * width * hidden + 2 * hidden * align)
    return pl.pallas_call(
        lambda *refs: mlp_kernel(across, width, hidden, align, *refs),
        out_shape=(
            jax.ShapeDtypeStruct((rows, width), F32),
            jax.ShapeDtypeStruct(lat.shape, F32),
        ),
        in_specs=[pl.BlockSpec(memory_space=pltpu.SMEM)]
        + [vmem()] * 3
        + [pl.BlockSpec(memory_space=pltpu.HBM)]
        + [vmem()] * 4
        + [pl.BlockSpec(memory_space=pltpu.HBM)] * len(pieces),
        out_specs=(vmem(), vmem()),
        scratch_shapes=[
            pltpu.VMEM((width, hidden), BF16),
            pltpu.VMEM((hidden, align), BF16),
            pltpu.VMEM((tokens, hidden), F32),
            pltpu.VMEM((tokens, width), BF16),
            pltpu.VMEM((tokens, align), F32),
            pltpu.VMEM((256, width), F32),
            pltpu.VMEM((tokens, align), BF16),
            pltpu.SemaphoreType.DMA((55,)),
        ],
        compiler_params=params(32),
        cost_estimate=pl.CostEstimate(
            flops=flops, bytes_accessed=8 << 20, transcendentals=2 * tokens * hidden
        ),
        name="projector",
    )(at, lat, below, above, in_hbm(target), ew, eb, pib, pob, in_hbm(pieces[0]), *pieces[1:])


def back_kernel(
    across, at_ref, gl_ref, far_ref, near_ref, f_ref, mean_ref, inv_ref, gain_ref, bias_ref,
    k_ref, embed_ref, send_ref, gs_ref, act, grads_t, by_bias, by_gain, pack,
):
    images, cells, channels = f_ref.shape
    per_group = channels // GROUPS
    gl, far, near = gl_ref[...], far_ref[...], near_ref[...]
    upper = at_ref[1] == 1
    before, after = jnp.where(upper, near, far), jnp.where(upper, far, near)
    col, row = lane_masks(gl.shape, across)
    lines = (
        jnp.where(row == 0, roll(gl, -across), roll(after, across)),
        gl,
        jnp.where(row == 0, roll(before, -across), roll(gl, across)),
    )
    parts = []
    for g in lines:
        parts.append(jnp.where(col < across - 1, roll(g, -1), 0.0))
        parts.append(g)
        parts.append(jnp.where(col > 0, roll(g, 1), 0.0))
    parts.append(jnp.zeros((LANES - TAPS * SUB, gl.shape[1]), F32))
    grads = jnp.concatenate(parts, axis=0)
    grads_t[...] = grads.T.astype(BF16)
    gain, bias = gain_ref[...], bias_ref[...]
    by_bias[...] = jnp.zeros_like(by_bias)
    by_gain[...] = jnp.zeros_like(by_gain)
    for i in range(images):
        at = slice(i * cells, (i + 1) * cells)
        v = f_ref[i].astype(F32)
        normed = (v - mean_ref[i : i + 1, :]) * inv_ref[i : i + 1, :]
        shifted = normed * gain + bias
        sig = sigmoid(shifted)
        act[at, :] = (shifted * sig).astype(BF16)
        grad_active = nn(grads_t[at, :], k_ref[...])
        gs = grad_active * (sig * (1.0 + shifted * (1.0 - sig)))
        gs_ref[i] = gs
        by_bias[i : i + 1, :] = jnp.sum(gs, axis=0, keepdims=True)
        by_gain[i : i + 1, :] = jnp.sum(gs * normed, axis=0, keepdims=True)
    conv = nn(grads.astype(BF16), act[...])
    stat = nn(by_bias[...] * gain, to_groups(channels, per_group, 0), HIGH) + nn(
        by_gain[...] * gain, to_groups(channels, per_group, GROUPS), HIGH
    )
    bias_part = jnp.sum(by_bias[...], axis=0, keepdims=True)
    gain_part = jnp.sum(by_gain[...], axis=0, keepdims=True)
    packed = halves(pack_stats(stat))
    for r in range(CHUNKS):
        send_ref[r, CHUNK_ROWS:ALL_ROWS, :] = packed
    blocks = channels // LANES
    half = CHUNKS // 2
    pack[...] = jnp.zeros_like(pack)
    for r in range(half):
        block, latent = r // LATENT, r % LATENT
        lanes = slice(block * LANES, (block + 1) * LANES)
        for position in range(TAPS):
            line = position * SUB + latent
            pack[r, position : position + 1, :] = conv[line : line + 1, lanes]
        lanes = slice((r // 2) * LANES, (r // 2 + 1) * LANES)
        for part in range(2):
            line = (r % 2) * 2 * SUB + part * SUB
            pack[half + r, part * LATENT : (part + 1) * LATENT, :] = embed_ref[
                line : line + LATENT, lanes
            ]
        if r < 2 * blocks:
            one = gain_part if r < blocks else bias_part
            lanes = slice((r % blocks) * LANES, (r % blocks + 1) * LANES)
            pack[half + r, SUB : SUB + 1, :] = one[:, lanes]
    for r in range(CHUNKS):
        send_ref[r, 0:CHUNK_ROWS, :] = pack[r].astype(BF16)


def conv_backward(at, gl, far, near, features, mean, inv, gain, bias, kernel_rows, embed, across):
    images, cells, channels = features.shape
    return pl.pallas_call(
        lambda *refs: back_kernel(across, *refs),
        out_shape=(
            jax.ShapeDtypeStruct((CHUNKS, ALL_ROWS, LANES), BF16),
            jax.ShapeDtypeStruct((images, cells, channels), F32),
        ),
        in_specs=[pl.BlockSpec(memory_space=pltpu.SMEM)] + [vmem()] * 10,
        out_specs=(vmem(),) * 2,
        scratch_shapes=[
            pltpu.VMEM((images * cells, channels), BF16),
            pltpu.VMEM((images * cells, LANES), BF16),
            pltpu.VMEM((STAT_ROWS, channels), F32),
            pltpu.VMEM((STAT_ROWS, channels), F32),
            pltpu.VMEM((CHUNKS, CHUNK_ROWS, LANES), F32),
        ],
        compiler_params=params(),
        name="back",
    )(at, gl, far, near, features, mean, inv, gain, bias, kernel_rows, embed)


def last_kernel(members, got_ref, f_ref, mean_ref, inv_ref, gain_ref, gs_ref, out_ref):
    images, _, channels = f_ref.shape
    per_group = channels // GROUPS
    total = unpack_stats(got_ref[...])
    first = nn(total, from_groups(channels, per_group, 0), HIGH) * (1.0 / members)
    second = nn(total, from_groups(channels, per_group, GROUPS), HIGH) * (1.0 / members)
    gain = gain_ref[...]
    for i in range(images):
        v = f_ref[i].astype(F32)
        inv = inv_ref[i : i + 1, :]
        normed = (v - mean_ref[i : i + 1, :]) * inv
        out = inv * (gs_ref[i] * gain - first[i : i + 1] - normed * second[i : i + 1])
        out_ref[i] = out.astype(BF16)


def feature_grad(got, features, mean, inv, gain, grad_shift, members):
    return pl.pallas_call(
        lambda *refs: last_kernel(members, *refs),
        out_shape=jax.ShapeDtypeStruct(features.shape, BF16),
        in_specs=[vmem()] * 6,
        out_specs=vmem(),
        compiler_params=params(),
        cost_estimate=pl.CostEstimate(
            flops=10 * features.size, bytes_accessed=8 * features.size, transcendentals=0
        ),
        name="last",
    )(got, features, mean, inv, gain, grad_shift)


def plane_kernel(at_ref, got_ref, out_ref):
    chunk = jnp.zeros((CHUNK_ROWS, LANES), F32)
    stat = jnp.zeros((SUB, LANES), F32)
    for r in range(CHUNKS):
        chunk = chunk + got_ref[r, 0:CHUNK_ROWS, :].astype(F32)
        pair = got_ref[r, CHUNK_ROWS:ALL_ROWS, :].astype(F32)
        stat = stat + jnp.where(at_ref[2] == (r // CORES) % YS, pair[:SUB] + pair[SUB:], 0.0)
    chunk, stat = chunk.astype(BF16), halves(stat)
    for r in range(out_ref.shape[0]):
        out_ref[r, 0:CHUNK_ROWS, :] = chunk
        out_ref[r, CHUNK_ROWS:ALL_ROWS, :] = stat


def plane_total(at, got):
    return pl.pallas_call(
        plane_kernel,
        out_shape=jax.ShapeDtypeStruct((ZHI * ZLO, ALL_ROWS, LANES), BF16),
        in_specs=[pl.BlockSpec(memory_space=pltpu.SMEM), vmem()],
        out_specs=vmem(),
        compiler_params=params(),
        name="plane",
    )(at, got)


def column_kernel(at_ref, got_ref, out_ref, stat_ref):
    chunk = jnp.zeros((CHUNK_ROWS, LANES), F32)
    stat = jnp.zeros((SUB, LANES), F32)
    for r in range(ZHI * ZLO):
        chunk = chunk + got_ref[r, 0:CHUNK_ROWS, :].astype(F32)
        pair = got_ref[r, CHUNK_ROWS:ALL_ROWS, :].astype(F32)
        stat = stat + jnp.where(at_ref[3] == r % ZLO, pair[:SUB] + pair[SUB:], 0.0)
    chunk = chunk.astype(BF16)
    for r in range(out_ref.shape[0]):
        out_ref[r] = chunk
    stat_ref[...] = stat


def column_total(at, got):
    return pl.pallas_call(
        column_kernel,
        out_shape=(
            jax.ShapeDtypeStruct((CHUNKS, CHUNK_ROWS, LANES), BF16),
            jax.ShapeDtypeStruct((SUB, LANES), F32),
        ),
        in_specs=[pl.BlockSpec(memory_space=pltpu.SMEM), vmem()],
        out_specs=(vmem(), vmem()),
        compiler_params=params(),
        name="column",
    )(at, got)


def unpack_kernel(got_ref, conv_ref, gain_ref, bias_ref, embed_ref, wide):
    channels = gain_ref.shape[1]
    blocks = channels // LANES
    half = CHUNKS // 2
    wide[...] = got_ref[...].astype(F32)
    for r in range(half):
        block, latent = r // LATENT, r % LATENT
        for position in range(TAPS):
            at = position * channels + block * LANES
            conv_ref[latent : latent + 1, at : at + LANES] = wide[r, position : position + 1, :]
        lanes = slice((r // 2) * LANES, (r // 2 + 1) * LANES)
        line = (r % 2) * SUB
        embed_ref[line : line + SUB, lanes] = wide[half + r, 0:SUB, :]
        lanes = slice((r % blocks) * LANES, (r % blocks + 1) * LANES)
        if r < blocks:
            gain_ref[:, lanes] = wide[half + r, SUB : SUB + 1, :]
        elif r < 2 * blocks:
            bias_ref[:, lanes] = wide[half + r, SUB : SUB + 1, :]


def unpack(got, channels, width):
    return pl.pallas_call(
        unpack_kernel,
        out_shape=(
            jax.ShapeDtypeStruct((LATENT, TAPS * channels), F32),
            jax.ShapeDtypeStruct((1, channels), F32),
            jax.ShapeDtypeStruct((1, channels), F32),
            jax.ShapeDtypeStruct((PATCH * PATCH * LATENT, width), F32),
        ),
        in_specs=[vmem()],
        out_specs=(vmem(),) * 4,
        scratch_shapes=[pltpu.VMEM(got.shape, F32)],
        compiler_params=params(),
        name="unpack",
    )(got)


def device(x, zhi, core, zlo, y):
    return ((x * ZHI + zhi) * CORES + core) * (ZLO * YS) + zlo * YS + y


BOTH = ("rows", "batch")
PLANE = [
    [device(x, h, c, d, y) for x in range(XS) for y in range(YS) for c in range(CORES)]
    for h in range(ZHI)
    for d in range(ZLO)
]
SHEET = [
    [device(x, h, c, d, y) for x in range(XS) for y in range(YS)]
    for h in range(ZHI)
    for d in range(ZLO)
    for c in range(CORES)
]
COLUMN = [
    [device(x, h, c, d, y) for h in range(ZHI) for d in range(ZLO)]
    for x in range(XS)
    for y in range(YS)
    for c in range(CORES)
]


def exchanged(value, groups):
    return lax.all_to_all(value, BOTH, 0, 0, axis_index_groups=groups, tiled=True)


def moved(value, where):
    pairs = []
    for x in range(XS):
        for zhi in range(ZHI):
            for core in range(CORES):
                for zlo in range(ZLO):
                    for y in range(YS):
                        a, b, c, d, e = where(x, zhi, core, zlo, y)
                        pairs.append((device(x, zhi, core, zlo, y), device(a, b, c, d, e)))
    return lax.ppermute(value, ("rows", "batch"), pairs)


def shard_kernel(at_ref, in_ref, out_ref, shard_ref, part_ref, sems):
    depth, hidden = in_ref.shape
    align = out_ref.shape[1]
    size = part_ref.shape[0]
    begin = pl.multiple_of(at_ref[2] * size, size)
    copies = []

    def put(source, lines, into, columns):
        copy = pltpu.make_async_copy(
            source.at[lines], into.at[:, columns], sems.at[len(copies)]
        )
        copy.start()
        copies.append(copy)

    for into, first, count in ((part_ref, begin, size), (shard_ref, 0, depth)):
        put(in_ref, pl.ds(first, count), into, pl.ds(0, hidden))
        for part in range(out_ref.shape[0] // depth):
            lines = pl.ds(part * depth + first, count)
            put(out_ref, lines, into, pl.ds(hidden + part * align, align))
    for copy in copies:
        copy.wait()


def shard_of(at, proj_in, proj_out):
    depth, hidden = proj_in.shape
    columns = hidden + proj_out.size // depth
    return pl.pallas_call(
        shard_kernel,
        out_shape=(
            jax.ShapeDtypeStruct((depth, columns), BF16),
            jax.ShapeDtypeStruct((depth // YS, columns), BF16),
        ),
        in_specs=[pl.BlockSpec(memory_space=pltpu.SMEM)]
        + [pl.BlockSpec(memory_space=pltpu.HBM)] * 2,
        out_specs=(vmem(), vmem()),
        scratch_shapes=[pltpu.SemaphoreType.DMA((6,))],
        compiler_params=params(),
        name="shard",
    )(at, in_hbm(proj_in), in_hbm(proj_out))


def crossed(part):
    return moved(part, lambda x, h, c, d, y: (x, 1 - h, c, ZLO - 1 - d, y))


def from_next(value):
    return moved(value, lambda x, h, c, d, y: ((x + XS - 1) % XS, h, c, d, y))


def from_last(value):
    return moved(value, lambda x, h, c, d, y: ((x + 1) % XS, h, c, d, y))


def along_x(shard):
    half = shard.shape[0] // 2
    plus, minus = from_next(shard), from_last(shard)
    near = jnp.concatenate([shard, plus, minus], axis=0)
    opposite = jnp.concatenate([from_next(plus[:half]), from_last(minus[half:])], axis=0)
    return near, opposite


def swapped(value):
    return moved(value, lambda x, h, c, d, y: (x, h, 1 - c, d, y))


def neighbours(far, near):
    count = lax.axis_size("rows")
    pairs = [(r, r + 1) for r in range(1, count - 1, 2)]
    pairs = pairs + [(b, a) for a, b in pairs]
    inside = [(r, r ^ 1) for r in range(count)]
    return lax.ppermute(far, "rows", pairs), lax.ppermute(near, "rows", inside)


def shards(
    features,
    norm_gain,
    norm_bias,
    conv_weight,
    embed_weight,
    embed_bias,
    proj_in,
    proj_in_bias,
    proj_out,
    proj_out_bias,
    targets,
):
    images, height, across, channels = features.shape
    width, align = embed_weight.shape[1], proj_out.shape[1]
    peers = lax.axis_size("rows")
    members = peers * height * across * (channels // GROUPS)
    flat = features.reshape(images, height * across, channels)
    gain, bias = norm_gain.reshape(1, channels), norm_bias.reshape(1, channels)
    rows, batch = lax.axis_index("rows"), lax.axis_index("batch")
    at = jnp.stack([(rows // CORES) % ZHI, rows % CORES, batch % YS, batch // YS, rows // (ZHI * CORES)])
    at = at.astype(jnp.int32)
    shard, part = shard_of(at, proj_in, proj_out)
    own_near, own_far = along_x(shard)
    taps = conv_weight.reshape(LATENT, TAPS, channels).transpose(1, 0, 2)
    taps = jnp.pad(taps, ((0, 0), (0, SUB - LATENT), (0, 0))).reshape(TAPS * SUB, channels)
    taps_full = jnp.pad(taps, ((0, LANES - TAPS * SUB), (0, 0)))

    flat, part = lax.optimization_barrier((flat, part))
    sums = group_stats(flat, peers)
    stats = lax.all_to_all(sums, "rows", 0, 0, tiled=True)
    cross, stats = lax.optimization_barrier((crossed(part), stats))
    cross = jnp.broadcast_to(cross[None], (XS * YS, *cross.shape))
    cross = exchanged(cross, SHEET).reshape(-1, shard.shape[1])
    lat, far, near, mean, inv = conv_forward(at, stats, flat, gain, bias, taps, across, members)
    above, below = neighbours(far, near)
    cross, own_near, own_far, above, below = lax.optimization_barrier((cross, own_near, own_far, above, below))
    pieces = [own_near, own_far, cross]
    pieces = pieces + [swapped(v) for v in pieces]
    target = targets.reshape(-1, align)
    embed_part, grad_lat = projector(
        at, lat, below, above, target, embed_weight, embed_bias.reshape(1, -1),
        proj_in_bias.reshape(1, -1), proj_out_bias.reshape(1, -1), pieces, across,
    )
    far, near = neighbours(grad_lat, grad_lat)
    send, grad_shift = conv_backward(
        at, grad_lat, far, near, flat, mean, inv, gain, bias, taps_full, embed_part, across
    )
    plane = exchanged(send, PLANE)
    column = exchanged(plane_total(at, plane), COLUMN)
    chunks, got = column_total(at, column)
    everything = exchanged(chunks, PLANE)
    grad_features = feature_grad(got, flat, mean, inv, gain, grad_shift, members)
    grad_conv, grad_gain, grad_bias, grad_embed = unpack(everything, channels, width)
    return (
        grad_features.reshape(features.shape),
        grad_conv,
        grad_gain.reshape(channels),
        grad_bias.reshape(channels),
        grad_embed,
    )


def solution(mesh):
    in_specs = (
        P("batch", "rows", None, None),
        P(),
        P(),
        P(),
        P(),
        P(),
        P("rows", None),
        P(),
        P("rows", None),
        P(),
        P("batch", "rows", None, None),
    )
    out_specs = (P("batch", "rows", None, None), P(), P(), P(), P())
    return jax.shard_map(shards, mesh=mesh, in_specs=in_specs, out_specs=out_specs, check_vma=False)
```

```python
import jax
import jax.numpy as jnp
from jax import lax
from jax.experimental import pallas as pl
from jax.experimental.pallas import tpu as pltpu
from jax.sharding import PartitionSpec as P

GROUPS = 32
LATENT = 4
PATCH = 2
EPS_NORM = 1e-06
EPS_UNIT = 1e-06

XS, ZHI, CORES, ZLO, YS = 4, 2, 2, 8, 4

HIGH = lax.Precision.HIGHEST
F32 = jnp.float32
BF16 = jnp.bfloat16
TAPS = 9
SUB = 8
LANES = 128
STAT_ROWS = 16
CHUNKS, CHUNK_ROWS, ALL_ROWS = 32, 16, 32
CONV_COST = 20_000_000_000
PART = 16


def params(limit_mb=12):
    return pltpu.CompilerParams(vmem_limit_bytes=limit_mb << 20)


def vmem():
    return pl.BlockSpec(memory_space=pltpu.VMEM)


def in_hbm(v):
    return pltpu.with_memory_space_constraint(v, pltpu.HBM)


def sigmoid(v):
    return 0.5 + 0.5 * jnp.tanh(0.5 * v)


def nt(a, b, precision=None):
    return lax.dot_general(
        a, b, (((1,), (1,)), ((), ())), preferred_element_type=F32, precision=precision
    )


def nn(a, b, precision=None):
    return lax.dot_general(
        a, b, (((1,), (0,)), ((), ())), preferred_element_type=F32, precision=precision
    )


def iota(shape, dim):
    return lax.broadcasted_iota(jnp.int32, shape, dim)


def to_groups(channels, per_group, offset):
    shape = (channels, LANES)
    return (iota(shape, 0) // per_group + offset == iota(shape, 1)).astype(F32)


def from_groups(channels, per_group, offset):
    shape = (LANES, channels)
    return (iota(shape, 1) // per_group + offset == iota(shape, 0)).astype(F32)


def pack_stats(total):
    lane = iota((SUB, LANES), 1)
    return jnp.where(lane < LANES // 2, total[:SUB], pltpu.roll(total[SUB:], LANES // 2, 1))


def unpack_stats(packed):
    return jnp.concatenate([packed, pltpu.roll(packed, LANES // 2, 1)], axis=0)


def parts(v):
    top = v.astype(BF16)
    return top, (v - top.astype(F32)).astype(BF16)


def halves(packed):
    top = packed.astype(BF16).astype(F32)
    return jnp.concatenate([top, packed - top], axis=0).astype(BF16)


def stats_kernel(f_ref, out_ref, sums, squares):
    images, _, channels = f_ref.shape
    sums[...] = jnp.zeros_like(sums)
    squares[...] = jnp.zeros_like(squares)
    for i in range(images):
        v = f_ref[i].astype(F32)
        sums[i : i + 1, :] = jnp.sum(v, axis=0, keepdims=True)
        squares[i : i + 1, :] = jnp.sum(v * v, axis=0, keepdims=True)
    per_group = channels // GROUPS
    total = nn(sums[...], to_groups(channels, per_group, 0), HIGH) + nn(
        squares[...], to_groups(channels, per_group, GROUPS), HIGH
    )
    packed = pack_stats(total)
    for r in range(out_ref.shape[0]):
        out_ref[r] = packed


def group_stats(features, peers):
    channels = features.shape[-1]
    return pl.pallas_call(
        stats_kernel,
        out_shape=jax.ShapeDtypeStruct((peers, SUB, LANES), F32),
        in_specs=[vmem()],
        out_specs=vmem(),
        scratch_shapes=[pltpu.VMEM((STAT_ROWS, channels), F32)] * 2,
        compiler_params=params(),
        name="stats",
    )(features)


def lane_masks(shape, across):
    lane = iota(shape, 1)
    return lane % across, (lane // across) % 2


def roll(v, shift):
    return pltpu.roll(v, shift % v.shape[1], 1)


def conv_kernel(
    across, members, at_ref, st_ref, f_ref, gain_ref, bias_ref, k_ref,
    lat_ref, far_ref, near_ref, mean_ref, inv_ref, act,
):
    images, cells, channels = f_ref.shape
    per_group = channels // GROUPS
    total = unpack_stats(jnp.sum(st_ref[...], axis=0))
    mean = nn(total, from_groups(channels, per_group, 0), HIGH) * (1.0 / members)
    square = nn(total, from_groups(channels, per_group, GROUPS), HIGH) * (1.0 / members)
    inv = lax.rsqrt(jnp.maximum(square - mean * mean, 0.0) + EPS_NORM)
    mean_ref[...] = mean
    inv_ref[...] = inv
    gain, bias = gain_ref[...], bias_ref[...]
    for i in range(images):
        v = f_ref[i].astype(F32)
        shifted = (v - mean[i : i + 1]) * inv[i : i + 1] * gain + bias
        act[i * cells : (i + 1) * cells, :] = (shifted * sigmoid(shifted)).astype(BF16)
    taps = nt(k_ref[...], act[...])
    shape = (SUB, images * cells)
    col, row = lane_masks(shape, across)

    def tap(position):
        return taps[position * SUB : (position + 1) * SUB]

    def line(dy):
        low = jnp.where(col > 0, roll(tap(3 * dy), 1), 0.0)
        high = jnp.where(col < across - 1, roll(tap(3 * dy + 2), -1), 0.0)
        return tap(3 * dy + 1) + low + high

    first, middle, last = line(0), line(1), line(2)
    last_up, first_down = roll(last, -across), roll(first, across)
    lat_ref[...] = middle + jnp.where(row == 0, last_up, first_down)
    up = jnp.where(row == 1, roll(last, across), 0.0)
    down = jnp.where(row == 0, roll(first, -across), 0.0)
    upper = at_ref[1] == 1
    far_ref[...] = jnp.where(upper, down, up)
    near_ref[...] = jnp.where(upper, up, down)


def conv_forward(at, stats, features, gain, bias, kernel_rows, across, members):
    images, cells, channels = features.shape
    line = jax.ShapeDtypeStruct((SUB, images * cells), F32)
    stat = jax.ShapeDtypeStruct((STAT_ROWS, channels), F32)
    return pl.pallas_call(
        lambda *refs: conv_kernel(across, members, *refs),
        out_shape=(line, line, line, stat, stat),
        in_specs=[pl.BlockSpec(memory_space=pltpu.SMEM)] + [vmem()] * 5,
        out_specs=(vmem(),) * 5,
        scratch_shapes=[pltpu.VMEM((images * cells, channels), BF16)],
        compiler_params=params(),
        cost_estimate=pl.CostEstimate(
            flops=CONV_COST, bytes_accessed=features.size * 2, transcendentals=features.size
        ),
        name="conv",
    )(at, stats, features, gain, bias, kernel_rows)


def mlp_kernel(
    across, width, hidden, align, at_ref, lat_ref, below_ref, above_ref, target_ref,
    ew_ref, eb_ref, pib_ref, pob_ref,
    own_near, own_far, cross, own_near_other, own_far_other, cross_other,
    embed_ref, gl_ref, w_in, w_out, pre, emb, acc, grad_emb, wanted, sems,
):
    zhi, core, x = at_ref[0], at_ref[1], at_ref[4]
    depth = width // (XS * ZHI * CORES)
    slab = hidden // (XS * ZHI * CORES)
    taken = PATCH * PATCH
    rows = taken * SUB
    copies = [pltpu.make_async_copy(target_ref, wanted, sems.at[0])]
    copies[0].start()

    def place(piece, at, source_x, of_zhi, of_core):
        shard = lax.rem(source_x, XS) * (ZHI * CORES) + of_zhi * CORES + of_core
        lines = pl.ds(at, depth)

        def put(columns, into):
            copy = pltpu.make_async_copy(piece.at[lines, columns], into, sems.at[len(copies)])
            copy.start()
            copies.append(copy)

        line = pl.multiple_of(shard * depth, depth)
        put(pl.ds(0, hidden), w_in.at[pl.ds(line, depth), :])
        for part in range(slab // depth):
            line = pl.multiple_of(shard * slab + part * depth, depth)
            put(pl.ds(hidden + part * align, align), w_out.at[pl.ds(line, depth), :])

    for near, opposite, far, of_core in (
        (own_near, own_far, cross, core),
        (own_near_other, own_far_other, cross_other, 1 - core),
    ):
        for k, step in enumerate((0, 1, XS - 1)):
            place(near, k * depth, x + step, zhi, of_core)
        place(opposite, 0, x + 2, zhi, of_core)
        for k in range(XS):
            place(far, k * depth, k, 1 - zhi, of_core)

    lat = lat_ref[...] + below_ref[...] + above_ref[...]
    top = lat.astype(BF16)
    rest = lat - top.astype(F32)
    mid = rest.astype(BF16)
    low_part = (rest - mid.astype(F32)).astype(BF16)
    split = jnp.concatenate(
        [top.astype(F32), mid.astype(F32), low_part.astype(F32)], axis=0
    ).astype(BF16)
    cells = lat.shape[1]
    tokens = target_ref.shape[0]
    room = 256
    cols = across // PATCH

    def selection(u, v):
        shape = (cells, room)
        token = iota(shape, 1)
        lane = (token // cols) * (PATCH * across) + u * across + (token % cols) * PATCH + v
        return jnp.where((lane == iota(shape, 0)) & (token < tokens), 1.0, 0.0).astype(BF16)

    picks = [selection(u, v) for u in range(PATCH) for v in range(PATCH)]
    lines = []
    for pick in picks:
        got = nn(split, pick)
        lines.append(got[0:SUB] + got[SUB : 2 * SUB] + got[2 * SUB :])
    patches_t = jnp.concatenate(lines, axis=0)
    patches = patches_t.T
    empty = jnp.zeros((SUB - LATENT, width), F32)
    spread = []
    for k in range(taken):
        spread += [ew_ref[k * LATENT : (k + 1) * LATENT, :], empty]
    ew_top, ew_low = parts(jnp.concatenate(spread, axis=0))
    p_top, p_low = parts(patches[:tokens])
    embedded = nn(p_top, ew_top) + nn(p_low, ew_top) + nn(p_top, ew_low)
    emb[...] = (embedded + eb_ref[...]).astype(BF16)

    for copy in copies:
        copy.wait()

    step = 1024
    acc[...] = jnp.zeros_like(acc)

    for tile in range(hidden // step):
        at = pl.ds(pl.multiple_of(tile * step, step), step)
        h = nn(emb[...], w_in[:, at]) + pib_ref[:, at]
        pre[:, at] = h
        acc[...] += nn((h * sigmoid(h)).astype(BF16), w_out[at, :])

    projected = acc[...] + pob_ref[...]
    target = wanted[...].astype(F32)
    unit_target = target * lax.rsqrt(jnp.sum(target * target, axis=1, keepdims=True) + EPS_UNIT)
    inv_len = lax.rsqrt(jnp.sum(projected * projected, axis=1, keepdims=True) + EPS_UNIT)
    unit_proj = projected * inv_len
    cosine = jnp.sum(unit_proj * unit_target, axis=1, keepdims=True)
    grad_out = (-inv_len * (unit_target - cosine * unit_proj)).astype(BF16)
    grad_emb[...] = jnp.zeros_like(grad_emb)

    for tile in range(hidden // step):
        at = pl.ds(pl.multiple_of(tile * step, step), step)
        back = nt(grad_out, w_out[at, :])
        h = pre[:, at]
        sig = sigmoid(h)
        grad_hidden = (back * (sig * (1.0 + h * (1.0 - sig)))).astype(BF16)
        grad_emb[0:tokens, :] += nt(grad_hidden, w_in[:, at])

    grad = grad_emb[...]
    g_top, g_low = parts(grad)
    t_top, t_low = parts(patches_t)
    both = nn(jnp.concatenate([t_top, t_low], axis=0), g_top)
    embed_ref[...] = both[:rows] + both[rows:] + nn(t_top, g_low)
    both = nt(jnp.concatenate([ew_top, ew_low], axis=0), g_top)
    grad_patch = both[:rows] + both[rows:] + nt(ew_top, g_low)
    total = jnp.zeros((SUB, cells), F32)
    for position, pick in enumerate(picks):
        part = grad_patch[position * SUB : (position + 1) * SUB].astype(BF16)
        total = total + nt(part, pick)
    gl_ref[...] = total


def projector(at, lat, below, above, target, ew, eb, pib, pob, pieces, across):
    rows, width = PATCH * PATCH * SUB, ew.shape[1]
    hidden, align = pib.shape[1], pob.shape[1]
    tokens = target.shape[0]
    flops = 2 * tokens * (2 * width * hidden + 2 * hidden * align)
    return pl.pallas_call(
        lambda *refs: mlp_kernel(across, width, hidden, align, *refs),
        out_shape=(
            jax.ShapeDtypeStruct((rows, width), F32),
            jax.ShapeDtypeStruct(lat.shape, F32),
        ),
        in_specs=[pl.BlockSpec(memory_space=pltpu.SMEM)]
        + [vmem()] * 3
        + [pl.BlockSpec(memory_space=pltpu.HBM)]
        + [vmem()] * 4
        + [pl.BlockSpec(memory_space=pltpu.HBM)] * len(pieces),
        out_specs=(vmem(), vmem()),
        scratch_shapes=[
            pltpu.VMEM((width, hidden), BF16),
            pltpu.VMEM((hidden, align), BF16),
            pltpu.VMEM((tokens, hidden), F32),
            pltpu.VMEM((tokens, width), BF16),
            pltpu.VMEM((tokens, align), F32),
            pltpu.VMEM((256, width), F32),
            pltpu.VMEM((tokens, align), BF16),
            pltpu.SemaphoreType.DMA((49,)),
        ],
        compiler_params=params(32),
        cost_estimate=pl.CostEstimate(
            flops=flops, bytes_accessed=8 << 20, transcendentals=2 * tokens * hidden
        ),
        name="projector",
    )(at, lat, below, above, in_hbm(target), ew, eb, pib, pob, in_hbm(pieces[0]), *pieces[1:])


def back_kernel(
    across, at_ref, gl_ref, far_ref, near_ref, f_ref, mean_ref, inv_ref, gain_ref, bias_ref,
    k_ref, embed_ref, send_ref, gs_ref, act, grads_t, by_bias, by_gain, pack,
):
    images, cells, channels = f_ref.shape
    per_group = channels // GROUPS
    gl, far, near = gl_ref[...], far_ref[...], near_ref[...]
    upper = at_ref[1] == 1
    before, after = jnp.where(upper, near, far), jnp.where(upper, far, near)
    col, row = lane_masks(gl.shape, across)
    lines = (
        jnp.where(row == 0, roll(gl, -across), roll(after, across)),
        gl,
        jnp.where(row == 0, roll(before, -across), roll(gl, across)),
    )
    parts = []
    for g in lines:
        parts.append(jnp.where(col < across - 1, roll(g, -1), 0.0))
        parts.append(g)
        parts.append(jnp.where(col > 0, roll(g, 1), 0.0))
    parts.append(jnp.zeros((LANES - TAPS * SUB, gl.shape[1]), F32))
    grads = jnp.concatenate(parts, axis=0)
    grads_t[...] = grads.T.astype(BF16)
    gain, bias = gain_ref[...], bias_ref[...]
    by_bias[...] = jnp.zeros_like(by_bias)
    by_gain[...] = jnp.zeros_like(by_gain)
    for i in range(images):
        at = slice(i * cells, (i + 1) * cells)
        v = f_ref[i].astype(F32)
        normed = (v - mean_ref[i : i + 1, :]) * inv_ref[i : i + 1, :]
        shifted = normed * gain + bias
        sig = sigmoid(shifted)
        act[at, :] = (shifted * sig).astype(BF16)
        grad_active = nn(grads_t[at, :], k_ref[...])
        gs = grad_active * (sig * (1.0 + shifted * (1.0 - sig)))
        gs_ref[i] = gs
        by_bias[i : i + 1, :] = jnp.sum(gs, axis=0, keepdims=True)
        by_gain[i : i + 1, :] = jnp.sum(gs * normed, axis=0, keepdims=True)
    conv = nn(grads.astype(BF16), act[...])
    stat = nn(by_bias[...] * gain, to_groups(channels, per_group, 0), HIGH) + nn(
        by_gain[...] * gain, to_groups(channels, per_group, GROUPS), HIGH
    )
    bias_part = jnp.sum(by_bias[...], axis=0, keepdims=True)
    gain_part = jnp.sum(by_gain[...], axis=0, keepdims=True)
    packed = halves(pack_stats(stat))
    for r in range(CHUNKS):
        send_ref[r, CHUNK_ROWS:ALL_ROWS, :] = packed
    blocks = channels // LANES
    half = CHUNKS // 2
    pack[...] = jnp.zeros_like(pack)
    for r in range(half):
        block, latent = r // LATENT, r % LATENT
        lanes = slice(block * LANES, (block + 1) * LANES)
        for position in range(TAPS):
            line = position * SUB + latent
            pack[r, position : position + 1, :] = conv[line : line + 1, lanes]
        lanes = slice((r // 2) * LANES, (r // 2 + 1) * LANES)
        for part in range(2):
            line = (r % 2) * 2 * SUB + part * SUB
            pack[half + r, part * LATENT : (part + 1) * LATENT, :] = embed_ref[
                line : line + LATENT, lanes
            ]
        if r < 2 * blocks:
            one = gain_part if r < blocks else bias_part
            lanes = slice((r % blocks) * LANES, (r % blocks + 1) * LANES)
            pack[half + r, SUB : SUB + 1, :] = one[:, lanes]
    for r in range(CHUNKS):
        send_ref[r, 0:CHUNK_ROWS, :] = pack[r].astype(BF16)


def conv_backward(at, gl, far, near, features, mean, inv, gain, bias, kernel_rows, embed, across):
    images, cells, channels = features.shape
    return pl.pallas_call(
        lambda *refs: back_kernel(across, *refs),
        out_shape=(
            jax.ShapeDtypeStruct((CHUNKS, ALL_ROWS, LANES), BF16),
            jax.ShapeDtypeStruct((images, cells, channels), F32),
        ),
        in_specs=[pl.BlockSpec(memory_space=pltpu.SMEM)] + [vmem()] * 10,
        out_specs=(vmem(),) * 2,
        scratch_shapes=[
            pltpu.VMEM((images * cells, channels), BF16),
            pltpu.VMEM((images * cells, LANES), BF16),
            pltpu.VMEM((STAT_ROWS, channels), F32),
            pltpu.VMEM((STAT_ROWS, channels), F32),
            pltpu.VMEM((CHUNKS, CHUNK_ROWS, LANES), F32),
        ],
        compiler_params=params(),
        name="back",
    )(at, gl, far, near, features, mean, inv, gain, bias, kernel_rows, embed)


def last_kernel(members, got_ref, f_ref, mean_ref, inv_ref, gain_ref, gs_ref, out_ref):
    images, _, channels = f_ref.shape
    per_group = channels // GROUPS
    total = unpack_stats(got_ref[...])
    first = nn(total, from_groups(channels, per_group, 0), HIGH) * (1.0 / members)
    second = nn(total, from_groups(channels, per_group, GROUPS), HIGH) * (1.0 / members)
    gain = gain_ref[...]
    for i in range(images):
        v = f_ref[i].astype(F32)
        inv = inv_ref[i : i + 1, :]
        normed = (v - mean_ref[i : i + 1, :]) * inv
        out = inv * (gs_ref[i] * gain - first[i : i + 1] - normed * second[i : i + 1])
        out_ref[i] = out.astype(BF16)


def feature_grad(got, features, mean, inv, gain, grad_shift, members):
    return pl.pallas_call(
        lambda *refs: last_kernel(members, *refs),
        out_shape=jax.ShapeDtypeStruct(features.shape, BF16),
        in_specs=[vmem()] * 6,
        out_specs=vmem(),
        compiler_params=params(),
        cost_estimate=pl.CostEstimate(
            flops=10 * features.size, bytes_accessed=8 * features.size, transcendentals=0
        ),
        name="last",
    )(got, features, mean, inv, gain, grad_shift)


def plane_kernel(at_ref, got_ref, out_ref):
    chunk = jnp.zeros((CHUNK_ROWS, LANES), F32)
    stat = jnp.zeros((SUB, LANES), F32)
    for r in range(CHUNKS):
        chunk = chunk + got_ref[r, 0:CHUNK_ROWS, :].astype(F32)
        pair = got_ref[r, CHUNK_ROWS:ALL_ROWS, :].astype(F32)
        stat = stat + jnp.where(at_ref[2] == (r // CORES) % YS, pair[:SUB] + pair[SUB:], 0.0)
    chunk, stat = chunk.astype(BF16), halves(stat)
    for r in range(out_ref.shape[0]):
        out_ref[r, 0:CHUNK_ROWS, :] = chunk
        out_ref[r, CHUNK_ROWS:ALL_ROWS, :] = stat


def plane_total(at, got):
    return pl.pallas_call(
        plane_kernel,
        out_shape=jax.ShapeDtypeStruct((ZHI * ZLO, ALL_ROWS, LANES), BF16),
        in_specs=[pl.BlockSpec(memory_space=pltpu.SMEM), vmem()],
        out_specs=vmem(),
        compiler_params=params(),
        name="plane",
    )(at, got)


def column_kernel(at_ref, got_ref, out_ref, stat_ref):
    chunk = jnp.zeros((CHUNK_ROWS, LANES), F32)
    stat = jnp.zeros((SUB, LANES), F32)
    for r in range(ZHI * ZLO):
        chunk = chunk + got_ref[r, 0:CHUNK_ROWS, :].astype(F32)
        pair = got_ref[r, CHUNK_ROWS:ALL_ROWS, :].astype(F32)
        stat = stat + jnp.where(at_ref[3] == r % ZLO, pair[:SUB] + pair[SUB:], 0.0)
    chunk = chunk.astype(BF16)
    for r in range(out_ref.shape[0]):
        out_ref[r] = chunk
    stat_ref[...] = stat


def column_total(at, got):
    return pl.pallas_call(
        column_kernel,
        out_shape=(
            jax.ShapeDtypeStruct((CHUNKS, CHUNK_ROWS, LANES), BF16),
            jax.ShapeDtypeStruct((SUB, LANES), F32),
        ),
        in_specs=[pl.BlockSpec(memory_space=pltpu.SMEM), vmem()],
        out_specs=(vmem(), vmem()),
        compiler_params=params(),
        name="column",
    )(at, got)


def unpack_kernel(got_ref, conv_ref, gain_ref, bias_ref, embed_ref, wide):
    channels = gain_ref.shape[1]
    blocks = channels // LANES
    half = CHUNKS // 2
    wide[...] = got_ref[...].astype(F32)
    for r in range(half):
        block, latent = r // LATENT, r % LATENT
        for position in range(TAPS):
            at = position * channels + block * LANES
            conv_ref[latent : latent + 1, at : at + LANES] = wide[r, position : position + 1, :]
        lanes = slice((r // 2) * LANES, (r // 2 + 1) * LANES)
        line = (r % 2) * SUB
        embed_ref[line : line + SUB, lanes] = wide[half + r, 0:SUB, :]
        lanes = slice((r % blocks) * LANES, (r % blocks + 1) * LANES)
        if r < blocks:
            gain_ref[:, lanes] = wide[half + r, SUB : SUB + 1, :]
        elif r < 2 * blocks:
            bias_ref[:, lanes] = wide[half + r, SUB : SUB + 1, :]


def unpack(got, channels, width):
    return pl.pallas_call(
        unpack_kernel,
        out_shape=(
            jax.ShapeDtypeStruct((LATENT, TAPS * channels), F32),
            jax.ShapeDtypeStruct((1, channels), F32),
            jax.ShapeDtypeStruct((1, channels), F32),
            jax.ShapeDtypeStruct((PATCH * PATCH * LATENT, width), F32),
        ),
        in_specs=[vmem()],
        out_specs=(vmem(),) * 4,
        scratch_shapes=[pltpu.VMEM(got.shape, F32)],
        compiler_params=params(),
        name="unpack",
    )(got)


def device(x, zhi, core, zlo, y):
    return ((x * ZHI + zhi) * CORES + core) * (ZLO * YS) + zlo * YS + y


BOTH = ("rows", "batch")
PLANE = [
    [device(x, h, c, d, y) for x in range(XS) for y in range(YS) for c in range(CORES)]
    for h in range(ZHI)
    for d in range(ZLO)
]
SHEET = [
    [device(x, h, c, d, y) for x in range(XS) for y in range(YS)]
    for h in range(ZHI)
    for d in range(ZLO)
    for c in range(CORES)
]
COLUMN = [
    [device(x, h, c, d, y) for h in range(ZHI) for d in range(ZLO)]
    for x in range(XS)
    for y in range(YS)
    for c in range(CORES)
]


def exchanged(value, groups):
    return lax.all_to_all(value, BOTH, 0, 0, axis_index_groups=groups, tiled=True)


def moved(value, where):
    pairs = []
    for x in range(XS):
        for zhi in range(ZHI):
            for core in range(CORES):
                for zlo in range(ZLO):
                    for y in range(YS):
                        a, b, c, d, e = where(x, zhi, core, zlo, y)
                        pairs.append((device(x, zhi, core, zlo, y), device(a, b, c, d, e)))
    return lax.ppermute(value, ("rows", "batch"), pairs)


def shard_kernel(at_ref, in_ref, out_ref, shard_ref, part_ref, sems):
    depth, hidden = in_ref.shape
    align = out_ref.shape[1]
    size = part_ref.shape[0]
    begin = pl.multiple_of(at_ref[2] * size, size)
    copies = []

    def put(source, lines, into, columns):
        copy = pltpu.make_async_copy(
            source.at[lines], into.at[:, columns], sems.at[len(copies)]
        )
        copy.start()
        copies.append(copy)

    for into, first, count in ((part_ref, begin, size), (shard_ref, 0, depth)):
        put(in_ref, pl.ds(first, count), into, pl.ds(0, hidden))
        for part in range(out_ref.shape[0] // depth):
            lines = pl.ds(part * depth + first, count)
            put(out_ref, lines, into, pl.ds(hidden + part * align, align))
    for copy in copies:
        copy.wait()


def shard_of(at, proj_in, proj_out):
    depth, hidden = proj_in.shape
    columns = hidden + proj_out.size // depth
    return pl.pallas_call(
        shard_kernel,
        out_shape=(
            jax.ShapeDtypeStruct((depth, columns), BF16),
            jax.ShapeDtypeStruct((depth // YS, columns), BF16),
        ),
        in_specs=[pl.BlockSpec(memory_space=pltpu.SMEM)]
        + [pl.BlockSpec(memory_space=pltpu.HBM)] * 2,
        out_specs=(vmem(), vmem()),
        scratch_shapes=[pltpu.SemaphoreType.DMA((6,))],
        compiler_params=params(),
        name="shard",
    )(at, in_hbm(proj_in), in_hbm(proj_out))


def crossed(part):
    return moved(part, lambda x, h, c, d, y: (x, 1 - h, c, ZLO - 1 - d, y))


def from_next(value):
    return moved(value, lambda x, h, c, d, y: ((x + XS - 1) % XS, h, c, d, y))


def from_last(value):
    return moved(value, lambda x, h, c, d, y: ((x + 1) % XS, h, c, d, y))


def along_x(shard):
    plus, minus = from_next(shard), from_last(shard)
    return jnp.concatenate([shard, plus, minus], axis=0), from_next(plus)


def swapped(value):
    return moved(value, lambda x, h, c, d, y: (x, h, 1 - c, d, y))


def neighbours(far, near):
    count = lax.axis_size("rows")
    pairs = [(r, r + 1) for r in range(1, count - 1, 2)]
    pairs = pairs + [(b, a) for a, b in pairs]
    inside = [(r, r ^ 1) for r in range(count)]
    return lax.ppermute(far, "rows", pairs), lax.ppermute(near, "rows", inside)


def shards(
    features,
    norm_gain,
    norm_bias,
    conv_weight,
    embed_weight,
    embed_bias,
    proj_in,
    proj_in_bias,
    proj_out,
    proj_out_bias,
    targets,
):
    images, height, across, channels = features.shape
    width, align = embed_weight.shape[1], proj_out.shape[1]
    peers = lax.axis_size("rows")
    members = peers * height * across * (channels // GROUPS)
    flat = features.reshape(images, height * across, channels)
    gain, bias = norm_gain.reshape(1, channels), norm_bias.reshape(1, channels)
    rows, batch = lax.axis_index("rows"), lax.axis_index("batch")
    at = jnp.stack([(rows // CORES) % ZHI, rows % CORES, batch % YS, batch // YS, rows // (ZHI * CORES)])
    at = at.astype(jnp.int32)
    shard, part = shard_of(at, proj_in, proj_out)
    own_near, own_far = along_x(shard)
    taps = conv_weight.reshape(LATENT, TAPS, channels).transpose(1, 0, 2)
    taps = jnp.pad(taps, ((0, 0), (0, SUB - LATENT), (0, 0))).reshape(TAPS * SUB, channels)
    taps_full = jnp.pad(taps, ((0, LANES - TAPS * SUB), (0, 0)))

    flat, part = lax.optimization_barrier((flat, part))
    sums = group_stats(flat, peers)
    stats = lax.all_to_all(sums, "rows", 0, 0, tiled=True)
    cross, stats = lax.optimization_barrier((crossed(part), stats))
    cross = jnp.broadcast_to(cross[None], (XS * YS, *cross.shape))
    cross = exchanged(cross, SHEET).reshape(-1, shard.shape[1])
    lat, far, near, mean, inv = conv_forward(at, stats, flat, gain, bias, taps, across, members)
    above, below = neighbours(far, near)
    cross, own_near, own_far, above, below = lax.optimization_barrier((cross, own_near, own_far, above, below))
    pieces = [own_near, own_far, cross]
    pieces = pieces + [swapped(v) for v in pieces]
    target = targets.reshape(-1, align)
    embed_part, grad_lat = projector(
        at, lat, below, above, target, embed_weight, embed_bias.reshape(1, -1),
        proj_in_bias.reshape(1, -1), proj_out_bias.reshape(1, -1), pieces, across,
    )
    far, near = neighbours(grad_lat, grad_lat)
    send, grad_shift = conv_backward(
        at, grad_lat, far, near, flat, mean, inv, gain, bias, taps_full, embed_part, across
    )
    plane = exchanged(send, PLANE)
    column = exchanged(plane_total(at, plane), COLUMN)
    chunks, got = column_total(at, column)
    everything = exchanged(chunks, PLANE)
    grad_features = feature_grad(got, flat, mean, inv, gain, grad_shift, members)
    grad_conv, grad_gain, grad_bias, grad_embed = unpack(everything, channels, width)
    return (
        grad_features.reshape(features.shape),
        grad_conv,
        grad_gain.reshape(channels),
        grad_bias.reshape(channels),
        grad_embed,
    )


def solution(mesh):
    in_specs = (
        P("batch", "rows", None, None),
        P(),
        P(),
        P(),
        P(),
        P(),
        P("rows", None),
        P(),
        P("rows", None),
        P(),
        P("batch", "rows", None, None),
    )
    out_specs = (P("batch", "rows", None, None), P(), P(), P(), P())
    return jax.shard_map(shards, mesh=mesh, in_specs=in_specs, out_specs=out_specs, check_vma=False)
```
